32 devices in a mesh: group: 2 (over y), tm: 4 (over z), mp: 4 (over x, core).
Axes of the slice: x: 2, y: 2, z: 4, core: 2. Of those that a mesh axis runs over, the one named last changes fastest.
Arguments:
- tokens: bfloat16 [3072, 1536], P(('group', 'tm'), 'mp'), parts along dimension 0, may hold values from -6 to 6
- segment_ids: int32 [3072], P(('group', 'tm')), parts along dimension 0, may hold values from 0 to 7, never falling along the last dimension, each value on 1 to 1152 neighbouring positions
- ln_att_gain: float32 [1536], replicated, may hold values from 0.25 to 1.75
- w_query: bfloat16 [1536, 1536], P(None, 'mp'), may hold values from -3 to 3
- w_keyval: bfloat16 [1536, 2, 1536], P(None, None, 'mp'), may hold values from -0.15625 to 0.15625
- w_out: bfloat16 [1536, 1536], P('mp'), may hold values from -0.21875 to 0.21875
- ln_conv_gain: float32 [1536], replicated, may hold values from 0.25 to 1.75
- w_glu: bfloat16 [1536, 2, 1536], P(None, None, 'mp'), may hold values from -0.15625 to 0.15625
- w_depth: bfloat16 [31, 1536], P(None, 'mp'), may hold values from -1 to 1
- bn_scale: float32 [1536], P('mp'), may hold values from 0.5 to 2
- bn_shift: float32 [1536], P('mp'), may hold values from -3 to 3
- w_proj: bfloat16 [1536, 1536], P('mp'), may hold values from -0.21875 to 0.21875
Outputs:
- block_out: bfloat16 [3072, 1536], P(('group', 'tm'), 'mp'), parts along dimension 0
The draws below stay inside these ranges and needn't reach their ends.
There are 2 independent parts, one for each index of `group`. The reference program is written for one: setup_inputs(seed, part) draws one part's arguments, and reference() takes and returns one part's arrays. A program takes and returns all parts, laid end to end along the dimension named above; an argument that names none is the same for every part. Nothing has to cross between parts.
Inputs may be any that keep to these rules, and one draw needn't show every extreme that they name: `segment_ids`: non-decreasing along the frames; each of the 8 recordings has 1 to 1152 frames and one has exactly that many.
All inputs are finite; a program needn't handle non-finite values.
Results may differ from the reference program's by a relative error of at most 0.015.
The reference program's roundings to bfloat16 on the way (of `normed`, `context`, `middle`, `normed_conv`, `gated` and `swished`) count: a program that leaves them out, or rounds other values in their place, can miss the bound.
Values may be sent and summed in bfloat16 or wider, within the bound.
A program may use at most 64 MiB of HBM per device.

```python
import math
import jax
import jax.numpy as jnp
import numpy as np
from jax import lax

D = 1536
HEADS = 16
KERNEL = 31
SEGS = 8
TOK_DEV = 384
TOKENS = 1536
N_TM = 4
N_MP = 4


def draw_w_query(key, part):
    base = jnp.clip(jax.random.normal(key, (D, D), jnp.float32), -4.0, 4.0)
    return (base / math.sqrt(D)).astype(jnp.bfloat16)


def spiked(drawn, rng, source, target, shards_of, factor):
    def block_of(dim):
        return (jnp.arange(drawn.shape[dim]) // (drawn.shape[dim] // shards_of)).reshape((-1,) + (1,) * (drawn.ndim - 1 - dim))

    near = jax.random.permutation(rng, shards_of)[block_of(target)]
    far = (block_of(target) + shards_of // 2) % shards_of
    return jnp.where((block_of(source) == near) | (block_of(source) == far), factor * drawn, drawn)


def block_scale(own_key, dims, split, low, top_value):
    factor_of = 1.0
    for axis_at, shards_of in split:
        heights = jax.random.uniform(jax.random.fold_in(jax.random.fold_in(own_key, 6), axis_at), (shards_of,), jnp.float32, low / len(split), top_value / len(split))
        factor_of = factor_of * jnp.repeat(jnp.exp(heights), dims[axis_at] // shards_of).reshape((-1,) + (1,) * (len(dims) - 1 - axis_at))
    return factor_of


def split_up(amount, total, bound, lean):
    portions = [(1 << 20) // math.isqrt(standing ** lean) + 1 for standing in range(2, amount + 1)]
    surplus, counts = total - bound - (amount - 1), [1] * (amount - 1)
    while surplus > 0:
        movable = [i for i in range(amount - 1) if counts[i] < bound]
        pool, left = sum([portions[i] for i in movable]), surplus
        for i in movable:
            addition = min(bound - counts[i], max(1, left * portions[i] // pool), surplus)
            counts[i] = counts[i] + addition
            surplus = surplus - addition
    return np.array([bound] + counts)


def ragged_sizes(key, count, total, reach, slope):
    if count == 2:
        one = jax.random.randint(key, (), max(1, total - reach), min(reach, total - 1) + 1)
        return jnp.stack([one, total - one])
    lengths = jnp.asarray(split_up(count, total, reach, slope), jnp.int32)
    pairs = (count - 1) // 2
    donor, taker = lengths[1:1 + 2 * pairs:2], lengths[2:2 + 2 * pairs:2]
    margin = jnp.minimum(donor - 1, reach - taker)
    passed = jax.random.randint(jax.random.fold_in(key, 1), (pairs,), 0, 1 << 20) % (margin + 1)
    lengths = lengths.at[1:1 + 2 * pairs:2].set(donor - passed).at[2:2 + 2 * pairs:2].set(taker + passed)
    return lengths[jax.random.permutation(jax.random.fold_in(key, 2), count)]


def gaussian(key, dims, width, most, shards=(), held_as=jnp.bfloat16):
    array = jax.random.normal(key, dims, jnp.float32) * width
    if len(shards) > 0:
        array = block_scale(key, dims, shards, -0.22, 0.18) * array
    return jnp.clip(array, min=-most, max=most).astype(held_as)


def gaussian_with(rng, dims, scale, limit, shards, heavy, held_as=jnp.bfloat16):
    array = scale * jax.random.normal(rng, dims, jnp.float32)
    if shards:
        array = array * block_scale(rng, dims, shards, -0.22, 0.18)
    return jnp.clip(spiked(array, jax.random.fold_in(rng, 3), *heavy), -limit, limit).astype(held_as)


def setup_inputs(seed: int = 0, part: int = 0) -> dict:
    seeds = jax.random.split(jax.random.key(seed), 13)
    own_keys = jax.random.split(jax.random.fold_in(seeds[12], part), 13)
    tokens = gaussian(own_keys[0], (TOKENS, D), 1.0, 6.0, ((0, 4), (1, 4)))
    segment_ids = jnp.searchsorted(jnp.cumsum(ragged_sizes(own_keys[1], SEGS, TOKENS, 3 * TOKENS // 4, 0)), jnp.arange(TOKENS), side="right").astype(jnp.int32)
    ln_att_gain = jnp.clip(1.0 + 0.15 * jax.random.normal(seeds[2], (D,), jnp.float32), 0.25, 1.75)
    w_query = draw_w_query(jax.random.fold_in(seeds[12], 71), part)
    w_keyval = gaussian(seeds[4], (D, 2, D), D ** -0.5, 0.15625, ((2, 4),))
    w_out = gaussian_with(seeds[5], (D, D), D ** -0.5, 0.21875, ((0, 4),), (0, 1, 4, 2.0))
    ln_conv_gain = jnp.clip(1.0 + 0.15 * jax.random.normal(seeds[6], (D,), jnp.float32), 0.25, 1.75)
    w_glu = gaussian(seeds[7], (D, 2, D), D ** -0.5, 0.15625, ((2, 4),))
    w_depth = gaussian(seeds[8], (KERNEL, D), KERNEL ** -0.5, 1.0, ((1, 4),))
    bn_scale = jnp.clip(jnp.exp(math.log(2.0) - 1.3862944 * jax.random.uniform(seeds[9], (D,), jnp.float32) ** block_scale(seeds[9], (D,), ((0, 4),), -0.2, 0.2)), 0.5, 2.0)
    bn_shift = gaussian(seeds[10], (D,), 0.5, 3.0, ((0, 4),), jnp.float32)
    w_proj = gaussian_with(seeds[11], (D, D), D ** -0.5, 0.21875, ((0, 4),), (0, 1, 4, 2.0))
    return dict(tokens=tokens, segment_ids=segment_ids, ln_att_gain=ln_att_gain, w_query=w_query, w_keyval=w_keyval, w_out=w_out, ln_conv_gain=ln_conv_gain, w_glu=w_glu, w_depth=w_depth, bn_scale=bn_scale, bn_shift=bn_shift, w_proj=w_proj)


def layer_norm(values_in, gain_vec):
    row_mean = lax.optimization_barrier(jnp.mean(values_in, axis=-1, keepdims=True))
    centered = values_in - row_mean
    spread = lax.optimization_barrier(jnp.mean(centered * centered, axis=-1, keepdims=True))
    return centered * lax.rsqrt(spread + 1e-05) * gain_vec

def grouped_product(left, right):
    group_width = left.shape[1] // N_MP
    summed = jnp.zeros((left.shape[0], right.shape[1]), jnp.float32)
    for group_index in range(N_MP):
        lower = group_index * group_width
        partial_value = jnp.dot(left[:, lower:lower + group_width], right[lower:lower + group_width], preferred_element_type=jnp.float32)
        summed = summed + lax.optimization_barrier(partial_value.astype(jnp.bfloat16)).astype(jnp.float32)
    return summed

def reference(tokens, segment_ids, ln_att_gain, w_query, w_keyval, w_out, ln_conv_gain, w_glu, w_depth, bn_scale, bn_shift, w_proj):
    head_dim = D // HEADS
    score_scale = head_dim ** (-0.5)
    normed = layer_norm(tokens.astype(jnp.float32), ln_att_gain).astype(jnp.bfloat16)
    queries = jnp.dot(normed, w_query, preferred_element_type=jnp.float32).astype(jnp.bfloat16)
    key_part = jnp.dot(normed, w_keyval[:, 0, :], preferred_element_type=jnp.float32).astype(jnp.bfloat16)
    value_part = jnp.dot(normed, w_keyval[:, 1, :], preferred_element_type=jnp.float32).astype(jnp.bfloat16)

    def to_heads(matrix):
        return matrix.reshape(TOKENS, HEADS, head_dim).transpose(1, 0, 2)

    def head_attention(operands):
        q_head, k_head, v_head = operands

        def query_block(offset):
            q_rows = lax.dynamic_slice_in_dim(q_head, offset, TOK_DEV, 0)
            seg_rows = lax.dynamic_slice_in_dim(segment_ids, offset, TOK_DEV, 0)
            scores = jnp.dot(q_rows, k_head.T, preferred_element_type=jnp.float32) * score_scale
            same_seg = seg_rows[:, None] == segment_ids[None, :]
            scores = jnp.where(same_seg, scores, -jnp.inf)
            row_max = lax.optimization_barrier(jnp.max(scores, axis=1, keepdims=True))
            weights = jnp.exp(scores - row_max)
            weight_sum = lax.optimization_barrier(jnp.sum(weights, axis=1, keepdims=True))
            weighted = jnp.dot(weights.astype(jnp.bfloat16), v_head, preferred_element_type=jnp.float32)
            return (weighted / weight_sum).astype(jnp.bfloat16)
        offsets = (jnp.arange(N_TM) * TOK_DEV).astype(jnp.int32)
        return lax.map(query_block, offsets).reshape(TOKENS, head_dim)
    context = lax.map(head_attention, (to_heads(queries), to_heads(key_part), to_heads(value_part)))
    context = context.transpose(1, 0, 2).reshape(TOKENS, D)
    middle = (tokens.astype(jnp.float32) + grouped_product(context, w_out)).astype(jnp.bfloat16)
    normed_conv = layer_norm(middle.astype(jnp.float32), ln_conv_gain).astype(jnp.bfloat16)
    value_half = jnp.dot(normed_conv, w_glu[:, 0, :], preferred_element_type=jnp.float32)
    gate_half = jnp.dot(normed_conv, w_glu[:, 1, :], preferred_element_type=jnp.float32)
    gated = (value_half * jax.nn.sigmoid(gate_half)).astype(jnp.bfloat16)
    half_width = (KERNEL - 1) // 2
    padded = jnp.pad(gated.astype(jnp.float32), ((half_width, half_width), (0, 0)))
    padded_segs = jnp.pad(segment_ids, (half_width, half_width), constant_values=-1)
    depth = jnp.zeros((TOKENS, D), jnp.float32)
    for tap_index in range(KERNEL):
        same_seg = (padded_segs[tap_index:tap_index + TOKENS] == segment_ids)[:, None]
        shifted = jnp.where(same_seg, padded[tap_index:tap_index + TOKENS], 0.0)
        depth = depth + shifted * w_depth[tap_index].astype(jnp.float32)
    normalized = depth * bn_scale + bn_shift
    swished = (normalized * jax.nn.sigmoid(normalized)).astype(jnp.bfloat16)
    return (middle.astype(jnp.float32) + grouped_product(swished, w_proj)).astype(jnp.bfloat16)
```

```python
import functools

import jax
import jax.numpy as jnp
from jax import lax
from jax.experimental import pallas as pl
from jax.experimental.pallas import tpu as pltpu
from jax.sharding import PartitionSpec as P

HEAD_DIM = 96


def with_halo(value, sides, width):
    for axis, dim in sides:
        count, length = (lax.axis_size(axis), value.shape[dim])
        up = [(i, (i + 1) % count) for i in range(count - 1)]
        down = [(j, i) for i, j in up]
        last = lax.slice_in_dim(value, length - width, length, axis=dim)
        initial = lax.slice_in_dim(value, 0, width, axis=dim)
        before = lax.ppermute(last, axis, up)
        after = lax.ppermute(initial, axis, down)
        value = jnp.concatenate([before, value, after], axis=dim)
    return value


def layer_norm(values_in, gain_vec):
    row_mean = jnp.mean(values_in, axis=-1, keepdims=True)
    centered = values_in - row_mean
    spread = jnp.mean(centered * centered, axis=-1, keepdims=True)
    return centered * lax.rsqrt(spread + 1e-05) * gain_vec


def fold_keys(carry_state, query_heads, query_segs, keyval, key_segs, local_cols, score_scale):
    row_max, weight_sum, weighted = carry_state
    key_rows = keyval.shape[0]
    heads_here = query_heads.shape[1]
    key_part = keyval[:, :local_cols].reshape(key_rows, heads_here, -1)
    value_part = keyval[:, local_cols:].reshape(key_rows, heads_here, -1)
    scores = (
        jnp.einsum("qhd,khd->qhk", query_heads, key_part, preferred_element_type=jnp.float32)
        * score_scale
    )
    same_seg = (query_segs[:, None] == key_segs[None, :])[:, None, :]
    scores = jnp.where(same_seg, scores, -jnp.inf)
    new_max = jnp.maximum(row_max, jnp.max(scores, axis=2))
    safe_max = jnp.where(new_max == -jnp.inf, 0.0, new_max)
    weights = jnp.exp(scores - safe_max[:, :, None])
    factor = jnp.exp(row_max - safe_max)
    weight_sum = weight_sum * factor + jnp.sum(weights, axis=2)
    weighted = weighted * factor[:, :, None] + jnp.einsum(
        "qhk,khd->qhd", weights.astype(jnp.bfloat16), value_part, preferred_element_type=jnp.float32
    )
    return (new_max, weight_sum, weighted)


def maybe_fold(carry_state, query_heads, query_segs, keyval, key_segs, local_cols, score_scale):
    return fold_keys(
        carry_state, query_heads, query_segs, keyval, key_segs, local_cols, score_scale
    )


def per_device(
    tokens,
    segment_ids,
    ln_att_gain,
    w_query,
    w_keyval,
    w_out,
    ln_conv_gain,
    w_glu,
    w_depth,
    bn_scale,
    bn_shift,
    w_proj,
):
    row_count = tokens.shape[0]
    full_width = ln_att_gain.shape[0]
    local_cols = w_query.shape[1]
    heads_here = local_cols // HEAD_DIM
    score_scale = HEAD_DIM ** (-0.5)
    all_segs = lax.all_gather(segment_ids, "tm", axis=0, tiled=True)
    anchor = lax.axis_index("tm") * row_count
    whole_rows = lax.all_gather(tokens, "mp", axis=1, tiled=True)
    normed = layer_norm(whole_rows.astype(jnp.float32), ln_att_gain).astype(jnp.bfloat16)
    queries = jnp.dot(normed, w_query, preferred_element_type=jnp.float32).astype(jnp.bfloat16)
    keyval = jnp.dot(
        normed, w_keyval.reshape(full_width, -1), preferred_element_type=jnp.float32
    ).astype(jnp.bfloat16)
    query_heads = queries.reshape(row_count, heads_here, HEAD_DIM)
    initial = (
        jnp.full((row_count, heads_here), -jnp.inf, jnp.float32),
        jnp.zeros((row_count, heads_here), jnp.float32),
        jnp.zeros((row_count, heads_here, HEAD_DIM), jnp.float32),
    )
    segment = lax.all_gather(keyval, "tm", axis=0, tiled=True)
    piece_rows = segment.shape[0]
    block_count = piece_rows // row_count

    def inner_step(state_in, element):
        return (
            maybe_fold(
                state_in, query_heads, segment_ids, element[0], element[1], local_cols, score_scale
            ),
            None,
        )

    stacked = (
        segment.reshape(block_count, row_count, -1),
        all_segs.reshape(block_count, row_count),
    )
    result, unused = lax.scan(inner_step, initial, stacked)
    row_max, weight_sum, weighted = result
    context = (
        (weighted / weight_sum[:, :, None]).reshape(row_count, local_cols).astype(jnp.bfloat16)
    )
    att_terms = jnp.dot(context, w_out, preferred_element_type=jnp.float32)
    att_summed = lax.psum_scatter(
        att_terms.astype(jnp.bfloat16), "mp", scatter_dimension=1, tiled=True
    ).astype(jnp.float32)
    middle = (tokens.astype(jnp.float32) + att_summed).astype(jnp.bfloat16)
    whole_mid = lax.all_gather(middle, "mp", axis=1, tiled=True)
    normed_conv = layer_norm(whole_mid.astype(jnp.float32), ln_conv_gain).astype(jnp.bfloat16)
    both_halves = jnp.dot(
        normed_conv, w_glu.reshape(full_width, -1), preferred_element_type=jnp.float32
    )
    gated = (both_halves[:, :local_cols] * jax.nn.sigmoid(both_halves[:, local_cols:])).astype(
        jnp.bfloat16
    )
    half_width = (w_depth.shape[0] - 1) // 2
    extended = with_halo(gated, (("tm", 0),), half_width).astype(jnp.float32)
    padded_segs = jnp.pad(all_segs, (half_width, half_width), constant_values=-1)
    window_segs = lax.dynamic_slice_in_dim(padded_segs, anchor, row_count + 2 * half_width, 0)
    depth = jnp.zeros((row_count, local_cols), jnp.float32)
    for tap_index in range(w_depth.shape[0]):
        same_seg = (window_segs[tap_index : tap_index + row_count] == segment_ids)[:, None]
        shifted = jnp.where(same_seg, extended[tap_index : tap_index + row_count], 0.0)
        depth = depth + shifted * w_depth[tap_index].astype(jnp.float32)
    normalized = depth * bn_scale + bn_shift
    swished = (normalized * jax.nn.sigmoid(normalized)).astype(jnp.bfloat16)
    conv_terms = jnp.dot(swished, w_proj, preferred_element_type=jnp.float32)
    conv_summed = lax.psum_scatter(
        conv_terms.astype(jnp.bfloat16), "mp", scatter_dimension=1, tiled=True
    ).astype(jnp.float32)
    return (middle.astype(jnp.float32) + conv_summed).astype(jnp.bfloat16)


NEG = -1e30
HALO = 16
NCH = 2
RS = 128
RN = 192
MESH = pl.DeviceIdType.MESH
F32 = jnp.float32
BF16 = jnp.bfloat16


def block_kernel(
    T, taps,
    tokens_h, seg_h, g_att_h, wq_h, wkv_h, wo_h, g_conv_h, wg_h, wdep_h, bn_s_h, bn_b_h, wp_h,
    out, tokens, seg, g_att, g_conv, wdep, bn_s, bn_b, small, segcol, gains, bns, bnb,
    tok, seg_all, seg_ext, wq, wkv, wo, wg, wp, nrm, kbuf, qm, vm, sc, pw, mst, lst, acc,
    ctx, keep, mid, ext, wdf, sa, sx, sb, ra, rx, rb,
    raw, wide32, wsem, tok_recv, z_send, x_send, m_send, seg_send, seg_recv, hs_send, hs_recv,
    hg_send, hg_recv, rs_send, rs_recv, mid_send, mid_recv,
):
    R, C = tokens_h.shape
    M = 4
    D = M * C
    heads = C // HEAD_DIM
    CR = R // NCH
    t = lax.axis_index("tm")
    m = lax.axis_index("mp")
    mate = m + 1 - 2 * (m % 2)
    cross = (m + 2) % 4
    diag = (mate + 2) % 4

    def rcopy(src, dst, ssem, rsem, **dev):
        return pltpu.make_async_remote_copy(
            src_ref=src, dst_ref=dst, send_sem=ssem, recv_sem=rsem,
            device_id=dev, device_id_type=MESH,
        )

    firsts = [
        pltpu.make_async_copy(src, dst, small.at[i])
        for i, (src, dst) in enumerate([
            (tokens_h, tokens), (seg_h, seg), (g_att_h, g_att), (g_conv_h, g_conv),
            (wdep_h, wdep), (bn_s_h, bn_s), (bn_b_h, bn_b)])
    ]
    for c in firsts:
        c.start()
    loads = [
        pltpu.make_async_copy(wq_h, wq, wsem.at[0]),
    ]
    for b in range(2):
        for k in range(C // 128):
            loads.append(pltpu.make_async_copy(
                (wkv_h, wg_h)[b].at[:, :, pl.ds(k * 128, 128)], raw.at[b, k],
                wsem.at[1 + b * (C // 128) + k]))
    plain = len(loads)
    for b in range(M):
        cols = pl.ds(b * C, C)
        loads.append(pltpu.make_async_copy(wo_h.at[:, cols], wo.at[b], wsem.at[plain + b]))
        loads.append(pltpu.make_async_copy(wp_h.at[:, cols], wp.at[b], wsem.at[plain + M + b]))
    for c in loads:
        c.start()

    def split_pairs(pairs, both, col):
        flat = pairs.reshape(2 * D, 128)

        @pl.loop(0, D // 128)
        def _(i):
            wide32[...] = flat[pl.ds(pl.multiple_of(i * 256, 256), 256), :].astype(F32)
            rows = pl.ds(pl.multiple_of(i * 128, 128), 128)
            for j in range(2):
                both[rows, pl.ds(j * C + col, 128)] = wide32[pl.ds(j, 128, 2), :].astype(BF16)

    barrier = pltpu.get_barrier_semaphore()
    for peer in (mate, cross):
        pl.semaphore_signal(barrier, inc=1, device_id={"mp": peer}, device_id_type=MESH)
    for d in range(1, T):
        pl.semaphore_signal(
            barrier, inc=1, device_id={"tm": (t + d) % T}, device_id_type=MESH
        )
    for c in firsts:
        c.wait()
    tok[t, m] = tokens[...]
    ids = seg[...].reshape(1, R)
    seg_all[t] = jnp.broadcast_to(ids, (8, R))
    segcol[...] = jnp.transpose(jnp.broadcast_to(ids, (128, R)))
    seg_ext[0, pl.ds(HALO, R), :] = segcol[...]
    gains[0] = g_att[...].reshape(1, D)
    gains[1] = g_conv[...].reshape(1, D)
    bns[...] = bn_s[...].reshape(1, C)
    bnb[...] = bn_b[...].reshape(1, C)
    pl.semaphore_wait(barrier, 1 + T)

    def z_right(s):
        return rcopy(tok.at[s, m], tok.at[s, m], z_send.at[0, s], tok_recv.at[s, m],
                     tm=(t + 1) % T)

    def z_left(s):
        return rcopy(tok.at[s, m], tok.at[s, m], z_send.at[1, s], tok_recv.at[s, m],
                     tm=(t + T - 1) % T)

    def over_x(s, col):
        return rcopy(tok.at[s, col], tok.at[s, col], x_send.at[s], tok_recv.at[s, col],
                     mp=cross)

    def to_mate(s, col, k):
        return rcopy(tok.at[s, col], tok.at[s, col], m_send.at[s, k], tok_recv.at[s, col],
                     mp=mate)

    def launch(s):
        @pl.when(jnp.logical_and(s <= t, t < T - 1))
        def _():
            z_right(s).start()

        @pl.when(jnp.logical_and(s >= t, t > 0))
        def _():
            z_left(s).start()

        to_mate(s, m, 0).start()

    launch(t)
    over_x(t, m).start()

    def seg_copy(d):
        return rcopy(seg_all.at[t], seg_all.at[t], seg_send.at[d], seg_recv.at[t],
                     tm=(t + d) % T)

    for d in range(1, T):
        seg_copy(d).start()

    def halo_right(ref, ssem, rsem):
        return rcopy(ref.at[:, pl.ds(R, HALO)], ref.at[:, pl.ds(0, HALO)], ssem.at[0],
                     rsem.at[0], tm=(t + 1) % T)

    def halo_left(ref, ssem, rsem):
        return rcopy(ref.at[:, pl.ds(HALO, HALO)], ref.at[:, pl.ds(R + HALO, HALO)],
                     ssem.at[1], rsem.at[1], tm=(t + T - 1) % T)

    has_right = t < T - 1
    has_left = t > 0
    edge = jnp.logical_or(t == 0, t == T - 1)

    @pl.when(has_right)
    def _():
        halo_right(seg_ext, hs_send, hs_recv).start()

    @pl.when(has_left)
    def _():
        halo_left(seg_ext, hs_send, hs_recv).start()

    @pl.when(jnp.logical_not(has_left))
    def _():
        seg_ext[0, pl.ds(0, HALO), :] = jnp.full((HALO, 128), -1, jnp.int32)
        ext[:, pl.ds(0, HALO), :] = jnp.zeros((C // 128, HALO, 128), F32)

    @pl.when(jnp.logical_not(has_right))
    def _():
        seg_ext[0, pl.ds(R + HALO, HALO), :] = jnp.full((HALO, 128), -1, jnp.int32)
        ext[:, pl.ds(R + HALO, HALO), :] = jnp.zeros((C // 128, HALO, 128), F32)

    wdf[pl.ds(0, taps), :] = wdep[...].astype(F32)
    mst[...] = jnp.full(mst.shape, NEG, F32)
    lst[...] = jnp.zeros(lst.shape, F32)
    acc[...] = jnp.zeros(acc.shape, F32)
    for b in range(2):
        for k in range(C // 128):
            loads[1 + b * (C // 128) + k].wait()
            split_pairs(raw.at[b, k], (wkv, wg)[b], k * 128)
    head_of = lax.broadcasted_iota(jnp.int32, (1, C), 1) // HEAD_DIM

    def norm_rows(load, gain, r0, n):
        parts = [load(b, r0, n).astype(F32) for b in range(M)]
        total = parts[0] + parts[1] + parts[2] + parts[3]
        mean = jnp.sum(total, axis=1, keepdims=True) * (1.0 / D)
        parts = [p - mean for p in parts]
        sq = parts[0] * parts[0]
        for p in parts[1:]:
            sq = sq + p * p
        inv = lax.rsqrt(jnp.sum(sq, axis=1, keepdims=True) * (1.0 / D) + 1e-05)
        for b in range(M):
            nrm[pl.ds(r0, n), pl.ds(b * C, C)] = (
                parts[b] * inv * gains[gain, :, pl.ds(b * C, C)]
            ).astype(BF16)

    RT = 64
    coef = float(HEAD_DIM ** (-0.5))

    def fold(x):
        return sum(x[:, k * 128:(k + 1) * 128] for k in range(1, C // 128)) + x[:, :128]

    def wide(col):
        return jnp.concatenate([col] * (C // 128), axis=1)

    def softmax_rows(s, rt):
        r0 = pl.multiple_of(rt * RS, RS)
        rows = pl.ds(r0, RS)
        bias = jnp.where(wide(segcol[rows, :]) == seg_all[s, pl.ds(0, 1), :], 0.0, NEG)
        hs = range(heads)
        xs = [sc[pl.ds(pl.multiple_of(h * R + r0, RS), RS), :] + bias for h in hs]
        olds = [mst[h, rows, :] for h in hs]
        sums = [lst[h, rows, :] for h in hs]
        news = [jnp.maximum(o, jnp.max(x, axis=1, keepdims=True)) for o, x in zip(olds, xs)]
        fs = [jnp.exp((o - n) * coef) for o, n in zip(olds, news)]
        ps = [jnp.exp((x - wide(n)) * coef) for x, n in zip(xs, news)]
        sums = [v * f + fold(p) for v, f, p in zip(sums, fs, ps)]
        lanes = wide(fs[0])
        for h in hs[1:]:
            lanes = jnp.where(head_of == h, wide(fs[h]), lanes)
        for h in hs:
            mst[h, rows, :] = news[h]
            lst[h, rows, :] = sums[h]
            pw[rows, pl.ds(h * R, R)] = ps[h].astype(BF16)
        acc[rows, :] = acc[rows, :] * lanes

    def block_step(i, code):
        s = code % T
        nxt = (code // T) % T
        after = (code // (T * T)) % T

        @pl.when(jnp.logical_or(i == 0, jnp.logical_and(edge, i + 1 < T)))
        def _():
            z_right(nxt).wait_recv()
            launch(nxt)

        @pl.when(jnp.logical_and(jnp.logical_not(edge), i < 2))
        def _():
            z_right(after).wait_recv()
            launch(after)

        @pl.when(i + 1 < T)
        def _():
            over_x(nxt, m).start()

        over_x(s, cross).wait_recv()
        to_mate(s, cross, 1).start()
        to_mate(s, mate, 0).wait_recv()
        to_mate(s, diag, 1).wait_recv()

        @pl.when(i == 0)
        def _():
            loads[0].wait()

        @pl.when(i > 0)
        def _():
            rcopy(seg_all.at[s], seg_all.at[s], seg_send.at[0], seg_recv.at[s],
                  tm=(t + 1) % T).wait_recv()

        @pl.loop(0, R // RN)
        def _(rt):
            norm_rows(lambda b, r0, n: tok[s, b, pl.ds(r0, n), :], 0,
                      pl.multiple_of(rt * RN, RN), RN)

        @pl.when(i == 0)
        def _():
            q = jnp.dot(nrm[...], wq[...], preferred_element_type=F32).astype(BF16)
            for h in range(heads):
                qm[pl.ds(h * R, R), :] = jnp.where(head_of == h, q, jnp.zeros_like(q))

        kbuf[...] = jnp.dot(
            nrm[...], wkv[:, pl.ds(0, C)], preferred_element_type=F32).astype(BF16)
        v = jnp.dot(nrm[...], wkv[:, pl.ds(C, C)], preferred_element_type=F32).astype(BF16)
        for h in range(heads):
            vm[pl.ds(h * R, R), :] = jnp.where(head_of == h, v, jnp.zeros_like(v))
        for h in range(heads):
            sc[pl.ds(h * R, R), :] = lax.dot_general(
                qm[pl.ds(h * R, R), :], kbuf[...], (((1,), (1,)), ((), ())),
                preferred_element_type=F32)

        @pl.loop(0, R // RS)
        def _(rt):
            softmax_rows(s, rt)

        acc[...] += jnp.dot(pw[...], vm[...], preferred_element_type=F32)
        return code // T

    order = 228 - 3 * ((t + 3) // 4) - 171 * ((t + 2) // 4) - 27 * ((t + 1) // 4)
    lax.fori_loop(0, T, block_step, order)

    den = None
    for h in range(heads):
        col = jnp.sum(lst[h, :, :], axis=1, keepdims=True)
        den = col if den is None else jnp.where(head_of == h, col, den)
    ctx[...] = (acc[...] / den).astype(BF16)

    def rs_a(ph, ch):
        return rcopy(sa.at[ph, ch], ra.at[ph, ch], rs_send.at[ph, ch, 0],
                     rs_recv.at[ph, ch, 0], mp=mate)

    def rs_x(ph, ch):
        return rcopy(sx.at[ph, ch], rx.at[ph, ch], rs_send.at[ph, ch, 1],
                     rs_recv.at[ph, ch, 1], mp=cross)

    def rs_b(ph, ch):
        return rcopy(sb.at[ph, ch], rb.at[ph, ch], rs_send.at[ph, ch, 2],
                     rs_recv.at[ph, ch, 2], mp=mate)

    def scatter_chunk(ph, w, ch):
        a = ctx[pl.ds(ch * CR, CR), :]
        sa[ph, ch] = jnp.dot(a, w[diag], preferred_element_type=F32).astype(BF16)
        rs_a(ph, ch).start()
        mine = jnp.dot(a, w[cross], preferred_element_type=F32)
        sb[ph, ch] = jnp.dot(a, w[mate], preferred_element_type=F32).astype(BF16)
        rs_b(ph, ch).start()
        rs_a(ph, ch).wait_recv()
        sx[ph, ch] = (mine + ra[ph, ch].astype(F32)).astype(BF16)
        rs_x(ph, ch).start()
        keep[pl.ds(ch * CR, CR), :] = (
            jnp.dot(a, w[m], preferred_element_type=F32).astype(BF16).astype(F32))

    def summed(ph, ch):
        rs_b(ph, ch).wait_recv()
        rs_x(ph, ch).wait_recv()
        return (keep[pl.ds(ch * CR, CR), :] + rb[ph, ch].astype(F32)) + rx[ph, ch].astype(F32)

    for b in range(M):
        loads[plain + 2 * b].wait()
    for ch in range(NCH):
        scatter_chunk(0, wo, ch)

    def mid_copy(col, ch, k, **dev):
        piece = mid.at[col, pl.ds(ch * CR, CR)]
        return rcopy(piece, piece, mid_send.at[ch, k], mid_recv.at[col, ch], **dev)

    for ch in range(NCH):
        rows = pl.ds(ch * CR, CR)
        mid[m, rows, :] = (tokens[rows, :].astype(F32) + summed(0, ch)).astype(BF16)
        mid_copy(m, ch, 0, mp=cross).start()
        mid_copy(m, ch, 1, mp=mate).start()
    for ch in range(NCH):
        rows = pl.ds(ch * CR, CR)
        mid_copy(cross, ch, 0, mp=cross).wait_recv()
        mid_copy(cross, ch, 2, mp=mate).start()
        mid_copy(mate, ch, 1, mp=mate).wait_recv()
        mid_copy(diag, ch, 2, mp=mate).wait_recv()

        @pl.loop(0, CR // RN)
        def _(rt):
            norm_rows(lambda b, r0, n: mid[b, pl.ds(r0, n), :], 1,
                      pl.multiple_of(ch * CR + rt * RN, RN), RN)

        a = nrm[rows, :]
        val = jnp.dot(a, wg[:, pl.ds(0, C)], preferred_element_type=F32)
        gate = jnp.dot(a, wg[:, pl.ds(C, C)], preferred_element_type=F32)
        gated = (val * jax.nn.sigmoid(gate)).astype(BF16).astype(F32)
        for k in range(C // 128):
            ext[k, pl.ds(HALO + ch * CR, CR), :] = gated[:, k * 128:(k + 1) * 128]
        if ch == 0:
            @pl.when(has_left)
            def _():
                halo_left(ext, hg_send, hg_recv).start()

    @pl.when(has_right)
    def _():
        halo_right(ext, hg_send, hg_recv).start()

    @pl.when(has_left)
    def _():
        halo_right(seg_ext, hs_send, hs_recv).wait_recv()
        halo_right(ext, hg_send, hg_recv).wait_recv()

    @pl.when(has_right)
    def _():
        halo_left(seg_ext, hs_send, hs_recv).wait_recv()
        halo_left(ext, hg_send, hg_recv).wait_recv()

    half = (taps - 1) // 2
    for b in range(M):
        loads[plain + 1 + 2 * b].wait()
    for ch in range(NCH):
        @pl.loop(0, CR // RT)
        def _(rt):
            r0 = pl.multiple_of(ch * CR + rt * RT, RT)
            here = segcol[pl.ds(r0, RT), :]
            groups = [pl.ds(k * 128, 128) for k in range(C // 128)]
            depth = [jnp.zeros((RT, 128), F32) for _ in groups]
            for j in range(taps):
                at = pl.ds(r0 + (j + HALO - half), RT)
                same = seg_ext[0, at, :] == here
                for k, g in enumerate(groups):
                    depth[k] += jnp.where(same, ext[k, at, :], 0.0) * wdf[pl.ds(j, 1), g]
            for k, g in enumerate(groups):
                z = depth[k] * bns[:, g] + bnb[:, g]
                ctx[pl.ds(r0, RT), g] = (z * jax.nn.sigmoid(z)).astype(BF16)

        scatter_chunk(1, wp, ch)
    for ch in range(NCH):
        rows = pl.ds(ch * CR, CR)
        out[rows, :] = (mid[m, rows, :].astype(F32) + summed(1, ch)).astype(BF16)

    for s in range(T):
        @pl.when(jnp.logical_and(s <= t, t < T - 1))
        def _():
            z_right(s).wait_send()

        @pl.when(jnp.logical_and(s >= t, t > 0))
        def _():
            z_left(s).wait_send()

        over_x(s, m).wait_send()
        to_mate(s, m, 0).wait_send()
        to_mate(s, cross, 1).wait_send()
    for d in range(1, T):
        seg_copy(d).wait_send()

    @pl.when(has_right)
    def _():
        halo_right(seg_ext, hs_send, hs_recv).wait_send()
        halo_right(ext, hg_send, hg_recv).wait_send()

    @pl.when(has_left)
    def _():
        halo_left(seg_ext, hs_send, hs_recv).wait_send()
        halo_left(ext, hg_send, hg_recv).wait_send()

    for ch in range(NCH):
        for ph in range(2):
            rs_a(ph, ch).wait_send()
            rs_x(ph, ch).wait_send()
            rs_b(ph, ch).wait_send()
        mid_copy(m, ch, 0, mp=cross).wait_send()
        mid_copy(m, ch, 1, mp=mate).wait_send()
        mid_copy(cross, ch, 2, mp=mate).wait_send()


def fused_device(
    tokens, segment_ids, ln_att_gain, w_query, w_keyval, w_out, ln_conv_gain, w_glu,
    w_depth, bn_scale, bn_shift, w_proj,
):
    R, C = tokens.shape
    D = ln_att_gain.shape[0]
    T = lax.axis_size("tm")
    M = D // C
    heads = C // HEAD_DIM
    taps = w_depth.shape[0]
    CR = R // NCH
    vmem = pl.BlockSpec(memory_space=pltpu.VMEM)
    hbm = pl.BlockSpec(memory_space=pltpu.HBM)
    dma = pltpu.SemaphoreType.DMA
    part = pltpu.VMEM((2, NCH, CR, C), BF16)
    return pl.pallas_call(
        functools.partial(block_kernel, T, taps),
        out_shape=jax.ShapeDtypeStruct((R, C), BF16),
        in_specs=[hbm] * 12,
        out_specs=vmem,
        scratch_shapes=[
            pltpu.VMEM((R, C), BF16), pltpu.VMEM((R,), jnp.int32), pltpu.VMEM((D,), F32),
            pltpu.VMEM((D,), F32), pltpu.VMEM((taps, C), BF16), pltpu.VMEM((C,), F32),
            pltpu.VMEM((C,), F32), dma((7,)),
            pltpu.VMEM((R, 128), jnp.int32),
            pltpu.VMEM((2, 1, D), F32),
            pltpu.VMEM((1, C), F32),
            pltpu.VMEM((1, C), F32),
            pltpu.VMEM((T, M, R, C), BF16),
            pltpu.VMEM((T, 8, R), jnp.int32),
            pltpu.VMEM((1, R + 2 * HALO, 128), jnp.int32),
            pltpu.VMEM((D, C), BF16),
            pltpu.VMEM((D, 2 * C), BF16),
            pltpu.VMEM((M, C, C), BF16),
            pltpu.VMEM((D, 2 * C), BF16),
            pltpu.VMEM((M, C, C), BF16),
            pltpu.VMEM((R, D), BF16),
            pltpu.VMEM((R, C), BF16),
            pltpu.VMEM((heads * R, C), BF16),
            pltpu.VMEM((heads * R, C), BF16),
            pltpu.VMEM((heads * R, R), F32),
            pltpu.VMEM((R, heads * R), BF16),
            pltpu.VMEM((heads, R, 128), F32),
            pltpu.VMEM((heads, R, 128), F32),
            pltpu.VMEM((R, C), F32),
            pltpu.VMEM((R, C), BF16),
            pltpu.VMEM((R, C), F32),
            pltpu.VMEM((M, R, C), BF16),
            pltpu.VMEM((C // 128, R + 2 * HALO, 128), F32),
            pltpu.VMEM((32, C), F32),
            part, part, part, part, part, part,
            pltpu.VMEM((2, C // 128, D, 2, 128), BF16), pltpu.VMEM((256, 128), F32),
            dma((1 + 2 * (C // 128) + 2 * M,)),
            dma((T, M)), dma((2, T)), dma((T,)), dma((T, 2)),
            dma((T,)), dma((T,)), dma((2,)), dma((2,)), dma((2,)), dma((2,)),
            dma((2, NCH, 3)), dma((2, NCH, 3)), dma((NCH, 3)), dma((M, NCH)),
        ],
        compiler_params=pltpu.CompilerParams(
            collective_id=0, has_side_effects=True, vmem_limit_bytes=52 * 2**20
        ),
    )(*[
        pltpu.with_memory_space_constraint(x, pltpu.HBM)
        for x in (tokens, segment_ids, ln_att_gain, w_query, w_keyval, w_out, ln_conv_gain,
                  w_glu, w_depth, bn_scale, bn_shift, w_proj)
    ])


def solution(mesh):
    placed = (
        P(("group", "tm"), "mp"),
        P(("group", "tm")),
        P(),
        P(None, "mp"),
        P(None, None, "mp"),
        P("mp", None),
        P(),
        P(None, None, "mp"),
        P(None, "mp"),
        P("mp"),
        P("mp"),
        P("mp", None),
    )
    fused = mesh.shape["tm"] == 4 and mesh.shape["mp"] == 4
    return jax.shard_map(
        fused_device if fused else per_device, mesh=mesh, in_specs=placed, out_specs=P(("group", "tm"), "mp"), check_vma=False
    )
```

```python
import functools

import jax
import jax.numpy as jnp
from jax import lax
from jax.experimental import pallas as pl
from jax.experimental.pallas import tpu as pltpu
from jax.sharding import PartitionSpec as P

HEAD_DIM = 96


def with_halo(value, sides, width):
    for axis, dim in sides:
        count, length = (lax.axis_size(axis), value.shape[dim])
        up = [(i, (i + 1) % count) for i in range(count - 1)]
        down = [(j, i) for i, j in up]
        last = lax.slice_in_dim(value, length - width, length, axis=dim)
        initial = lax.slice_in_dim(value, 0, width, axis=dim)
        before = lax.ppermute(last, axis, up)
        after = lax.ppermute(initial, axis, down)
        value = jnp.concatenate([before, value, after], axis=dim)
    return value


def layer_norm(values_in, gain_vec):
    row_mean = jnp.mean(values_in, axis=-1, keepdims=True)
    centered = values_in - row_mean
    spread = jnp.mean(centered * centered, axis=-1, keepdims=True)
    return centered * lax.rsqrt(spread + 1e-05) * gain_vec


def fold_keys(carry_state, query_heads, query_segs, keyval, key_segs, local_cols, score_scale):
    row_max, weight_sum, weighted = carry_state
    key_rows = keyval.shape[0]
    heads_here = query_heads.shape[1]
    key_part = keyval[:, :local_cols].reshape(key_rows, heads_here, -1)
    value_part = keyval[:, local_cols:].reshape(key_rows, heads_here, -1)
    scores = (
        jnp.einsum("qhd,khd->qhk", query_heads, key_part, preferred_element_type=jnp.float32)
        * score_scale
    )
    same_seg = (query_segs[:, None] == key_segs[None, :])[:, None, :]
    scores = jnp.where(same_seg, scores, -jnp.inf)
    new_max = jnp.maximum(row_max, jnp.max(scores, axis=2))
    safe_max = jnp.where(new_max == -jnp.inf, 0.0, new_max)
    weights = jnp.exp(scores - safe_max[:, :, None])
    factor = jnp.exp(row_max - safe_max)
    weight_sum = weight_sum * factor + jnp.sum(weights, axis=2)
    weighted = weighted * factor[:, :, None] + jnp.einsum(
        "qhk,khd->qhd", weights.astype(jnp.bfloat16), value_part, preferred_element_type=jnp.float32
    )
    return (new_max, weight_sum, weighted)


def maybe_fold(carry_state, query_heads, query_segs, keyval, key_segs, local_cols, score_scale):
    return fold_keys(
        carry_state, query_heads, query_segs, keyval, key_segs, local_cols, score_scale
    )


def per_device(
    tokens,
    segment_ids,
    ln_att_gain,
    w_query,
    w_keyval,
    w_out,
    ln_conv_gain,
    w_glu,
    w_depth,
    bn_scale,
    bn_shift,
    w_proj,
):
    row_count = tokens.shape[0]
    full_width = ln_att_gain.shape[0]
    local_cols = w_query.shape[1]
    heads_here = local_cols // HEAD_DIM
    score_scale = HEAD_DIM ** (-0.5)
    all_segs = lax.all_gather(segment_ids, "tm", axis=0, tiled=True)
    anchor = lax.axis_index("tm") * row_count
    whole_rows = lax.all_gather(tokens, "mp", axis=1, tiled=True)
    normed = layer_norm(whole_rows.astype(jnp.float32), ln_att_gain).astype(jnp.bfloat16)
    queries = jnp.dot(normed, w_query, preferred_element_type=jnp.float32).astype(jnp.bfloat16)
    keyval = jnp.dot(
        normed, w_keyval.reshape(full_width, -1), preferred_element_type=jnp.float32
    ).astype(jnp.bfloat16)
    query_heads = queries.reshape(row_count, heads_here, HEAD_DIM)
    initial = (
        jnp.full((row_count, heads_here), -jnp.inf, jnp.float32),
        jnp.zeros((row_count, heads_here), jnp.float32),
        jnp.zeros((row_count, heads_here, HEAD_DIM), jnp.float32),
    )
    segment = lax.all_gather(keyval, "tm", axis=0, tiled=True)
    piece_rows = segment.shape[0]
    block_count = piece_rows // row_count

    def inner_step(state_in, element):
        return (
            maybe_fold(
                state_in, query_heads, segment_ids, element[0], element[1], local_cols, score_scale
            ),
            None,
        )

    stacked = (
        segment.reshape(block_count, row_count, -1),
        all_segs.reshape(block_count, row_count),
    )
    result, unused = lax.scan(inner_step, initial, stacked)
    row_max, weight_sum, weighted = result
    context = (
        (weighted / weight_sum[:, :, None]).reshape(row_count, local_cols).astype(jnp.bfloat16)
    )
    att_terms = jnp.dot(context, w_out, preferred_element_type=jnp.float32)
    att_summed = lax.psum_scatter(
        att_terms.astype(jnp.bfloat16), "mp", scatter_dimension=1, tiled=True
    ).astype(jnp.float32)
    middle = (tokens.astype(jnp.float32) + att_summed).astype(jnp.bfloat16)
    whole_mid = lax.all_gather(middle, "mp", axis=1, tiled=True)
    normed_conv = layer_norm(whole_mid.astype(jnp.float32), ln_conv_gain).astype(jnp.bfloat16)
    both_halves = jnp.dot(
        normed_conv, w_glu.reshape(full_width, -1), preferred_element_type=jnp.float32
    )
    gated = (both_halves[:, :local_cols] * jax.nn.sigmoid(both_halves[:, local_cols:])).astype(
        jnp.bfloat16
    )
    half_width = (w_depth.shape[0] - 1) // 2
    extended = with_halo(gated, (("tm", 0),), half_width).astype(jnp.float32)
    padded_segs = jnp.pad(all_segs, (half_width, half_width), constant_values=-1)
    window_segs = lax.dynamic_slice_in_dim(padded_segs, anchor, row_count + 2 * half_width, 0)
    depth = jnp.zeros((row_count, local_cols), jnp.float32)
    for tap_index in range(w_depth.shape[0]):
        same_seg = (window_segs[tap_index : tap_index + row_count] == segment_ids)[:, None]
        shifted = jnp.where(same_seg, extended[tap_index : tap_index + row_count], 0.0)
        depth = depth + shifted * w_depth[tap_index].astype(jnp.float32)
    normalized = depth * bn_scale + bn_shift
    swished = (normalized * jax.nn.sigmoid(normalized)).astype(jnp.bfloat16)
    conv_terms = jnp.dot(swished, w_proj, preferred_element_type=jnp.float32)
    conv_summed = lax.psum_scatter(
        conv_terms.astype(jnp.bfloat16), "mp", scatter_dimension=1, tiled=True
    ).astype(jnp.float32)
    return (middle.astype(jnp.float32) + conv_summed).astype(jnp.bfloat16)


NEG = -1e30
HALO = 16
LANES = 128
FIRST = 256
RS = 128
CHUNKS = ((224, 160), (0, 160), (160, 64))
REGIONS = (((240, 128),), ((16, 128),), ((144, 96), (0, 16), (368, 16)))
MESH = pl.DeviceIdType.MESH
F32 = jnp.float32
BF16 = jnp.bfloat16


def block_kernel(
    T, taps,
    tokens_h, seg_h, g_att_h, wq_h, wkv_h, wo_h, g_conv_h, wg_h, wdep_h, bn_s_h, bn_b_h, wp_h,
    out, seg, g_att, g_conv, wdep, bn_s, bn_b, small, segcol, gains, bns, bnb,
    tok, seg_all, seg_ext, rawq, raw, wide32, sc, pw, wq, wkv, wo, wg, wp, nrm, qp, kp, vp, mst, lst, acc,
    ctx, swi, keep, keep2, mid, ext, wdf, sa, ra, sx, rx, sa2, ra2, sx2, rx2, sb2, rb2,
    wsem, tok_recv, z_send, x_send, m_send, seg_send, seg_recv, hs_send, hs_recv,
    hg_send, hg_recv, ar_send, ar_recv, mid_send, mid_recv, rs_send, rs_recv,
):
    R, C = tokens_h.shape
    M = 4
    D = M * C
    heads = C // HEAD_DIM
    HP = heads * LANES
    tiles = C // LANES
    pieces = ((0, FIRST), (FIRST, R - FIRST))
    t = lax.axis_index("tm")
    m = lax.axis_index("mp")
    mate = m + 1 - 2 * (m % 2)
    cross = (m + 2) % 4
    diag = (mate + 2) % 4

    def rcopy(src, dst, ssem, rsem, **dev):
        return pltpu.make_async_remote_copy(
            src_ref=src, dst_ref=dst, send_sem=ssem, recv_sem=rsem,
            device_id=dev, device_id_type=MESH,
        )

    firsts = [
        pltpu.make_async_copy(src, dst, small.at[i])
        for i, (src, dst) in enumerate([
            (tokens_h, tok.at[t, m]), (seg_h, seg), (g_att_h, g_att), (g_conv_h, g_conv),
            (wdep_h, wdep), (bn_s_h, bn_s), (bn_b_h, bn_b)])
    ]
    loads, at = {}, 0

    def load(name, src, dst):
        nonlocal at
        loads[name] = pltpu.make_async_copy(src, dst, wsem.at[at])
        at += 1

    for k in range(tiles):
        load(("kv", k), wkv_h.at[:, :, pl.ds(k * LANES, LANES)], raw.at[0, k])
    load("q", wq_h, rawq)
    for k in range(tiles):
        load(("g", k), wg_h.at[:, :, pl.ds(k * LANES, LANES)], raw.at[1, k])
    for b in range(M):
        cols = pl.ds(b * C, C)
        for h in range(heads):
            load(("o", b, h), wo_h.at[pl.ds(h * HEAD_DIM, HEAD_DIM), cols],
                 wo.at[b, pl.ds(h * LANES, HEAD_DIM)])
    for b in range(M):
        load(("p", b), wp_h.at[:, pl.ds(b * C, C)], wp.at[b])
    for c in firsts:
        c.start()

    barrier = pltpu.get_barrier_semaphore()
    for peer in (mate, cross):
        pl.semaphore_signal(barrier, inc=1, device_id={"mp": peer}, device_id_type=MESH)
    for d in range(1, T):
        pl.semaphore_signal(
            barrier, inc=1, device_id={"tm": (t + d) % T}, device_id_type=MESH
        )
    for c in loads.values():
        c.start()
    for c in firsts:
        c.wait()
    ids = seg[...].reshape(1, R)
    seg_all[t] = jnp.broadcast_to(ids, (8, R))
    pl.semaphore_wait(barrier, 1 + T)

    def z_right(s, p):
        piece = tok.at[s, m, pl.ds(*pieces[p])]
        return rcopy(piece, piece, z_send.at[0, s, p], tok_recv.at[s, m, p], tm=(t + 1) % T)

    def z_left(s, p):
        piece = tok.at[s, m, pl.ds(*pieces[p])]
        return rcopy(piece, piece, z_send.at[1, s, p], tok_recv.at[s, m, p], tm=(t + T - 1) % T)

    def over_x(s, col, p):
        piece = tok.at[s, col, pl.ds(*pieces[p])]
        return rcopy(piece, piece, x_send.at[s, p], tok_recv.at[s, col, p], mp=cross)

    def to_mate(s, col, k, p):
        piece = tok.at[s, col, pl.ds(*pieces[p])]
        return rcopy(piece, piece, m_send.at[s, k, p], tok_recv.at[s, col, p], mp=mate)

    def launch(s, p):
        @pl.when(jnp.logical_and(s <= t, t < T - 1))
        def _():
            z_right(s, p).start()

        @pl.when(jnp.logical_and(s >= t, t > 0))
        def _():
            z_left(s, p).start()

    for p in range(2):
        over_x(t, m, p).start()
        launch(t, p)
        to_mate(t, m, 0, p).start()

    def seg_copy(d):
        return rcopy(seg_all.at[t], seg_all.at[t], seg_send.at[d], seg_recv.at[t],
                     tm=(t + d) % T)

    for d in range(1, T):
        seg_copy(d).start()

    def halo_right(ref, ssem, rsem):
        return rcopy(ref.at[:, pl.ds(R, HALO)], ref.at[:, pl.ds(0, HALO)], ssem.at[0],
                     rsem.at[0], tm=(t + 1) % T)

    def halo_left(ref, ssem, rsem):
        return rcopy(ref.at[:, pl.ds(HALO, HALO)], ref.at[:, pl.ds(R + HALO, HALO)],
                     ssem.at[1], rsem.at[1], tm=(t + T - 1) % T)

    has_right = t < T - 1
    has_left = t > 0
    edge = jnp.logical_or(t == 0, t == T - 1)

    segcol[...] = jnp.transpose(jnp.broadcast_to(ids, (LANES, R)))
    seg_ext[0, pl.ds(HALO, R), :] = segcol[...]

    @pl.when(has_right)
    def _():
        halo_right(seg_ext, hs_send, hs_recv).start()

    @pl.when(has_left)
    def _():
        halo_left(seg_ext, hs_send, hs_recv).start()

    @pl.when(jnp.logical_not(has_left))
    def _():
        seg_ext[0, pl.ds(0, HALO), :] = jnp.full((HALO, LANES), -1, jnp.int32)
        ext[:, pl.ds(0, HALO), :] = jnp.zeros((tiles, HALO, LANES), F32)

    @pl.when(jnp.logical_not(has_right))
    def _():
        seg_ext[0, pl.ds(R + HALO, HALO), :] = jnp.full((HALO, LANES), -1, jnp.int32)
        ext[:, pl.ds(R + HALO, HALO), :] = jnp.zeros((tiles, HALO, LANES), F32)

    gains[0] = g_att[...].reshape(1, D)
    gains[1] = g_conv[...].reshape(1, D)
    bns[...] = bn_s[...].reshape(1, C)
    bnb[...] = bn_b[...].reshape(1, C)

    def by_head(x):
        gap = jnp.zeros((x.shape[0], LANES - HEAD_DIM), F32)
        cols = []
        for h in range(heads):
            cols += [x[:, h * HEAD_DIM:(h + 1) * HEAD_DIM], gap]
        return jnp.concatenate(cols, axis=1).astype(BF16)

    for k in range(tiles):
        loads["kv", k].wait()

    def widen(b, i, n):
        for k in range(tiles):
            wide32[k, pl.ds(0, 2 * n), :] = raw.at[b, k].reshape(2 * D, LANES)[
                pl.ds(pl.multiple_of(i * 2 * n, 2 * n), 2 * n), :].astype(F32)

    @pl.loop(0, D // 256)
    def _(i):
        rows = pl.ds(pl.multiple_of(i * 256, 256), 256)
        widen(0, i, 256)
        for j in range(2):
            x = jnp.concatenate([wide32[k, pl.ds(j, 256, 2), :] for k in range(tiles)], axis=1)
            wkv[rows, pl.ds(j * HP, HP)] = by_head(x)

    loads["q"].wait()

    @pl.loop(0, D // 256)
    def _(i):
        rows = pl.ds(pl.multiple_of(i * 256, 256), 256)
        wq[rows, :] = by_head(rawq[rows, :].astype(F32))

    def split_gates():
        for k in range(tiles):
            loads["g", k].wait()

        @pl.loop(0, D // 128)
        def _(i):
            rows = pl.ds(pl.multiple_of(i * 128, 128), 128)
            widen(1, i, 128)
            for j in range(2):
                for k in range(tiles):
                    wg[rows, pl.ds(j * C + k * LANES, LANES)] = (
                        wide32[k, pl.ds(j, 128, 2), :].astype(BF16))

    wdf[pl.ds(0, taps), :] = wdep[...].astype(F32)
    mst[...] = jnp.full(mst.shape, NEG, F32)
    lst[...] = jnp.zeros(lst.shape, F32)
    acc[...] = jnp.zeros(acc.shape, F32)
    for b in range(M):
        for h in range(heads):
            wo[b, pl.ds(h * LANES + HEAD_DIM, LANES - HEAD_DIM), :] = jnp.zeros(
                (LANES - HEAD_DIM, C), BF16)

    def norm_rows(load_part, gain, r0, n):
        parts = [load_part(b, r0, n).astype(F32) for b in range(M)]
        total = parts[0] + parts[1] + parts[2] + parts[3]
        mean = jnp.sum(total, axis=1, keepdims=True) * (1.0 / D)
        parts = [p - mean for p in parts]
        sq = parts[0] * parts[0]
        for p in parts[1:]:
            sq = sq + p * p
        inv = lax.rsqrt(jnp.sum(sq, axis=1, keepdims=True) * (1.0 / D) + 1e-05)
        for b in range(M):
            nrm[pl.ds(r0, n), pl.ds(b * C, C)] = (
                parts[b] * inv * gains[gain, :, pl.ds(b * C, C)]
            ).astype(BF16)

    coef = float(HEAD_DIM ** (-0.5) * 1.4426950408889634)

    hs = range(heads)

    def lanes(h):
        return pl.ds(h * LANES, LANES)

    def weigh(s, r0, n, c0, nk, score, keep_weights):
        rows, keys = pl.ds(r0, n), pl.ds(c0, nk)

        def fold(x):
            return sum(x[:, k * LANES:(k + 1) * LANES] for k in range(1, nk // LANES)) + x[:, :LANES]

        def wide(col):
            return jnp.concatenate([col] * (nk // LANES), axis=1)

        bias = jnp.where(wide(segcol[rows, :]) == seg_all[s, pl.ds(0, 1), keys], 0.0, NEG)
        xs = [score(h) + bias for h in hs]
        olds = [mst[h, rows, :] for h in hs]
        sums = [lst[h, rows, :] for h in hs]
        accs = [acc[rows, lanes(h)] for h in hs]
        news = [jnp.maximum(o, jnp.max(x, axis=1, keepdims=True)) for o, x in zip(olds, xs)]
        fs = [jnp.exp2((o - v) * coef) for o, v in zip(olds, news)]
        ps = [jnp.exp2((x - wide(v)) * coef) for x, v in zip(xs, news)]
        sums = [v * f + fold(w) for v, f, w in zip(sums, fs, ps)]
        for h in hs:
            mst[h, rows, :] = news[h]
            lst[h, rows, :] = sums[h]
        keep_weights([w.astype(BF16) for w in ps], [a * f for a, f in zip(accs, fs)])

    def score_block(r0, n, c0, nk, h):
        return lax.dot_general(
            qp[pl.ds(r0, n), lanes(h)], kp[pl.ds(c0, nk), lanes(h)], (((1,), (1,)), ((), ())),
            preferred_element_type=F32)

    def attend(s, c0, nk):
        keys = pl.ds(c0, nk)
        for h in hs:
            sc[h, :, pl.ds(0, nk)] = score_block(0, R, c0, nk, h)

        @pl.loop(0, R // RS)
        def _(rt):
            r0 = pl.multiple_of(rt * RS, RS)
            rows = pl.ds(r0, RS)

            def kept(ws, scaled):
                for h in hs:
                    pw[h, rows, pl.ds(0, nk)] = ws[h]
                    acc[rows, lanes(h)] = scaled[h]

            weigh(s, r0, RS, c0, nk, lambda h: sc[h, rows, pl.ds(0, nk)], kept)

        for h in hs:
            acc[:, lanes(h)] += jnp.dot(
                pw[h, :, pl.ds(0, nk)], vp[keys, lanes(h)], preferred_element_type=F32)

    def attend_last(s, r0, n, c0, nk):
        rows, keys = pl.ds(r0, n), pl.ds(c0, nk)

        def kept(ws, scaled):
            for h in hs:
                total = scaled[h] + jnp.dot(
                    ws[h], vp[keys, lanes(h)], preferred_element_type=F32)
                den = jnp.sum(lst[h, rows, :], axis=1, keepdims=True)
                ctx[rows, lanes(h)] = (total / den).astype(BF16)

        weigh(s, r0, n, c0, nk, lambda h: score_block(r0, n, c0, nk, h), kept)

    def project(s, i, p, midway):
        r0, n = pieces[p]
        rows = pl.ds(r0, n)

        @pl.loop(0, n // 128)
        def _(rt):
            norm_rows(lambda b, at, k: tok[s, b, pl.ds(at, k), :], 0,
                      pl.multiple_of(r0 + rt * 128, 128), 128)

        @pl.when(i == 0)
        def _():
            qp[rows, :] = jnp.dot(
                nrm[rows, :], wq[...], preferred_element_type=F32).astype(BF16)

        kp[rows, :] = jnp.dot(
            nrm[rows, :], wkv[:, pl.ds(0, HP)], preferred_element_type=F32).astype(BF16)
        midway()
        vp[rows, :] = jnp.dot(
            nrm[rows, :], wkv[:, pl.ds(HP, HP)], preferred_element_type=F32).astype(BF16)

    def digit(code, i):
        return (code // (T ** i)) % T

    order = 228 - 3 * ((t + 3) // 4) - 171 * ((t + 2) // 4) - 27 * ((t + 1) // 4)

    def block_step(i, code):
        s, nxt, after = digit(code, 0), digit(code, 1), digit(code, 2)

        def relay(p):
            @pl.when(jnp.logical_or(i == 0, jnp.logical_and(edge, i + 1 < T)))
            def _():
                z_right(nxt, p).wait_recv()
                launch(nxt, p)

            @pl.when(i + 1 < T)
            def _():
                over_x(nxt, m, p).start()
                to_mate(nxt, m, 0, p).start()

            @pl.when(jnp.logical_and(jnp.logical_not(edge), i < 2))
            def _():
                z_right(after, p).wait_recv()
                launch(after, p)

            over_x(s, cross, p).wait_recv()
            to_mate(s, cross, 1, p).start()

        def arrive(p):
            to_mate(s, mate, 0, p).wait_recv()
            to_mate(s, diag, 1, p).wait_recv()

        relay(0)

        @pl.when(i > 0)
        def _():
            rcopy(seg_all.at[s], seg_all.at[s], seg_send.at[0], seg_recv.at[s],
                  tm=(t + 1) % T).wait_recv()

        arrive(0)
        project(s, i, 0, lambda: relay(1))
        arrive(1)
        project(s, i, 1, lambda: None)

        @pl.when(i < T - 1)
        def _():
            attend(s, 0, R)

        return code // T

    final = digit(order, T - 1)
    lax.fori_loop(0, T, block_step, order)

    def ar_mate(i):
        rows = pl.ds(*CHUNKS[i])
        return rcopy(sa.at[:, rows], ra.at[:, rows], ar_send.at[i, 0], ar_recv.at[i, 0], mp=mate)

    def ar_x(i):
        rows = pl.ds(*CHUNKS[i])
        return rcopy(sx.at[:, rows], rx.at[:, rows], ar_send.at[i, 1], ar_recv.at[i, 1], mp=cross)

    def mid_copy(i, j, col):
        piece = mid.at[col, pl.ds(*CHUNKS[i])]
        return rcopy(piece, piece, mid_send.at[i, j], mid_recv.at[i, j], mp=mate)

    def rounded(a, w):
        return jnp.dot(a, w, preferred_element_type=F32).astype(BF16)

    def finish(i):
        r0, n = CHUNKS[i]
        rows = pl.ds(r0, n)
        attend_last(final, r0, n, 0, R)
        a = ctx[rows, :]
        sa[0, rows, :] = rounded(a, wo[mate])
        sa[1, rows, :] = rounded(a, wo[diag])
        ar_mate(i).start()
        keep[0, rows, :] = rounded(a, wo[m]).astype(F32)
        keep[1, rows, :] = rounded(a, wo[cross]).astype(F32)

    def chip_sum(i):
        rows = pl.ds(*CHUNKS[i])
        ar_mate(i).wait_recv()
        for j in range(2):
            both = keep[j, rows, :] + ra[j, rows, :].astype(F32)
            keep[j, rows, :] = both
            sx[1 - j, rows, :] = both.astype(BF16)
        ar_x(i).start()

    def middle(i):
        rows = pl.ds(*CHUNKS[i])
        ar_x(i).wait_recv()
        for j, col in enumerate((m, cross)):
            mid[col, rows, :] = (
                tok[t, col, rows, :].astype(F32) + (keep[j, rows, :] + rx[j, rows, :].astype(F32))
            ).astype(BF16)
            mid_copy(i, j, col).start()

    def gate(i):
        r0, n = CHUNKS[i]
        rows = pl.ds(r0, n)
        for j, col in enumerate((mate, diag)):
            mid_copy(i, j, col).wait_recv()

        @pl.loop(0, n // 32)
        def _(rt):
            norm_rows(lambda b, at, k: mid[b, pl.ds(at, k), :], 1,
                      pl.multiple_of(r0 + rt * 32, 32), 32)

        both = jnp.dot(nrm[rows, :], wg[...], preferred_element_type=F32)
        gated = (both[:, :C] * jax.nn.sigmoid(both[:, C:])).astype(BF16).astype(F32)
        for k in range(tiles):
            ext[k, pl.ds(HALO + r0, n), :] = gated[:, k * LANES:(k + 1) * LANES]

    half = (taps - 1) // 2
    RT = 64
    places, place = [], 0
    for region in REGIONS:
        first = place
        spots = []
        for r0, n in region:
            spots.append((r0, n, place))
            place += n
        places.append((first, place - first, spots))

    def rs_a(i):
        rows = pl.ds(*places[i][:2])
        return rcopy(sa2.at[rows], ra2.at[rows], rs_send.at[i, 0], rs_recv.at[i, 0], mp=mate)

    def rs_x(i):
        rows = pl.ds(*places[i][:2])
        return rcopy(sx2.at[rows], rx2.at[rows], rs_send.at[i, 1], rs_recv.at[i, 1], mp=cross)

    def rs_b(i):
        rows = pl.ds(*places[i][:2])
        return rcopy(sb2.at[rows], rb2.at[rows], rs_send.at[i, 2], rs_recv.at[i, 2], mp=mate)

    def convolve_rows(r0, n, to):
        here = segcol[pl.ds(r0, n), :]
        groups = [pl.ds(k * LANES, LANES) for k in range(tiles)]
        depth = [jnp.zeros((n, LANES), F32) for _ in groups]
        for j in range(taps):
            at = pl.ds(r0 + (j + HALO - half), n)
            same = seg_ext[0, at, :] == here
            for k, g in enumerate(groups):
                depth[k] += jnp.where(same, ext[k, at, :], 0.0) * wdf[pl.ds(j, 1), g]
        for k, g in enumerate(groups):
            z = depth[k] * bns[:, g] + bnb[:, g]
            swi[pl.ds(to, n), g] = (z * jax.nn.sigmoid(z)).astype(BF16)

    def convolve(i):
        for r0, n, to in places[i][2]:
            if n >= RT:
                @pl.loop(0, n // RT)
                def _(rt):
                    convolve_rows(pl.multiple_of(r0 + rt * RT, 16), RT,
                                  pl.multiple_of(to + rt * RT, 16))
            if n % RT:
                done = n - n % RT
                convolve_rows(r0 + done, n % RT, to + done)

        rows = pl.ds(*places[i][:2])
        a = swi[rows, :]
        sa2[rows, :] = rounded(a, wp[diag])
        rs_a(i).start()
        keep2[rows, :] = jnp.dot(a, wp[cross], preferred_element_type=F32)
        sb2[rows, :] = rounded(a, wp[mate])
        rs_b(i).start()

    def pass_on(i):
        rows = pl.ds(*places[i][:2])
        rs_a(i).wait_recv()
        sx2[rows, :] = (keep2[rows, :] + ra2[rows, :].astype(F32)).astype(BF16)
        rs_x(i).start()
        keep2[rows, :] = rounded(swi[rows, :], wp[m]).astype(F32)

    for b in range(M):
        for h in range(heads):
            loads["o", b, h].wait()
    finish(0)
    finish(1)
    chip_sum(0)
    finish(2)
    chip_sum(1)
    split_gates()
    chip_sum(2)
    for b in range(M):
        loads["p", b].wait()
    middle(0)
    gate(0)

    @pl.when(has_right)
    def _():
        halo_right(ext, hg_send, hg_recv).start()

    convolve(0)
    middle(1)
    pass_on(0)
    gate(1)

    @pl.when(has_left)
    def _():
        halo_left(ext, hg_send, hg_recv).start()

    middle(2)
    convolve(1)
    gate(2)
    pass_on(1)

    @pl.when(has_left)
    def _():
        halo_right(seg_ext, hs_send, hs_recv).wait_recv()
        halo_right(ext, hg_send, hg_recv).wait_recv()

    @pl.when(has_right)
    def _():
        halo_left(seg_ext, hs_send, hs_recv).wait_recv()
        halo_left(ext, hg_send, hg_recv).wait_recv()

    convolve(2)
    pass_on(2)
    for i in range(len(REGIONS)):
        rs_b(i).wait_recv()
        rs_x(i).wait_recv()
        for r0, n, to in places[i][2]:
            rows, spot = pl.ds(r0, n), pl.ds(to, n)
            summed = (keep2[spot, :] + rb2[spot, :].astype(F32)) + rx2[spot, :].astype(F32)
            out[rows, :] = (mid[m, rows, :].astype(F32) + summed).astype(BF16)

    for p in range(2):
        for s in range(T):
            @pl.when(jnp.logical_and(s <= t, t < T - 1))
            def _():
                z_right(s, p).wait_send()

            @pl.when(jnp.logical_and(s >= t, t > 0))
            def _():
                z_left(s, p).wait_send()

            over_x(s, m, p).wait_send()
            to_mate(s, m, 0, p).wait_send()
            to_mate(s, cross, 1, p).wait_send()
    for d in range(1, T):
        seg_copy(d).wait_send()

    @pl.when(has_right)
    def _():
        halo_right(seg_ext, hs_send, hs_recv).wait_send()
        halo_right(ext, hg_send, hg_recv).wait_send()

    @pl.when(has_left)
    def _():
        halo_left(seg_ext, hs_send, hs_recv).wait_send()
        halo_left(ext, hg_send, hg_recv).wait_send()

    for i in range(len(CHUNKS)):
        ar_mate(i).wait_send()
        ar_x(i).wait_send()
        mid_copy(i, 0, m).wait_send()
        mid_copy(i, 1, cross).wait_send()
    for i in range(len(REGIONS)):
        rs_a(i).wait_send()
        rs_x(i).wait_send()
        rs_b(i).wait_send()


def fused_device(
    tokens, segment_ids, ln_att_gain, w_query, w_keyval, w_out, ln_conv_gain, w_glu,
    w_depth, bn_scale, bn_shift, w_proj,
):
    R, C = tokens.shape
    D = ln_att_gain.shape[0]
    T = lax.axis_size("tm")
    M = D // C
    heads = C // HEAD_DIM
    HP = heads * LANES
    tiles = C // LANES
    taps = w_depth.shape[0]
    vmem = pl.BlockSpec(memory_space=pltpu.VMEM)
    hbm = pl.BlockSpec(memory_space=pltpu.HBM)
    dma = pltpu.SemaphoreType.DMA
    NC, NR = len(CHUNKS), len(REGIONS)
    part, pair = pltpu.VMEM((R, C), BF16), pltpu.VMEM((2, R, C), BF16)
    return pl.pallas_call(
        functools.partial(block_kernel, T, taps),
        out_shape=jax.ShapeDtypeStruct((R, C), BF16),
        in_specs=[hbm] * 12,
        out_specs=vmem,
        scratch_shapes=[
            pltpu.VMEM((R,), jnp.int32), pltpu.VMEM((D,), F32), pltpu.VMEM((D,), F32),
            pltpu.VMEM((taps, C), BF16), pltpu.VMEM((C,), F32), pltpu.VMEM((C,), F32), dma((7,)),
            pltpu.VMEM((R, LANES), jnp.int32),
            pltpu.VMEM((2, 1, D), F32),
            pltpu.VMEM((1, C), F32),
            pltpu.VMEM((1, C), F32),
            pltpu.VMEM((T, M, R, C), BF16),
            pltpu.VMEM((T, 8, R), jnp.int32),
            pltpu.VMEM((1, R + 2 * HALO, LANES), jnp.int32),
            pltpu.VMEM((D, C), BF16),
            pltpu.VMEM((2, tiles, D, 2, LANES), BF16),
            pltpu.VMEM((tiles, 512, LANES), F32),
            pltpu.VMEM((heads, R, R), F32),
            pltpu.VMEM((heads, R, R), BF16),
            pltpu.VMEM((D, HP), BF16),
            pltpu.VMEM((D, 2 * HP), BF16),
            pltpu.VMEM((M, HP, C), BF16),
            pltpu.VMEM((D, 2 * C), BF16),
            pltpu.VMEM((M, C, C), BF16),
            pltpu.VMEM((R, D), BF16),
            pltpu.VMEM((R, HP), BF16),
            pltpu.VMEM((R, HP), BF16),
            pltpu.VMEM((R, HP), BF16),
            pltpu.VMEM((heads, R, LANES), F32),
            pltpu.VMEM((heads, R, LANES), F32),
            pltpu.VMEM((R, HP), F32),
            pltpu.VMEM((R, HP), BF16),
            part,
            pltpu.VMEM((2, R, C), F32),
            pltpu.VMEM((R, C), F32),
            pltpu.VMEM((M, R, C), BF16),
            pltpu.VMEM((tiles, R + 2 * HALO, LANES), F32),
            pltpu.VMEM((32, C), F32),
            pair, pair, pair, pair, part, part, part, part, part, part,
            dma((2 * tiles + 1 + M * heads + M,)),
            dma((T, M, 2)), dma((2, T, 2)), dma((T, 2)), dma((T, 2, 2)),
            dma((T,)), dma((T,)), dma((2,)), dma((2,)), dma((2,)), dma((2,)),
            dma((NC, 2)), dma((NC, 2)), dma((NC, 2)), dma((NC, 2)), dma((NR, 3)), dma((NR, 3)),
        ],
        compiler_params=pltpu.CompilerParams(
            collective_id=0, has_side_effects=True, vmem_limit_bytes=52 * 2**20
        ),
    )(*[
        pltpu.with_memory_space_constraint(x, pltpu.HBM)
        for x in (tokens, segment_ids, ln_att_gain, w_query, w_keyval, w_out, ln_conv_gain,
                  w_glu, w_depth, bn_scale, bn_shift, w_proj)
    ])


def solution(mesh):
    placed = (
        P(("group", "tm"), "mp"),
        P(("group", "tm")),
        P(),
        P(None, "mp"),
        P(None, None, "mp"),
        P("mp", None),
        P(),
        P(None, None, "mp"),
        P(None, "mp"),
        P("mp"),
        P("mp"),
        P("mp", None),
    )
    fused = mesh.shape["tm"] == 4 and mesh.shape["mp"] == 4
    return jax.shard_map(
        fused_device if fused else per_device, mesh=mesh, in_specs=placed, out_specs=P(("group", "tm"), "mp"), check_vma=False
    )
```

```python
import functools

import jax
import jax.numpy as jnp
from jax import lax
from jax.experimental import pallas as pl
from jax.experimental.pallas import tpu as pltpu
from jax.sharding import PartitionSpec as P

HEAD_DIM = 96


def with_halo(value, sides, width):
    for axis, dim in sides:
        count, length = (lax.axis_size(axis), value.shape[dim])
        up = [(i, (i + 1) % count) for i in range(count - 1)]
        down = [(j, i) for i, j in up]
        last = lax.slice_in_dim(value, length - width, length, axis=dim)
        initial = lax.slice_in_dim(value, 0, width, axis=dim)
        before = lax.ppermute(last, axis, up)
        after = lax.ppermute(initial, axis, down)
        value = jnp.concatenate([before, value, after], axis=dim)
    return value


def layer_norm(values_in, gain_vec):
    row_mean = jnp.mean(values_in, axis=-1, keepdims=True)
    centered = values_in - row_mean
    spread = jnp.mean(centered * centered, axis=-1, keepdims=True)
    return centered * lax.rsqrt(spread + 1e-05) * gain_vec


def fold_keys(carry_state, query_heads, query_segs, keyval, key_segs, local_cols, score_scale):
    row_max, weight_sum, weighted = carry_state
    key_rows = keyval.shape[0]
    heads_here = query_heads.shape[1]
    key_part = keyval[:, :local_cols].reshape(key_rows, heads_here, -1)
    value_part = keyval[:, local_cols:].reshape(key_rows, heads_here, -1)
    scores = (
        jnp.einsum("qhd,khd->qhk", query_heads, key_part, preferred_element_type=jnp.float32)
        * score_scale
    )
    same_seg = (query_segs[:, None] == key_segs[None, :])[:, None, :]
    scores = jnp.where(same_seg, scores, -jnp.inf)
    new_max = jnp.maximum(row_max, jnp.max(scores, axis=2))
    safe_max = jnp.where(new_max == -jnp.inf, 0.0, new_max)
    weights = jnp.exp(scores - safe_max[:, :, None])
    factor = jnp.exp(row_max - safe_max)
    weight_sum = weight_sum * factor + jnp.sum(weights, axis=2)
    weighted = weighted * factor[:, :, None] + jnp.einsum(
        "qhk,khd->qhd", weights.astype(jnp.bfloat16), value_part, preferred_element_type=jnp.float32
    )
    return (new_max, weight_sum, weighted)


def maybe_fold(carry_state, query_heads, query_segs, keyval, key_segs, local_cols, score_scale):
    return fold_keys(
        carry_state, query_heads, query_segs, keyval, key_segs, local_cols, score_scale
    )


def per_device(
    tokens,
    segment_ids,
    ln_att_gain,
    w_query,
    w_keyval,
    w_out,
    ln_conv_gain,
    w_glu,
    w_depth,
    bn_scale,
    bn_shift,
    w_proj,
):
    row_count = tokens.shape[0]
    full_width = ln_att_gain.shape[0]
    local_cols = w_query.shape[1]
    heads_here = local_cols // HEAD_DIM
    score_scale = HEAD_DIM ** (-0.5)
    all_segs = lax.all_gather(segment_ids, "tm", axis=0, tiled=True)
    anchor = lax.axis_index("tm") * row_count
    whole_rows = lax.all_gather(tokens, "mp", axis=1, tiled=True)
    normed = layer_norm(whole_rows.astype(jnp.float32), ln_att_gain).astype(jnp.bfloat16)
    queries = jnp.dot(normed, w_query, preferred_element_type=jnp.float32).astype(jnp.bfloat16)
    keyval = jnp.dot(
        normed, w_keyval.reshape(full_width, -1), preferred_element_type=jnp.float32
    ).astype(jnp.bfloat16)
    query_heads = queries.reshape(row_count, heads_here, HEAD_DIM)
    initial = (
        jnp.full((row_count, heads_here), -jnp.inf, jnp.float32),
        jnp.zeros((row_count, heads_here), jnp.float32),
        jnp.zeros((row_count, heads_here, HEAD_DIM), jnp.float32),
    )
    segment = lax.all_gather(keyval, "tm", axis=0, tiled=True)
    piece_rows = segment.shape[0]
    block_count = piece_rows // row_count

    def inner_step(state_in, element):
        return (
            maybe_fold(
                state_in, query_heads, segment_ids, element[0], element[1], local_cols, score_scale
            ),
            None,
        )

    stacked = (
        segment.reshape(block_count, row_count, -1),
        all_segs.reshape(block_count, row_count),
    )
    result, unused = lax.scan(inner_step, initial, stacked)
    row_max, weight_sum, weighted = result
    context = (
        (weighted / weight_sum[:, :, None]).reshape(row_count, local_cols).astype(jnp.bfloat16)
    )
    att_terms = jnp.dot(context, w_out, preferred_element_type=jnp.float32)
    att_summed = lax.psum_scatter(
        att_terms.astype(jnp.bfloat16), "mp", scatter_dimension=1, tiled=True
    ).astype(jnp.float32)
    middle = (tokens.astype(jnp.float32) + att_summed).astype(jnp.bfloat16)
    whole_mid = lax.all_gather(middle, "mp", axis=1, tiled=True)
    normed_conv = layer_norm(whole_mid.astype(jnp.float32), ln_conv_gain).astype(jnp.bfloat16)
    both_halves = jnp.dot(
        normed_conv, w_glu.reshape(full_width, -1), preferred_element_type=jnp.float32
    )
    gated = (both_halves[:, :local_cols] * jax.nn.sigmoid(both_halves[:, local_cols:])).astype(
        jnp.bfloat16
    )
    half_width = (w_depth.shape[0] - 1) // 2
    extended = with_halo(gated, (("tm", 0),), half_width).astype(jnp.float32)
    padded_segs = jnp.pad(all_segs, (half_width, half_width), constant_values=-1)
    window_segs = lax.dynamic_slice_in_dim(padded_segs, anchor, row_count + 2 * half_width, 0)
    depth = jnp.zeros((row_count, local_cols), jnp.float32)
    for tap_index in range(w_depth.shape[0]):
        same_seg = (window_segs[tap_index : tap_index + row_count] == segment_ids)[:, None]
        shifted = jnp.where(same_seg, extended[tap_index : tap_index + row_count], 0.0)
        depth = depth + shifted * w_depth[tap_index].astype(jnp.float32)
    normalized = depth * bn_scale + bn_shift
    swished = (normalized * jax.nn.sigmoid(normalized)).astype(jnp.bfloat16)
    conv_terms = jnp.dot(swished, w_proj, preferred_element_type=jnp.float32)
    conv_summed = lax.psum_scatter(
        conv_terms.astype(jnp.bfloat16), "mp", scatter_dimension=1, tiled=True
    ).astype(jnp.float32)
    return (middle.astype(jnp.float32) + conv_summed).astype(jnp.bfloat16)


NEG = -1e30
HALO = 16
LANES = 128
PIECES = ((0, 128), (128, 128), (256, 128))
RS = 128
CHUNKS = ((224, 160), (0, 160), (160, 64))
REGIONS = (((240, 128),), ((16, 128),), ((144, 96), (0, 16), (368, 16)))
MESH = pl.DeviceIdType.MESH
F32 = jnp.float32
BF16 = jnp.bfloat16


def block_kernel(
    T, taps,
    tokens_h, seg_h, g_att_h, wq_h, wkv_h, wo_h, g_conv_h, wg_h, wdep_h, bn_s_h, bn_b_h, wp_h,
    out, seg, g_att, g_conv, wdep, bn_s, bn_b, small, segcol, gains, bns, bnb,
    tok, seg_all, seg_ext, rawq, raw, wide32, sc, pw, wq, wkv, wo, wg, wp, nrm, qp, kp, vp, mst, lst, acc,
    ctx, swi, keep, keep2, mid, ext, wdf, sa, ra, sx, rx, sa2, ra2, sx2, rx2, sb2, rb2,
    wsem, tok_recv, z_send, x_send, m_send, r_send, seg_send, seg_recv, hs_send, hs_recv,
    hg_send, hg_recv, ar_send, ar_recv, mid_send, mid_recv, rs_send, rs_recv,
):
    R, C = tokens_h.shape
    M = 4
    D = M * C
    heads = C // HEAD_DIM
    HP = heads * LANES
    tiles = C // LANES
    t = lax.axis_index("tm")
    m = lax.axis_index("mp")
    mate = m + 1 - 2 * (m % 2)
    cross = (m + 2) % 4
    diag = (mate + 2) % 4

    def rcopy(src, dst, ssem, rsem, **dev):
        return pltpu.make_async_remote_copy(
            src_ref=src, dst_ref=dst, send_sem=ssem, recv_sem=rsem,
            device_id=dev, device_id_type=MESH,
        )

    firsts = [
        pltpu.make_async_copy(src, dst, small.at[i])
        for i, (src, dst) in enumerate([
            (tokens_h, tok.at[t, m]), (seg_h, seg), (g_att_h, g_att), (g_conv_h, g_conv),
            (wdep_h, wdep), (bn_s_h, bn_s), (bn_b_h, bn_b)])
    ]
    loads, at = {}, 0

    def load(name, src, dst):
        nonlocal at
        loads[name] = pltpu.make_async_copy(src, dst, wsem.at[at])
        at += 1

    for k in range(tiles):
        load(("kv", k), wkv_h.at[:, :, pl.ds(k * LANES, LANES)], raw.at[0, k])
    load("q", wq_h, rawq)
    for k in range(tiles):
        load(("g", k), wg_h.at[:, :, pl.ds(k * LANES, LANES)], raw.at[1, k])
    for b in range(M):
        cols = pl.ds(b * C, C)
        for h in range(heads):
            load(("o", b, h), wo_h.at[pl.ds(h * HEAD_DIM, HEAD_DIM), cols],
                 wo.at[b, pl.ds(h * LANES, HEAD_DIM)])
    for b in range(M):
        load(("p", b), wp_h.at[:, pl.ds(b * C, C)], wp.at[b])
    for c in firsts:
        c.start()

    barrier = pltpu.get_barrier_semaphore()
    for peer in (mate, cross):
        pl.semaphore_signal(barrier, inc=1, device_id={"mp": peer}, device_id_type=MESH)
    for d in range(1, T):
        pl.semaphore_signal(
            barrier, inc=1, device_id={"tm": (t + d) % T}, device_id_type=MESH
        )
    for c in loads.values():
        c.start()
    for c in firsts:
        c.wait()
    ids = seg[...].reshape(1, R)
    seg_all[t] = jnp.broadcast_to(ids, (8, R))
    pl.semaphore_wait(barrier, 1 + T)

    def z_right(s, p):
        piece = tok.at[s, m, pl.ds(*PIECES[p])]
        return rcopy(piece, piece, z_send.at[0, s, p], tok_recv.at[s, m, p], tm=(t + 1) % T)

    def z_left(s, p):
        piece = tok.at[s, m, pl.ds(*PIECES[p])]
        return rcopy(piece, piece, z_send.at[1, s, p], tok_recv.at[s, m, p], tm=(t + T - 1) % T)

    def over_x(s, col, p):
        piece = tok.at[s, col, pl.ds(*PIECES[p])]
        return rcopy(piece, piece, x_send.at[s, p], tok_recv.at[s, col, p], mp=cross)

    def to_mate(s, col, k, p):
        piece = tok.at[s, col, pl.ds(*PIECES[p])]
        return rcopy(piece, piece, m_send.at[s, k, p], tok_recv.at[s, col, p], mp=mate)

    def launch(s, p):
        @pl.when(jnp.logical_and(s <= t, t < T - 1))
        def _():
            z_right(s, p).start()

        @pl.when(jnp.logical_and(s >= t, t > 0))
        def _():
            z_left(s, p).start()

    def straight(s, p):
        inner = jnp.logical_and(s > 0, s < T - 1)
        return jnp.logical_or(p < 2, jnp.logical_or(s == t, inner))

    def round_right(s):
        piece = tok.at[s, cross, pl.ds(*PIECES[2])]
        return rcopy(piece, piece, r_send.at[0], tok_recv.at[s, cross, 2], tm=(t + 1) % T)

    def round_left(s):
        piece = tok.at[s, cross, pl.ds(*PIECES[2])]
        return rcopy(piece, piece, r_send.at[1], tok_recv.at[s, cross, 2], tm=(t + T - 1) % T)

    def send_round(s):
        @pl.when(jnp.logical_and(s == 0, t < T - 1))
        def _():
            round_right(s).start()

        @pl.when(jnp.logical_and(s == T - 1, t > 0))
        def _():
            round_left(s).start()

    for p in range(3):
        over_x(t, m, p).start()
        launch(t, p)
        to_mate(t, m, 0, p).start()

    def seg_copy(d):
        return rcopy(seg_all.at[t], seg_all.at[t], seg_send.at[d], seg_recv.at[t],
                     tm=(t + d) % T)

    for d in range(1, T):
        seg_copy(d).start()

    def halo_right(ref, ssem, rsem):
        return rcopy(ref.at[:, pl.ds(R, HALO)], ref.at[:, pl.ds(0, HALO)], ssem.at[0],
                     rsem.at[0], tm=(t + 1) % T)

    def halo_left(ref, ssem, rsem):
        return rcopy(ref.at[:, pl.ds(HALO, HALO)], ref.at[:, pl.ds(R + HALO, HALO)],
                     ssem.at[1], rsem.at[1], tm=(t + T - 1) % T)

    has_right = t < T - 1
    has_left = t > 0
    edge = jnp.logical_or(t == 0, t == T - 1)

    segcol[...] = jnp.transpose(jnp.broadcast_to(ids, (LANES, R)))
    seg_ext[0, pl.ds(HALO, R), :] = segcol[...]

    @pl.when(has_right)
    def _():
        halo_right(seg_ext, hs_send, hs_recv).start()

    @pl.when(has_left)
    def _():
        halo_left(seg_ext, hs_send, hs_recv).start()

    @pl.when(jnp.logical_not(has_left))
    def _():
        seg_ext[0, pl.ds(0, HALO), :] = jnp.full((HALO, LANES), -1, jnp.int32)
        ext[:, pl.ds(0, HALO), :] = jnp.zeros((tiles, HALO, LANES), F32)

    @pl.when(jnp.logical_not(has_right))
    def _():
        seg_ext[0, pl.ds(R + HALO, HALO), :] = jnp.full((HALO, LANES), -1, jnp.int32)
        ext[:, pl.ds(R + HALO, HALO), :] = jnp.zeros((tiles, HALO, LANES), F32)

    gains[0] = g_att[...].reshape(1, D)
    gains[1] = g_conv[...].reshape(1, D)
    bns[...] = bn_s[...].reshape(1, C)
    bnb[...] = bn_b[...].reshape(1, C)

    def by_head(x):
        gap = jnp.zeros((x.shape[0], LANES - HEAD_DIM), F32)
        cols = []
        for h in range(heads):
            cols += [x[:, h * HEAD_DIM:(h + 1) * HEAD_DIM], gap]
        return jnp.concatenate(cols, axis=1).astype(BF16)

    for k in range(tiles):
        loads["kv", k].wait()

    def widen(b, i, n):
        for k in range(tiles):
            wide32[k, pl.ds(0, 2 * n), :] = raw.at[b, k].reshape(2 * D, LANES)[
                pl.ds(pl.multiple_of(i * 2 * n, 2 * n), 2 * n), :].astype(F32)

    @pl.loop(0, D // 256)
    def _(i):
        rows = pl.ds(pl.multiple_of(i * 256, 256), 256)
        widen(0, i, 256)
        for j in range(2):
            x = jnp.concatenate([wide32[k, pl.ds(j, 256, 2), :] for k in range(tiles)], axis=1)
            wkv[rows, pl.ds(j * HP, HP)] = by_head(x)

    loads["q"].wait()

    @pl.loop(0, D // 256)
    def _(i):
        rows = pl.ds(pl.multiple_of(i * 256, 256), 256)
        wq[rows, :] = by_head(rawq[rows, :].astype(F32))

    def split_gates():
        for k in range(tiles):
            loads["g", k].wait()

        @pl.loop(0, D // 128)
        def _(i):
            rows = pl.ds(pl.multiple_of(i * 128, 128), 128)
            widen(1, i, 128)
            for j in range(2):
                for k in range(tiles):
                    wg[rows, pl.ds(j * C + k * LANES, LANES)] = (
                        wide32[k, pl.ds(j, 128, 2), :].astype(BF16))

    wdf[pl.ds(0, taps), :] = wdep[...].astype(F32)
    mst[...] = jnp.full(mst.shape, NEG, F32)
    lst[...] = jnp.zeros(lst.shape, F32)
    acc[...] = jnp.zeros(acc.shape, F32)
    for b in range(M):
        for h in range(heads):
            wo[b, pl.ds(h * LANES + HEAD_DIM, LANES - HEAD_DIM), :] = jnp.zeros(
                (LANES - HEAD_DIM, C), BF16)

    def norm_rows(load_part, gain, r0, n):
        parts = [load_part(b, r0, n).astype(F32) for b in range(M)]
        total = parts[0] + parts[1] + parts[2] + parts[3]
        mean = jnp.sum(total, axis=1, keepdims=True) * (1.0 / D)
        parts = [p - mean for p in parts]
        sq = parts[0] * parts[0]
        for p in parts[1:]:
            sq = sq + p * p
        inv = lax.rsqrt(jnp.sum(sq, axis=1, keepdims=True) * (1.0 / D) + 1e-05)
        for b in range(M):
            nrm[pl.ds(r0, n), pl.ds(b * C, C)] = (
                parts[b] * inv * gains[gain, :, pl.ds(b * C, C)]
            ).astype(BF16)

    coef = float(HEAD_DIM ** (-0.5) * 1.4426950408889634)

    hs = range(heads)

    def lanes(h):
        return pl.ds(h * LANES, LANES)

    def weigh(s, r0, n, c0, nk, score, keep_weights):
        rows, keys = pl.ds(r0, n), pl.ds(c0, nk)

        def fold(x):
            return sum(x[:, k * LANES:(k + 1) * LANES] for k in range(1, nk // LANES)) + x[:, :LANES]

        def wide(col):
            return jnp.concatenate([col] * (nk // LANES), axis=1)

        bias = jnp.where(wide(segcol[rows, :]) == seg_all[s, pl.ds(0, 1), keys], 0.0, NEG)
        xs = [score(h) + bias for h in hs]
        olds = [mst[h, rows, :] for h in hs]
        sums = [lst[h, rows, :] for h in hs]
        accs = [acc[rows, lanes(h)] for h in hs]
        news = [jnp.maximum(o, jnp.max(x, axis=1, keepdims=True)) for o, x in zip(olds, xs)]
        fs = [jnp.exp2((o - v) * coef) for o, v in zip(olds, news)]
        ps = [jnp.exp2((x - wide(v)) * coef) for x, v in zip(xs, news)]
        sums = [v * f + fold(w) for v, f, w in zip(sums, fs, ps)]
        for h in hs:
            mst[h, rows, :] = news[h]
            lst[h, rows, :] = sums[h]
        keep_weights([w.astype(BF16) for w in ps], [a * f for a, f in zip(accs, fs)])

    def score_block(r0, n, c0, nk, h):
        return lax.dot_general(
            qp[pl.ds(r0, n), lanes(h)], kp[pl.ds(c0, nk), lanes(h)], (((1,), (1,)), ((), ())),
            preferred_element_type=F32)

    def attend(s, c0, nk):
        keys = pl.ds(c0, nk)
        for h in hs:
            sc[h, :, pl.ds(0, nk)] = score_block(0, R, c0, nk, h)

        @pl.loop(0, R // RS)
        def _(rt):
            r0 = pl.multiple_of(rt * RS, RS)
            rows = pl.ds(r0, RS)

            def kept(ws, scaled):
                for h in hs:
                    pw[h, rows, pl.ds(0, nk)] = ws[h]
                    acc[rows, lanes(h)] = scaled[h]

            weigh(s, r0, RS, c0, nk, lambda h: sc[h, rows, pl.ds(0, nk)], kept)

        for h in hs:
            acc[:, lanes(h)] += jnp.dot(
                pw[h, :, pl.ds(0, nk)], vp[keys, lanes(h)], preferred_element_type=F32)

    def attend_last(s, r0, n, c0, nk):
        rows, keys = pl.ds(r0, n), pl.ds(c0, nk)

        def kept(ws, scaled):
            for h in hs:
                total = scaled[h] + jnp.dot(
                    ws[h], vp[keys, lanes(h)], preferred_element_type=F32)
                den = jnp.sum(lst[h, rows, :], axis=1, keepdims=True)
                ctx[rows, lanes(h)] = (total / den).astype(BF16)

        weigh(s, r0, n, c0, nk, lambda h: score_block(r0, n, c0, nk, h), kept)

    def project(s, r0, n, with_queries, midway):
        rows = pl.ds(r0, n)

        @pl.loop(0, n // 128)
        def _(rt):
            norm_rows(lambda b, at, k: tok[s, b, pl.ds(at, k), :], 0,
                      pl.multiple_of(r0 + rt * 128, 128), 128)

        if with_queries is not None:
            @pl.when(with_queries)
            def _():
                qp[rows, :] = jnp.dot(
                    nrm[rows, :], wq[...], preferred_element_type=F32).astype(BF16)

        kp[rows, :] = jnp.dot(
            nrm[rows, :], wkv[:, pl.ds(0, HP)], preferred_element_type=F32).astype(BF16)
        midway()
        vp[rows, :] = jnp.dot(
            nrm[rows, :], wkv[:, pl.ds(HP, HP)], preferred_element_type=F32).astype(BF16)

    def digit(code, i):
        return (code // (T ** i)) % T

    order = 228 - 3 * ((t + 3) // 4) - 195 * ((t + 2) // 4) - 3 * ((t + 1) // 4)

    def take(s, p):
        over_x(s, cross, p).wait_recv()
        to_mate(s, cross, 1, p).start()

    def arrive(s, p):
        to_mate(s, mate, 0, p).wait_recv()
        to_mate(s, diag, 1, p).wait_recv()

    def ids_arrive(s):
        rcopy(seg_all.at[s], seg_all.at[s], seg_send.at[0], seg_recv.at[s],
              tm=(t + 1) % T).wait_recv()

    def block_step(i, code):
        s, nxt, after = digit(code, 0), digit(code, 1), digit(code, 2)

        def relay(ps):
            for p in ps:
                @pl.when(jnp.logical_or(i == 0, edge))
                def _():
                    z_right(nxt, p).wait_recv()
                    launch(nxt, p)

                @pl.when(straight(nxt, p))
                def _():
                    over_x(nxt, m, p).start()

                to_mate(nxt, m, 0, p).start()

                @pl.when(jnp.logical_and(jnp.logical_not(edge), i < 2))
                def _():
                    z_right(after, p).wait_recv()
                    launch(after, p)

            for p in ps:
                take(s, p)
                if p == 2:
                    send_round(s)

        @pl.when(jnp.logical_and(jnp.logical_not(edge), i == T - 2))
        def _():
            take(nxt, 2)
            send_round(nxt)

        relay((0, 1))

        @pl.when(i > 0)
        def _():
            ids_arrive(s)

        arrive(s, 0)
        arrive(s, 1)
        project(s, 0, 256, i == 0, lambda: relay((2,)))
        arrive(s, 2)
        project(s, 256, 128, i == 0, lambda: None)

        @pl.when(i == T - 2)
        def _():
            take(nxt, 0)

        @pl.when(jnp.logical_and(edge, i == T - 2))
        def _():
            take(nxt, 2)

        attend(s, 0, R)
        return code // T

    final = digit(order, T - 1)
    lax.fori_loop(0, T - 1, block_step, order)
    ids_arrive(final)
    arrive(final, 2)
    project(final, 256, 128, None, lambda: take(final, 1))
    arrive(final, 0)
    project(final, 0, 128, None, lambda: None)
    arrive(final, 1)
    project(final, 128, 128, None, lambda: None)

    def ar_mate(i):
        rows = pl.ds(*CHUNKS[i])
        return rcopy(sa.at[:, rows], ra.at[:, rows], ar_send.at[i, 0], ar_recv.at[i, 0], mp=mate)

    def ar_x(i):
        rows = pl.ds(*CHUNKS[i])
        return rcopy(sx.at[:, rows], rx.at[:, rows], ar_send.at[i, 1], ar_recv.at[i, 1], mp=cross)

    def mid_copy(i, j, col):
        piece = mid.at[col, pl.ds(*CHUNKS[i])]
        return rcopy(piece, piece, mid_send.at[i, j], mid_recv.at[i, j], mp=mate)

    def rounded(a, w):
        return jnp.dot(a, w, preferred_element_type=F32).astype(BF16)

    def finish(i):
        r0, n = CHUNKS[i]
        rows = pl.ds(r0, n)
        attend_last(final, r0, n, 0, R)
        a = ctx[rows, :]
        sa[0, rows, :] = rounded(a, wo[mate])
        sa[1, rows, :] = rounded(a, wo[diag])
        ar_mate(i).start()
        keep[0, rows, :] = rounded(a, wo[m]).astype(F32)
        keep[1, rows, :] = rounded(a, wo[cross]).astype(F32)

    def chip_sum(i):
        rows = pl.ds(*CHUNKS[i])
        ar_mate(i).wait_recv()
        for j in range(2):
            both = keep[j, rows, :] + ra[j, rows, :].astype(F32)
            keep[j, rows, :] = both
            sx[1 - j, rows, :] = both.astype(BF16)
        ar_x(i).start()

    def middle(i):
        rows = pl.ds(*CHUNKS[i])
        ar_x(i).wait_recv()
        for j, col in enumerate((m, cross)):
            mid[col, rows, :] = (
                tok[t, col, rows, :].astype(F32) + (keep[j, rows, :] + rx[j, rows, :].astype(F32))
            ).astype(BF16)
            mid_copy(i, j, col).start()

    def gate(i):
        r0, n = CHUNKS[i]
        rows = pl.ds(r0, n)
        for j, col in enumerate((mate, diag)):
            mid_copy(i, j, col).wait_recv()

        @pl.loop(0, n // 32)
        def _(rt):
            norm_rows(lambda b, at, k: mid[b, pl.ds(at, k), :], 1,
                      pl.multiple_of(r0 + rt * 32, 32), 32)

        both = jnp.dot(nrm[rows, :], wg[...], preferred_element_type=F32)
        gated = (both[:, :C] * jax.nn.sigmoid(both[:, C:])).astype(BF16).astype(F32)
        for k in range(tiles):
            ext[k, pl.ds(HALO + r0, n), :] = gated[:, k * LANES:(k + 1) * LANES]

    half = (taps - 1) // 2
    RT = 64
    places, place = [], 0
    for region in REGIONS:
        first = place
        spots = []
        for r0, n in region:
            spots.append((r0, n, place))
            place += n
        places.append((first, place - first, spots))

    def rs_a(i):
        rows = pl.ds(*places[i][:2])
        return rcopy(sa2.at[rows], ra2.at[rows], rs_send.at[i, 0], rs_recv.at[i, 0], mp=mate)

    def rs_x(i):
        rows = pl.ds(*places[i][:2])
        return rcopy(sx2.at[rows], rx2.at[rows], rs_send.at[i, 1], rs_recv.at[i, 1], mp=cross)

    def rs_b(i):
        rows = pl.ds(*places[i][:2])
        return rcopy(sb2.at[rows], rb2.at[rows], rs_send.at[i, 2], rs_recv.at[i, 2], mp=mate)

    def convolve_rows(r0, n, to):
        here = segcol[pl.ds(r0, n), :]
        groups = [pl.ds(k * LANES, LANES) for k in range(tiles)]
        depth = [jnp.zeros((n, LANES), F32) for _ in groups]
        for j in range(taps):
            at = pl.ds(r0 + (j + HALO - half), n)
            same = seg_ext[0, at, :] == here
            for k, g in enumerate(groups):
                depth[k] += jnp.where(same, ext[k, at, :], 0.0) * wdf[pl.ds(j, 1), g]
        for k, g in enumerate(groups):
            z = depth[k] * bns[:, g] + bnb[:, g]
            swi[pl.ds(to, n), g] = (z * jax.nn.sigmoid(z)).astype(BF16)

    def convolve(i):
        for r0, n, to in places[i][2]:
            if n >= RT:
                @pl.loop(0, n // RT)
                def _(rt):
                    convolve_rows(pl.multiple_of(r0 + rt * RT, 16), RT,
                                  pl.multiple_of(to + rt * RT, 16))
            if n % RT:
                done = n - n % RT
                convolve_rows(r0 + done, n % RT, to + done)

        rows = pl.ds(*places[i][:2])
        a = swi[rows, :]
        sa2[rows, :] = rounded(a, wp[diag])
        rs_a(i).start()
        keep2[rows, :] = jnp.dot(a, wp[cross], preferred_element_type=F32)
        sb2[rows, :] = rounded(a, wp[mate])
        rs_b(i).start()

    def pass_on(i):
        rows = pl.ds(*places[i][:2])
        rs_a(i).wait_recv()
        sx2[rows, :] = (keep2[rows, :] + ra2[rows, :].astype(F32)).astype(BF16)
        rs_x(i).start()
        keep2[rows, :] = rounded(swi[rows, :], wp[m]).astype(F32)

    for b in range(M):
        for h in range(heads):
            loads["o", b, h].wait()
    finish(0)
    finish(1)
    chip_sum(0)
    finish(2)
    chip_sum(1)
    split_gates()
    chip_sum(2)
    for b in range(M):
        loads["p", b].wait()
    middle(0)
    gate(0)

    @pl.when(has_right)
    def _():
        halo_right(ext, hg_send, hg_recv).start()

    convolve(0)
    middle(1)
    pass_on(0)
    gate(1)

    @pl.when(has_left)
    def _():
        halo_left(ext, hg_send, hg_recv).start()

    middle(2)
    convolve(1)
    gate(2)
    pass_on(1)

    @pl.when(has_left)
    def _():
        halo_right(seg_ext, hs_send, hs_recv).wait_recv()
        halo_right(ext, hg_send, hg_recv).wait_recv()

    @pl.when(has_right)
    def _():
        halo_left(seg_ext, hs_send, hs_recv).wait_recv()
        halo_left(ext, hg_send, hg_recv).wait_recv()

    convolve(2)
    pass_on(2)
    for i in range(len(REGIONS)):
        rs_b(i).wait_recv()
        rs_x(i).wait_recv()
        for r0, n, to in places[i][2]:
            rows, spot = pl.ds(r0, n), pl.ds(to, n)
            summed = (keep2[spot, :] + rb2[spot, :].astype(F32)) + rx2[spot, :].astype(F32)
            out[rows, :] = (mid[m, rows, :].astype(F32) + summed).astype(BF16)

    @pl.when(has_right)
    def _():
        round_right(0).wait_send()

    @pl.when(has_left)
    def _():
        round_left(T - 1).wait_send()

    for p in range(3):
        for s in range(T):
            @pl.when(jnp.logical_and(s <= t, t < T - 1))
            def _():
                z_right(s, p).wait_send()

            @pl.when(jnp.logical_and(s >= t, t > 0))
            def _():
                z_left(s, p).wait_send()

            @pl.when(straight(s, p))
            def _():
                over_x(s, m, p).wait_send()

            to_mate(s, m, 0, p).wait_send()
            to_mate(s, cross, 1, p).wait_send()
    for d in range(1, T):
        seg_copy(d).wait_send()

    @pl.when(has_right)
    def _():
        halo_right(seg_ext, hs_send, hs_recv).wait_send()
        halo_right(ext, hg_send, hg_recv).wait_send()

    @pl.when(has_left)
    def _():
        halo_left(seg_ext, hs_send, hs_recv).wait_send()
        halo_left(ext, hg_send, hg_recv).wait_send()

    for i in range(len(CHUNKS)):
        ar_mate(i).wait_send()
        ar_x(i).wait_send()
        mid_copy(i, 0, m).wait_send()
        mid_copy(i, 1, cross).wait_send()
    for i in range(len(REGIONS)):
        rs_a(i).wait_send()
        rs_x(i).wait_send()
        rs_b(i).wait_send()


def fused_device(
    tokens, segment_ids, ln_att_gain, w_query, w_keyval, w_out, ln_conv_gain, w_glu,
    w_depth, bn_scale, bn_shift, w_proj,
):
    R, C = tokens.shape
    D = ln_att_gain.shape[0]
    T = lax.axis_size("tm")
    M = D // C
    heads = C // HEAD_DIM
    HP = heads * LANES
    tiles = C // LANES
    taps = w_depth.shape[0]
    vmem = pl.BlockSpec(memory_space=pltpu.VMEM)
    hbm = pl.BlockSpec(memory_space=pltpu.HBM)
    dma = pltpu.SemaphoreType.DMA
    NC, NR = len(CHUNKS), len(REGIONS)
    part, pair = pltpu.VMEM((R, C), BF16), pltpu.VMEM((2, R, C), BF16)
    return pl.pallas_call(
        functools.partial(block_kernel, T, taps),
        out_shape=jax.ShapeDtypeStruct((R, C), BF16),
        in_specs=[hbm] * 12,
        out_specs=vmem,
        scratch_shapes=[
            pltpu.VMEM((R,), jnp.int32), pltpu.VMEM((D,), F32), pltpu.VMEM((D,), F32),
            pltpu.VMEM((taps, C), BF16), pltpu.VMEM((C,), F32), pltpu.VMEM((C,), F32), dma((7,)),
            pltpu.VMEM((R, LANES), jnp.int32),
            pltpu.VMEM((2, 1, D), F32),
            pltpu.VMEM((1, C), F32),
            pltpu.VMEM((1, C), F32),
            pltpu.VMEM((T, M, R, C), BF16),
            pltpu.VMEM((T, 8, R), jnp.int32),
            pltpu.VMEM((1, R + 2 * HALO, LANES), jnp.int32),
            pltpu.VMEM((D, C), BF16),
            pltpu.VMEM((2, tiles, D, 2, LANES), BF16),
            pltpu.VMEM((tiles, 512, LANES), F32),
            pltpu.VMEM((heads, R, R), F32),
            pltpu.VMEM((heads, R, R), BF16),
            pltpu.VMEM((D, HP), BF16),
            pltpu.VMEM((D, 2 * HP), BF16),
            pltpu.VMEM((M, HP, C), BF16),
            pltpu.VMEM((D, 2 * C), BF16),
            pltpu.VMEM((M, C, C), BF16),
            pltpu.VMEM((R, D), BF16),
            pltpu.VMEM((R, HP), BF16),
            pltpu.VMEM((R, HP), BF16),
            pltpu.VMEM((R, HP), BF16),
            pltpu.VMEM((heads, R, LANES), F32),
            pltpu.VMEM((heads, R, LANES), F32),
            pltpu.VMEM((R, HP), F32),
            pltpu.VMEM((R, HP), BF16),
            part,
            pltpu.VMEM((2, R, C), F32),
            pltpu.VMEM((R, C), F32),
            pltpu.VMEM((M, R, C), BF16),
            pltpu.VMEM((tiles, R + 2 * HALO, LANES), F32),
            pltpu.VMEM((32, C), F32),
            pair, pair, pair, pair, part, part, part, part, part, part,
            dma((2 * tiles + 1 + M * heads + M,)),
            dma((T, M, 3)), dma((2, T, 3)), dma((T, 3)), dma((T, 2, 3)), dma((2,)),
            dma((T,)), dma((T,)), dma((2,)), dma((2,)), dma((2,)), dma((2,)),
            dma((NC, 2)), dma((NC, 2)), dma((NC, 2)), dma((NC, 2)), dma((NR, 3)), dma((NR, 3)),
        ],
        compiler_params=pltpu.CompilerParams(
            collective_id=0, has_side_effects=True, vmem_limit_bytes=52 * 2**20
        ),
    )(*[
        pltpu.with_memory_space_constraint(x, pltpu.HBM)
        for x in (tokens, segment_ids, ln_att_gain, w_query, w_keyval, w_out, ln_conv_gain,
                  w_glu, w_depth, bn_scale, bn_shift, w_proj)
    ])


def solution(mesh):
    placed = (
        P(("group", "tm"), "mp"),
        P(("group", "tm")),
        P(),
        P(None, "mp"),
        P(None, None, "mp"),
        P("mp", None),
        P(),
        P(None, None, "mp"),
        P(None, "mp"),
        P("mp"),
        P("mp"),
        P("mp", None),
    )
    fused = mesh.shape["tm"] == 4 and mesh.shape["mp"] == 4
    return jax.shard_map(
        fused_device if fused else per_device, mesh=mesh, in_specs=placed, out_specs=P(("group", "tm"), "mp"), check_vma=False
    )
```

```python
import functools

import jax
import jax.numpy as jnp
from jax import lax
from jax.experimental import pallas as pl
from jax.experimental.pallas import tpu as pltpu
from jax.sharding import PartitionSpec as P

HEAD_DIM = 96


def with_halo(value, sides, width):
    for axis, dim in sides:
        count, length = (lax.axis_size(axis), value.shape[dim])
        up = [(i, (i + 1) % count) for i in range(count - 1)]
        down = [(j, i) for i, j in up]
        last = lax.slice_in_dim(value, length - width, length, axis=dim)
        initial = lax.slice_in_dim(value, 0, width, axis=dim)
        before = lax.ppermute(last, axis, up)
        after = lax.ppermute(initial, axis, down)
        value = jnp.concatenate([before, value, after], axis=dim)
    return value


def layer_norm(values_in, gain_vec):
    row_mean = jnp.mean(values_in, axis=-1, keepdims=True)
    centered = values_in - row_mean
    spread = jnp.mean(centered * centered, axis=-1, keepdims=True)
    return centered * lax.rsqrt(spread + 1e-05) * gain_vec


def fold_keys(carry_state, query_heads, query_segs, keyval, key_segs, local_cols, score_scale):
    row_max, weight_sum, weighted = carry_state
    key_rows = keyval.shape[0]
    heads_here = query_heads.shape[1]
    key_part = keyval[:, :local_cols].reshape(key_rows, heads_here, -1)
    value_part = keyval[:, local_cols:].reshape(key_rows, heads_here, -1)
    scores = (
        jnp.einsum("qhd,khd->qhk", query_heads, key_part, preferred_element_type=jnp.float32)
        * score_scale
    )
    same_seg = (query_segs[:, None] == key_segs[None, :])[:, None, :]
    scores = jnp.where(same_seg, scores, -jnp.inf)
    new_max = jnp.maximum(row_max, jnp.max(scores, axis=2))
    safe_max = jnp.where(new_max == -jnp.inf, 0.0, new_max)
    weights = jnp.exp(scores - safe_max[:, :, None])
    factor = jnp.exp(row_max - safe_max)
    weight_sum = weight_sum * factor + jnp.sum(weights, axis=2)
    weighted = weighted * factor[:, :, None] + jnp.einsum(
        "qhk,khd->qhd", weights.astype(jnp.bfloat16), value_part, preferred_element_type=jnp.float32
    )
    return (new_max, weight_sum, weighted)


def maybe_fold(carry_state, query_heads, query_segs, keyval, key_segs, local_cols, score_scale):
    return fold_keys(
        carry_state, query_heads, query_segs, keyval, key_segs, local_cols, score_scale
    )


def per_device(
    tokens,
    segment_ids,
    ln_att_gain,
    w_query,
    w_keyval,
    w_out,
    ln_conv_gain,
    w_glu,
    w_depth,
    bn_scale,
    bn_shift,
    w_proj,
):
    row_count = tokens.shape[0]
    full_width = ln_att_gain.shape[0]
    local_cols = w_query.shape[1]
    heads_here = local_cols // HEAD_DIM
    score_scale = HEAD_DIM ** (-0.5)
    all_segs = lax.all_gather(segment_ids, "tm", axis=0, tiled=True)
    anchor = lax.axis_index("tm") * row_count
    whole_rows = lax.all_gather(tokens, "mp", axis=1, tiled=True)
    normed = layer_norm(whole_rows.astype(jnp.float32), ln_att_gain).astype(jnp.bfloat16)
    queries = jnp.dot(normed, w_query, preferred_element_type=jnp.float32).astype(jnp.bfloat16)
    keyval = jnp.dot(
        normed, w_keyval.reshape(full_width, -1), preferred_element_type=jnp.float32
    ).astype(jnp.bfloat16)
    query_heads = queries.reshape(row_count, heads_here, HEAD_DIM)
    initial = (
        jnp.full((row_count, heads_here), -jnp.inf, jnp.float32),
        jnp.zeros((row_count, heads_here), jnp.float32),
        jnp.zeros((row_count, heads_here, HEAD_DIM), jnp.float32),
    )
    segment = lax.all_gather(keyval, "tm", axis=0, tiled=True)
    piece_rows = segment.shape[0]
    block_count = piece_rows // row_count

    def inner_step(state_in, element):
        return (
            maybe_fold(
                state_in, query_heads, segment_ids, element[0], element[1], local_cols, score_scale
            ),
            None,
        )

    stacked = (
        segment.reshape(block_count, row_count, -1),
        all_segs.reshape(block_count, row_count),
    )
    result, unused = lax.scan(inner_step, initial, stacked)
    row_max, weight_sum, weighted = result
    context = (
        (weighted / weight_sum[:, :, None]).reshape(row_count, local_cols).astype(jnp.bfloat16)
    )
    att_terms = jnp.dot(context, w_out, preferred_element_type=jnp.float32)
    att_summed = lax.psum_scatter(
        att_terms.astype(jnp.bfloat16), "mp", scatter_dimension=1, tiled=True
    ).astype(jnp.float32)
    middle = (tokens.astype(jnp.float32) + att_summed).astype(jnp.bfloat16)
    whole_mid = lax.all_gather(middle, "mp", axis=1, tiled=True)
    normed_conv = layer_norm(whole_mid.astype(jnp.float32), ln_conv_gain).astype(jnp.bfloat16)
    both_halves = jnp.dot(
        normed_conv, w_glu.reshape(full_width, -1), preferred_element_type=jnp.float32
    )
    gated = (both_halves[:, :local_cols] * jax.nn.sigmoid(both_halves[:, local_cols:])).astype(
        jnp.bfloat16
    )
    half_width = (w_depth.shape[0] - 1) // 2
    extended = with_halo(gated, (("tm", 0),), half_width).astype(jnp.float32)
    padded_segs = jnp.pad(all_segs, (half_width, half_width), constant_values=-1)
    window_segs = lax.dynamic_slice_in_dim(padded_segs, anchor, row_count + 2 * half_width, 0)
    depth = jnp.zeros((row_count, local_cols), jnp.float32)
    for tap_index in range(w_depth.shape[0]):
        same_seg = (window_segs[tap_index : tap_index + row_count] == segment_ids)[:, None]
        shifted = jnp.where(same_seg, extended[tap_index : tap_index + row_count], 0.0)
        depth = depth + shifted * w_depth[tap_index].astype(jnp.float32)
    normalized = depth * bn_scale + bn_shift
    swished = (normalized * jax.nn.sigmoid(normalized)).astype(jnp.bfloat16)
    conv_terms = jnp.dot(swished, w_proj, preferred_element_type=jnp.float32)
    conv_summed = lax.psum_scatter(
        conv_terms.astype(jnp.bfloat16), "mp", scatter_dimension=1, tiled=True
    ).astype(jnp.float32)
    return (middle.astype(jnp.float32) + conv_summed).astype(jnp.bfloat16)


NEG = -1e30
HALO = 16
LANES = 128
PIECES = ((0, 128), (128, 128), (256, 128))
RS = 128
CHUNKS = ((320, 64), (192, 128), (0, 128), (128, 64))
REGIONS = (((208, 160),), ((16, 96),), ((0, 16), (368, 16)), ((112, 96),))
MESH = pl.DeviceIdType.MESH
F32 = jnp.float32
BF16 = jnp.bfloat16


def block_kernel(
    T, taps,
    tokens_h, seg_h, g_att_h, wq_h, wkv_h, wo_h, g_conv_h, wg_h, wdep_h, bn_s_h, bn_b_h, wp_h,
    out, seg, g_att, g_conv, wdep, bn_s, bn_b, small, segcol, gains, bns, bnb,
    tok, seg_all, seg_ext, rawq, raw, wide32, sc, pw, wq, wkv, wo, wg, wp, nrm, qp, kp, vp, mst, lst, acc,
    ctx, swi, keep, keep2, mid, ext, wdf, sa, ra, sx, rx, sa2, ra2, sx2, rx2, sb2, rb2,
    wsem, tok_recv, z_send, x_send, m_send, r_send, seg_send, seg_recv, hs_send, hs_recv,
    hg_send, hg_recv, ar_send, ar_recv, mid_send, mid_recv, rs_send, rs_recv,
):
    R, C = tokens_h.shape
    M = 4
    D = M * C
    heads = C // HEAD_DIM
    HP = heads * LANES
    tiles = C // LANES
    t = lax.axis_index("tm")
    m = lax.axis_index("mp")
    mate = m + 1 - 2 * (m % 2)
    cross = (m + 2) % 4
    diag = (mate + 2) % 4

    def rcopy(src, dst, ssem, rsem, **dev):
        return pltpu.make_async_remote_copy(
            src_ref=src, dst_ref=dst, send_sem=ssem, recv_sem=rsem,
            device_id=dev, device_id_type=MESH,
        )

    firsts = [
        pltpu.make_async_copy(src, dst, small.at[i])
        for i, (src, dst) in enumerate([
            (tokens_h, tok.at[t, m]), (seg_h, seg), (g_att_h, g_att), (g_conv_h, g_conv),
            (wdep_h, wdep), (bn_s_h, bn_s), (bn_b_h, bn_b)])
    ]
    loads, at = {}, 0

    def load(name, src, dst):
        nonlocal at
        loads[name] = pltpu.make_async_copy(src, dst, wsem.at[at])
        at += 1

    for k in range(tiles):
        load(("kv", k), wkv_h.at[:, :, pl.ds(k * LANES, LANES)], raw.at[0, k])
    load("q", wq_h, rawq)
    for k in range(tiles):
        load(("g", k), wg_h.at[:, :, pl.ds(k * LANES, LANES)], raw.at[1, k])
    for b in range(M):
        cols = pl.ds(b * C, C)
        for h in range(heads):
            load(("o", b, h), wo_h.at[pl.ds(h * HEAD_DIM, HEAD_DIM), cols],
                 wo.at[b, pl.ds(h * LANES, HEAD_DIM)])
    for b in range(M):
        load(("p", b), wp_h.at[:, pl.ds(b * C, C)], wp.at[b])
    for c in firsts:
        c.start()

    barrier = pltpu.get_barrier_semaphore()
    for peer in (mate, cross):
        pl.semaphore_signal(barrier, inc=1, device_id={"mp": peer}, device_id_type=MESH)
    for d in range(1, T):
        pl.semaphore_signal(
            barrier, inc=1, device_id={"tm": (t + d) % T}, device_id_type=MESH
        )
    for c in loads.values():
        c.start()
    for c in firsts:
        c.wait()
    ids = seg[...].reshape(1, R)
    seg_all[t] = jnp.broadcast_to(ids, (8, R))
    pl.semaphore_wait(barrier, 1 + T)

    def z_right(s, p):
        piece = tok.at[s, m, pl.ds(*PIECES[p])]
        return rcopy(piece, piece, z_send.at[0, s, p], tok_recv.at[s, m, p], tm=(t + 1) % T)

    def z_left(s, p):
        piece = tok.at[s, m, pl.ds(*PIECES[p])]
        return rcopy(piece, piece, z_send.at[1, s, p], tok_recv.at[s, m, p], tm=(t + T - 1) % T)

    def over_x(s, col, p):
        piece = tok.at[s, col, pl.ds(*PIECES[p])]
        return rcopy(piece, piece, x_send.at[s, p], tok_recv.at[s, col, p], mp=cross)

    def to_mate(s, col, k, p):
        piece = tok.at[s, col, pl.ds(*PIECES[p])]
        return rcopy(piece, piece, m_send.at[s, k, p], tok_recv.at[s, col, p], mp=mate)

    def launch(s, p):
        @pl.when(jnp.logical_and(s <= t, t < T - 1))
        def _():
            z_right(s, p).start()

        @pl.when(jnp.logical_and(s >= t, t > 0))
        def _():
            z_left(s, p).start()

    def straight(s, p):
        inner = jnp.logical_and(s > 0, s < T - 1)
        return jnp.logical_or(p < 2, jnp.logical_or(s == t, inner))

    def round_right(s):
        piece = tok.at[s, cross, pl.ds(*PIECES[2])]
        return rcopy(piece, piece, r_send.at[0], tok_recv.at[s, cross, 2], tm=(t + 1) % T)

    def round_left(s):
        piece = tok.at[s, cross, pl.ds(*PIECES[2])]
        return rcopy(piece, piece, r_send.at[1], tok_recv.at[s, cross, 2], tm=(t + T - 1) % T)

    def send_round(s):
        @pl.when(jnp.logical_and(s == 0, t < T - 1))
        def _():
            round_right(s).start()

        @pl.when(jnp.logical_and(s == T - 1, t > 0))
        def _():
            round_left(s).start()

    for p in range(3):
        over_x(t, m, p).start()
        launch(t, p)
        to_mate(t, m, 0, p).start()

    def seg_copy(d):
        return rcopy(seg_all.at[t], seg_all.at[t], seg_send.at[d], seg_recv.at[t],
                     tm=(t + d) % T)

    for d in range(1, T):
        seg_copy(d).start()

    def halo_right(ref, ssem, rsem):
        return rcopy(ref.at[:, pl.ds(R, HALO)], ref.at[:, pl.ds(0, HALO)], ssem.at[0],
                     rsem.at[0], tm=(t + 1) % T)

    def halo_left(ref, ssem, rsem):
        return rcopy(ref.at[:, pl.ds(HALO, HALO)], ref.at[:, pl.ds(R + HALO, HALO)],
                     ssem.at[1], rsem.at[1], tm=(t + T - 1) % T)

    has_right = t < T - 1
    has_left = t > 0
    edge = jnp.logical_or(t == 0, t == T - 1)

    segcol[...] = jnp.transpose(jnp.broadcast_to(ids, (LANES, R)))
    seg_ext[0, pl.ds(HALO, R), :] = segcol[...]

    @pl.when(has_right)
    def _():
        halo_right(seg_ext, hs_send, hs_recv).start()

    @pl.when(has_left)
    def _():
        halo_left(seg_ext, hs_send, hs_recv).start()

    @pl.when(jnp.logical_not(has_left))
    def _():
        seg_ext[0, pl.ds(0, HALO), :] = jnp.full((HALO, LANES), -1, jnp.int32)
        ext[:, pl.ds(0, HALO), :] = jnp.zeros((tiles, HALO, LANES), F32)

    @pl.when(jnp.logical_not(has_right))
    def _():
        seg_ext[0, pl.ds(R + HALO, HALO), :] = jnp.full((HALO, LANES), -1, jnp.int32)
        ext[:, pl.ds(R + HALO, HALO), :] = jnp.zeros((tiles, HALO, LANES), F32)

    gains[0] = g_att[...].reshape(1, D)
    gains[1] = g_conv[...].reshape(1, D)
    bns[...] = bn_s[...].reshape(1, C)
    bnb[...] = bn_b[...].reshape(1, C)

    def by_head(x):
        gap = jnp.zeros((x.shape[0], LANES - HEAD_DIM), F32)
        cols = []
        for h in range(heads):
            cols += [x[:, h * HEAD_DIM:(h + 1) * HEAD_DIM], gap]
        return jnp.concatenate(cols, axis=1).astype(BF16)

    for k in range(tiles):
        loads["kv", k].wait()

    def widen(b, i, n):
        for k in range(tiles):
            wide32[k, pl.ds(0, 2 * n), :] = raw.at[b, k].reshape(2 * D, LANES)[
                pl.ds(pl.multiple_of(i * 2 * n, 2 * n), 2 * n), :].astype(F32)

    @pl.loop(0, D // 256)
    def _(i):
        rows = pl.ds(pl.multiple_of(i * 256, 256), 256)
        widen(0, i, 256)
        for j in range(2):
            x = jnp.concatenate([wide32[k, pl.ds(j, 256, 2), :] for k in range(tiles)], axis=1)
            wkv[rows, pl.ds(j * HP, HP)] = by_head(x)

    loads["q"].wait()

    @pl.loop(0, D // 256)
    def _(i):
        rows = pl.ds(pl.multiple_of(i * 256, 256), 256)
        wq[rows, :] = by_head(rawq[rows, :].astype(F32))

    def split_gates():
        for k in range(tiles):
            loads["g", k].wait()

        @pl.loop(0, D // 128)
        def _(i):
            rows = pl.ds(pl.multiple_of(i * 128, 128), 128)
            widen(1, i, 128)
            for j in range(2):
                for k in range(tiles):
                    wg[rows, pl.ds(j * C + k * LANES, LANES)] = (
                        wide32[k, pl.ds(j, 128, 2), :].astype(BF16))

    wdf[pl.ds(0, taps), :] = wdep[...].astype(F32)
    mst[...] = jnp.full(mst.shape, NEG, F32)
    lst[...] = jnp.zeros(lst.shape, F32)
    acc[...] = jnp.zeros(acc.shape, F32)
    for b in range(M):
        for h in range(heads):
            wo[b, pl.ds(h * LANES + HEAD_DIM, LANES - HEAD_DIM), :] = jnp.zeros(
                (LANES - HEAD_DIM, C), BF16)

    def norm_rows(load_part, gain, r0, n):
        parts = [load_part(b, r0, n).astype(F32) for b in range(M)]
        total = parts[0] + parts[1] + parts[2] + parts[3]
        mean = jnp.sum(total, axis=1, keepdims=True) * (1.0 / D)
        parts = [p - mean for p in parts]
        sq = parts[0] * parts[0]
        for p in parts[1:]:
            sq = sq + p * p
        inv = lax.rsqrt(jnp.sum(sq, axis=1, keepdims=True) * (1.0 / D) + 1e-05)
        for b in range(M):
            nrm[pl.ds(r0, n), pl.ds(b * C, C)] = (
                parts[b] * inv * gains[gain, :, pl.ds(b * C, C)]
            ).astype(BF16)

    coef = float(HEAD_DIM ** (-0.5) * 1.4426950408889634)

    hs = range(heads)

    def lanes(h):
        return pl.ds(h * LANES, LANES)

    def weigh(key_ids, r0, n, score, keep_weights):
        rows, nk = pl.ds(r0, n), key_ids.shape[1]

        def fold(x):
            return sum(x[:, k * LANES:(k + 1) * LANES] for k in range(1, nk // LANES)) + x[:, :LANES]

        def wide(col):
            return jnp.concatenate([col] * (nk // LANES), axis=1)

        bias = jnp.where(wide(segcol[rows, :]) == key_ids, 0.0, NEG)
        xs = [score(h) + bias for h in hs]
        olds = [mst[h, rows, :] for h in hs]
        sums = [lst[h, rows, :] for h in hs]
        accs = [acc[rows, lanes(h)] for h in hs]
        news = [jnp.maximum(o, jnp.max(x, axis=1, keepdims=True)) for o, x in zip(olds, xs)]
        fs = [jnp.exp2((o - v) * coef) for o, v in zip(olds, news)]
        ps = [jnp.exp2((x - wide(v)) * coef) for x, v in zip(xs, news)]
        sums = [v * f + fold(w) for v, f, w in zip(sums, fs, ps)]
        for h in hs:
            mst[h, rows, :] = news[h]
            lst[h, rows, :] = sums[h]
        keep_weights([w.astype(BF16) for w in ps], [a * f for a, f in zip(accs, fs)])

    def score_block(r0, n, c0, nk, h):
        return lax.dot_general(
            qp[pl.ds(r0, n), lanes(h)], kp[pl.ds(c0, nk), lanes(h)], (((1,), (1,)), ((), ())),
            preferred_element_type=F32)

    def ids_of(s):
        return seg_all[s, pl.ds(0, 1), :]

    def attend(s):
        for h in hs:
            sc[h] = score_block(0, R, 0, R, h)

        @pl.loop(0, R // RS)
        def _(rt):
            r0 = pl.multiple_of(rt * RS, RS)
            rows = pl.ds(r0, RS)

            def kept(ws, scaled):
                for h in hs:
                    pw[h, rows, :] = ws[h]
                    acc[rows, lanes(h)] = scaled[h]

            weigh(ids_of(s), r0, RS, lambda h: sc[h, rows, :], kept)

        for h in hs:
            acc[:, lanes(h)] += jnp.dot(
                pw[h], vp[pl.ds(0, R), lanes(h)], preferred_element_type=F32)

    def attend_last(r0, n):
        rows = pl.ds(r0, n)

        def kept(ws, scaled):
            for h in hs:
                total = scaled[h] + jnp.dot(
                    ws[h], vp[:, lanes(h)], preferred_element_type=F32)
                den = jnp.sum(lst[h, rows, :], axis=1, keepdims=True)
                ctx[rows, lanes(h)] = (total / den).astype(BF16)

        key_ids = jnp.concatenate([ids_of(late), ids_of(final)], axis=1)
        weigh(key_ids, r0, n, lambda h: score_block(r0, n, 0, 2 * R, h), kept)

    def project(s, r0, n, base, with_queries, midway):
        rows, spot = pl.ds(r0, n), pl.ds(base + r0, n)

        @pl.loop(0, n // 128)
        def _(rt):
            norm_rows(lambda b, at, k: tok[s, b, pl.ds(at, k), :], 0,
                      pl.multiple_of(r0 + rt * 128, 128), 128)

        if with_queries is not None:
            @pl.when(with_queries)
            def _():
                qp[rows, :] = jnp.dot(
                    nrm[rows, :], wq[...], preferred_element_type=F32).astype(BF16)

        kp[spot, :] = jnp.dot(
            nrm[rows, :], wkv[:, pl.ds(0, HP)], preferred_element_type=F32).astype(BF16)
        midway()
        vp[spot, :] = jnp.dot(
            nrm[rows, :], wkv[:, pl.ds(HP, HP)], preferred_element_type=F32).astype(BF16)

    def digit(code, i):
        return (code // (T ** i)) % T

    order = 228 - 3 * ((t + 3) // 4) - 195 * ((t + 2) // 4) - 3 * ((t + 1) // 4)

    def take(s, p):
        over_x(s, cross, p).wait_recv()
        to_mate(s, cross, 1, p).start()

    def arrive(s, p):
        to_mate(s, mate, 0, p).wait_recv()
        to_mate(s, diag, 1, p).wait_recv()

    def ids_arrive(s):
        rcopy(seg_all.at[s], seg_all.at[s], seg_send.at[0], seg_recv.at[s],
              tm=(t + 1) % T).wait_recv()

    def block_step(i, carry):
        code, before = carry
        s, nxt, after = digit(code, 0), digit(code, 1), digit(code, 2)

        def relay(ps):
            for p in ps:
                @pl.when(jnp.logical_or(i == 0, edge))
                def _():
                    z_right(nxt, p).wait_recv()
                    launch(nxt, p)

                @pl.when(straight(nxt, p))
                def _():
                    over_x(nxt, m, p).start()

                to_mate(nxt, m, 0, p).start()

                @pl.when(jnp.logical_and(jnp.logical_not(edge), i < 2))
                def _():
                    z_right(after, p).wait_recv()
                    launch(after, p)

            for p in ps:
                take(s, p)
                if p == 2:
                    send_round(s)

        @pl.when(jnp.logical_and(jnp.logical_not(edge), i == T - 2))
        def _():
            take(nxt, 2)
            send_round(nxt)

        relay((0, 1))

        @pl.when(i > 0)
        def _():
            attend(before)
            ids_arrive(s)

        def early():
            @pl.when(i == T - 2)
            def _():
                take(nxt, 0)

            @pl.when(jnp.logical_and(edge, i == T - 2))
            def _():
                take(nxt, 2)

        arrive(s, 0)
        arrive(s, 1)
        project(s, 0, 256, 0, i == 0, lambda: relay((2,)))
        arrive(s, 2)
        project(s, 256, 128, 0, i == 0, early)
        return code // T, s

    late, final = digit(order, T - 2), digit(order, T - 1)
    lax.fori_loop(0, T - 1, block_step, (order, t))
    ids_arrive(final)
    arrive(final, 2)
    project(final, 256, 128, R, None, lambda: take(final, 1))
    arrive(final, 0)
    project(final, 0, 128, R, None, lambda: None)
    arrive(final, 1)
    project(final, 128, 128, R, None, lambda: None)

    def ar_mate(i):
        rows = pl.ds(*CHUNKS[i])
        return rcopy(sa.at[:, rows], ra.at[:, rows], ar_send.at[i, 0], ar_recv.at[i, 0], mp=mate)

    def ar_x(i):
        rows = pl.ds(*CHUNKS[i])
        return rcopy(sx.at[:, rows], rx.at[:, rows], ar_send.at[i, 1], ar_recv.at[i, 1], mp=cross)

    def mid_copy(i, j, col):
        piece = mid.at[col, pl.ds(*CHUNKS[i])]
        return rcopy(piece, piece, mid_send.at[i, j], mid_recv.at[i, j], mp=mate)

    def rounded(a, w):
        return jnp.dot(a, w, preferred_element_type=F32).astype(BF16)

    def project_out(i):
        rows = pl.ds(*CHUNKS[i])
        a = ctx[rows, :]
        sa[0, rows, :] = rounded(a, wo[mate])
        sa[1, rows, :] = rounded(a, wo[diag])
        ar_mate(i).start()
        keep[0, rows, :] = rounded(a, wo[m]).astype(F32)
        keep[1, rows, :] = rounded(a, wo[cross]).astype(F32)

    def chip_sum(i):
        rows = pl.ds(*CHUNKS[i])
        ar_mate(i).wait_recv()
        for j in range(2):
            both = keep[j, rows, :] + ra[j, rows, :].astype(F32)
            keep[j, rows, :] = both
            sx[1 - j, rows, :] = both.astype(BF16)
        ar_x(i).start()

    def middle(i):
        rows = pl.ds(*CHUNKS[i])
        ar_x(i).wait_recv()
        for j, col in enumerate((m, cross)):
            mid[col, rows, :] = (
                tok[t, col, rows, :].astype(F32) + (keep[j, rows, :] + rx[j, rows, :].astype(F32))
            ).astype(BF16)
            mid_copy(i, j, col).start()

    def gate(i):
        r0, n = CHUNKS[i]
        rows = pl.ds(r0, n)
        for j, col in enumerate((mate, diag)):
            mid_copy(i, j, col).wait_recv()

        @pl.loop(0, n // 32)
        def _(rt):
            norm_rows(lambda b, at, k: mid[b, pl.ds(at, k), :], 1,
                      pl.multiple_of(r0 + rt * 32, 32), 32)

        both = jnp.dot(nrm[rows, :], wg[...], preferred_element_type=F32)
        gated = (both[:, :C] * jax.nn.sigmoid(both[:, C:])).astype(BF16).astype(F32)
        for k in range(tiles):
            ext[k, pl.ds(HALO + r0, n), :] = gated[:, k * LANES:(k + 1) * LANES]

    half = (taps - 1) // 2
    RT = 64
    places, place = [], 0
    for region in REGIONS:
        first = place
        spots = []
        for r0, n in region:
            spots.append((r0, n, place))
            place += n
        places.append((first, place - first, spots))

    def rs_a(i):
        rows = pl.ds(*places[i][:2])
        return rcopy(sa2.at[rows], ra2.at[rows], rs_send.at[i, 0], rs_recv.at[i, 0], mp=mate)

    def rs_x(i):
        rows = pl.ds(*places[i][:2])
        return rcopy(sx2.at[rows], rx2.at[rows], rs_send.at[i, 1], rs_recv.at[i, 1], mp=cross)

    def rs_b(i):
        rows = pl.ds(*places[i][:2])
        return rcopy(sb2.at[rows], rb2.at[rows], rs_send.at[i, 2], rs_recv.at[i, 2], mp=mate)

    def convolve_rows(r0, n, to):
        here = segcol[pl.ds(r0, n), :]
        groups = [pl.ds(k * LANES, LANES) for k in range(tiles)]
        depth = [jnp.zeros((n, LANES), F32) for _ in groups]
        for j in range(taps):
            at = pl.ds(r0 + (j + HALO - half), n)
            same = seg_ext[0, at, :] == here
            for k, g in enumerate(groups):
                depth[k] += jnp.where(same, ext[k, at, :], 0.0) * wdf[pl.ds(j, 1), g]
        for k, g in enumerate(groups):
            z = depth[k] * bns[:, g] + bnb[:, g]
            swi[pl.ds(to, n), g] = (z * jax.nn.sigmoid(z)).astype(BF16)

    def convolve(i):
        for r0, n, to in places[i][2]:
            if n >= RT:
                @pl.loop(0, n // RT)
                def _(rt):
                    convolve_rows(pl.multiple_of(r0 + rt * RT, 16), RT,
                                  pl.multiple_of(to + rt * RT, 16))
            if n % RT:
                done = n - n % RT
                convolve_rows(r0 + done, n % RT, to + done)

        rows = pl.ds(*places[i][:2])
        a = swi[rows, :]
        sa2[rows, :] = rounded(a, wp[diag])
        rs_a(i).start()
        keep2[rows, :] = jnp.dot(a, wp[cross], preferred_element_type=F32)
        sb2[rows, :] = rounded(a, wp[mate])
        rs_b(i).start()

    def pass_on(i):
        rows = pl.ds(*places[i][:2])
        rs_a(i).wait_recv()
        sx2[rows, :] = (keep2[rows, :] + ra2[rows, :].astype(F32)).astype(BF16)
        rs_x(i).start()
        keep2[rows, :] = rounded(swi[rows, :], wp[m]).astype(F32)

    for b in range(M):
        for h in range(heads):
            loads["o", b, h].wait()
    attend_last(*CHUNKS[0])
    project_out(0)
    attend_last(*CHUNKS[1])
    chip_sum(0)
    project_out(1)
    attend_last(*CHUNKS[2])
    chip_sum(1)
    project_out(2)
    attend_last(*CHUNKS[3])
    chip_sum(2)
    project_out(3)
    split_gates()
    chip_sum(3)
    for b in range(M):
        loads["p", b].wait()
    middle(0)
    gate(0)

    @pl.when(has_right)
    def _():
        halo_right(ext, hg_send, hg_recv).start()

    middle(1)
    gate(1)
    convolve(0)
    middle(2)
    pass_on(0)
    gate(2)

    @pl.when(has_left)
    def _():
        halo_left(ext, hg_send, hg_recv).start()

    middle(3)
    convolve(1)
    gate(3)
    convolve(3)
    pass_on(1)

    @pl.when(has_left)
    def _():
        halo_right(seg_ext, hs_send, hs_recv).wait_recv()
        halo_right(ext, hg_send, hg_recv).wait_recv()

    @pl.when(has_right)
    def _():
        halo_left(seg_ext, hs_send, hs_recv).wait_recv()
        halo_left(ext, hg_send, hg_recv).wait_recv()

    convolve(2)
    pass_on(3)
    pass_on(2)
    for i in (0, 1, 3, 2):
        rs_b(i).wait_recv()
        rs_x(i).wait_recv()
        for r0, n, to in places[i][2]:
            rows, spot = pl.ds(r0, n), pl.ds(to, n)
            summed = (keep2[spot, :] + rb2[spot, :].astype(F32)) + rx2[spot, :].astype(F32)
            out[rows, :] = (mid[m, rows, :].astype(F32) + summed).astype(BF16)

    @pl.when(has_right)
    def _():
        round_right(0).wait_send()

    @pl.when(has_left)
    def _():
        round_left(T - 1).wait_send()

    for p in range(3):
        for s in range(T):
            @pl.when(jnp.logical_and(s <= t, t < T - 1))
            def _():
                z_right(s, p).wait_send()

            @pl.when(jnp.logical_and(s >= t, t > 0))
            def _():
                z_left(s, p).wait_send()

            @pl.when(straight(s, p))
            def _():
                over_x(s, m, p).wait_send()

            to_mate(s, m, 0, p).wait_send()
            to_mate(s, cross, 1, p).wait_send()
    for d in range(1, T):
        seg_copy(d).wait_send()

    @pl.when(has_right)
    def _():
        halo_right(seg_ext, hs_send, hs_recv).wait_send()
        halo_right(ext, hg_send, hg_recv).wait_send()

    @pl.when(has_left)
    def _():
        halo_left(seg_ext, hs_send, hs_recv).wait_send()
        halo_left(ext, hg_send, hg_recv).wait_send()

    for i in range(len(CHUNKS)):
        ar_mate(i).wait_send()
        ar_x(i).wait_send()
        mid_copy(i, 0, m).wait_send()
        mid_copy(i, 1, cross).wait_send()
    for i in range(len(REGIONS)):
        rs_a(i).wait_send()
        rs_x(i).wait_send()
        rs_b(i).wait_send()


def fused_device(
    tokens, segment_ids, ln_att_gain, w_query, w_keyval, w_out, ln_conv_gain, w_glu,
    w_depth, bn_scale, bn_shift, w_proj,
):
    R, C = tokens.shape
    D = ln_att_gain.shape[0]
    T = lax.axis_size("tm")
    M = D // C
    heads = C // HEAD_DIM
    HP = heads * LANES
    tiles = C // LANES
    taps = w_depth.shape[0]
    vmem = pl.BlockSpec(memory_space=pltpu.VMEM)
    hbm = pl.BlockSpec(memory_space=pltpu.HBM)
    dma = pltpu.SemaphoreType.DMA
    NC, NR = len(CHUNKS), len(REGIONS)
    part, pair = pltpu.VMEM((R, C), BF16), pltpu.VMEM((2, R, C), BF16)
    return pl.pallas_call(
        functools.partial(block_kernel, T, taps),
        out_shape=jax.ShapeDtypeStruct((R, C), BF16),
        in_specs=[hbm] * 12,
        out_specs=vmem,
        scratch_shapes=[
            pltpu.VMEM((R,), jnp.int32), pltpu.VMEM((D,), F32), pltpu.VMEM((D,), F32),
            pltpu.VMEM((taps, C), BF16), pltpu.VMEM((C,), F32), pltpu.VMEM((C,), F32), dma((7,)),
            pltpu.VMEM((R, LANES), jnp.int32),
            pltpu.VMEM((2, 1, D), F32),
            pltpu.VMEM((1, C), F32),
            pltpu.VMEM((1, C), F32),
            pltpu.VMEM((T, M, R, C), BF16),
            pltpu.VMEM((T, 8, R), jnp.int32),
            pltpu.VMEM((1, R + 2 * HALO, LANES), jnp.int32),
            pltpu.VMEM((D, C), BF16),
            pltpu.VMEM((2, tiles, D, 2, LANES), BF16),
            pltpu.VMEM((tiles, 512, LANES), F32),
            pltpu.VMEM((heads, R, R), F32),
            pltpu.VMEM((heads, R, R), BF16),
            pltpu.VMEM((D, HP), BF16),
            pltpu.VMEM((D, 2 * HP), BF16),
            pltpu.VMEM((M, HP, C), BF16),
            pltpu.VMEM((D, 2 * C), BF16),
            pltpu.VMEM((M, C, C), BF16),
            pltpu.VMEM((R, D), BF16),
            pltpu.VMEM((R, HP), BF16),
            pltpu.VMEM((2 * R, HP), BF16),
            pltpu.VMEM((2 * R, HP), BF16),
            pltpu.VMEM((heads, R, LANES), F32),
            pltpu.VMEM((heads, R, LANES), F32),
            pltpu.VMEM((R, HP), F32),
            pltpu.VMEM((R, HP), BF16),
            part,
            pltpu.VMEM((2, R, C), F32),
            pltpu.VMEM((R, C), F32),
            pltpu.VMEM((M, R, C), BF16),
            pltpu.VMEM((tiles, R + 2 * HALO, LANES), F32),
            pltpu.VMEM((32, C), F32),
            pair, pair, pair, pair, part, part, part, part, part, part,
            dma((2 * tiles + 1 + M * heads + M,)),
            dma((T, M, 3)), dma((2, T, 3)), dma((T, 3)), dma((T, 2, 3)), dma((2,)),
            dma((T,)), dma((T,)), dma((2,)), dma((2,)), dma((2,)), dma((2,)),
            dma((NC, 2)), dma((NC, 2)), dma((NC, 2)), dma((NC, 2)), dma((NR, 3)), dma((NR, 3)),
        ],
        compiler_params=pltpu.CompilerParams(
            collective_id=0, has_side_effects=True, vmem_limit_bytes=52 * 2**20
        ),
    )(*[
        pltpu.with_memory_space_constraint(x, pltpu.HBM)
        for x in (tokens, segment_ids, ln_att_gain, w_query, w_keyval, w_out, ln_conv_gain,
                  w_glu, w_depth, bn_scale, bn_shift, w_proj)
    ])


def solution(mesh):
    placed = (
        P(("group", "tm"), "mp"),
        P(("group", "tm")),
        P(),
        P(None, "mp"),
        P(None, None, "mp"),
        P("mp", None),
        P(),
        P(None, None, "mp"),
        P(None, "mp"),
        P("mp"),
        P("mp"),
        P("mp", None),
    )
    fused = mesh.shape["tm"] == 4 and mesh.shape["mp"] == 4
    return jax.shard_map(
        fused_device if fused else per_device, mesh=mesh, in_specs=placed, out_specs=P(("group", "tm"), "mp"), check_vma=False
    )
```

```python
import functools

import jax
import jax.numpy as jnp
from jax import lax
from jax.experimental import pallas as pl
from jax.experimental.pallas import tpu as pltpu
from jax.sharding import PartitionSpec as P

HEAD_DIM = 96


def with_halo(value, sides, width):
    for axis, dim in sides:
        count, length = (lax.axis_size(axis), value.shape[dim])
        up = [(i, (i + 1) % count) for i in range(count - 1)]
        down = [(j, i) for i, j in up]
        last = lax.slice_in_dim(value, length - width, length, axis=dim)
        initial = lax.slice_in_dim(value, 0, width, axis=dim)
        before = lax.ppermute(last, axis, up)
        after = lax.ppermute(initial, axis, down)
        value = jnp.concatenate([before, value, after], axis=dim)
    return value


def layer_norm(values_in, gain_vec):
    row_mean = jnp.mean(values_in, axis=-1, keepdims=True)
    centered = values_in - row_mean
    spread = jnp.mean(centered * centered, axis=-1, keepdims=True)
    return centered * lax.rsqrt(spread + 1e-05) * gain_vec


def fold_keys(carry_state, query_heads, query_segs, keyval, key_segs, local_cols, score_scale):
    row_max, weight_sum, weighted = carry_state
    key_rows = keyval.shape[0]
    heads_here = query_heads.shape[1]
    key_part = keyval[:, :local_cols].reshape(key_rows, heads_here, -1)
    value_part = keyval[:, local_cols:].reshape(key_rows, heads_here, -1)
    scores = (
        jnp.einsum("qhd,khd->qhk", query_heads, key_part, preferred_element_type=jnp.float32)
        * score_scale
    )
    same_seg = (query_segs[:, None] == key_segs[None, :])[:, None, :]
    scores = jnp.where(same_seg, scores, -jnp.inf)
    new_max = jnp.maximum(row_max, jnp.max(scores, axis=2))
    safe_max = jnp.where(new_max == -jnp.inf, 0.0, new_max)
    weights = jnp.exp(scores - safe_max[:, :, None])
    factor = jnp.exp(row_max - safe_max)
    weight_sum = weight_sum * factor + jnp.sum(weights, axis=2)
    weighted = weighted * factor[:, :, None] + jnp.einsum(
        "qhk,khd->qhd", weights.astype(jnp.bfloat16), value_part, preferred_element_type=jnp.float32
    )
    return (new_max, weight_sum, weighted)


def maybe_fold(carry_state, query_heads, query_segs, keyval, key_segs, local_cols, score_scale):
    return fold_keys(
        carry_state, query_heads, query_segs, keyval, key_segs, local_cols, score_scale
    )


def per_device(
    tokens,
    segment_ids,
    ln_att_gain,
    w_query,
    w_keyval,
    w_out,
    ln_conv_gain,
    w_glu,
    w_depth,
    bn_scale,
    bn_shift,
    w_proj,
):
    row_count = tokens.shape[0]
    full_width = ln_att_gain.shape[0]
    local_cols = w_query.shape[1]
    heads_here = local_cols // HEAD_DIM
    score_scale = HEAD_DIM ** (-0.5)
    all_segs = lax.all_gather(segment_ids, "tm", axis=0, tiled=True)
    anchor = lax.axis_index("tm") * row_count
    whole_rows = lax.all_gather(tokens, "mp", axis=1, tiled=True)
    normed = layer_norm(whole_rows.astype(jnp.float32), ln_att_gain).astype(jnp.bfloat16)
    queries = jnp.dot(normed, w_query, preferred_element_type=jnp.float32).astype(jnp.bfloat16)
    keyval = jnp.dot(
        normed, w_keyval.reshape(full_width, -1), preferred_element_type=jnp.float32
    ).astype(jnp.bfloat16)
    query_heads = queries.reshape(row_count, heads_here, HEAD_DIM)
    initial = (
        jnp.full((row_count, heads_here), -jnp.inf, jnp.float32),
        jnp.zeros((row_count, heads_here), jnp.float32),
        jnp.zeros((row_count, heads_here, HEAD_DIM), jnp.float32),
    )
    segment = lax.all_gather(keyval, "tm", axis=0, tiled=True)
    piece_rows = segment.shape[0]
    block_count = piece_rows // row_count

    def inner_step(state_in, element):
        return (
            maybe_fold(
                state_in, query_heads, segment_ids, element[0], element[1], local_cols, score_scale
            ),
            None,
        )

    stacked = (
        segment.reshape(block_count, row_count, -1),
        all_segs.reshape(block_count, row_count),
    )
    result, unused = lax.scan(inner_step, initial, stacked)
    row_max, weight_sum, weighted = result
    context = (
        (weighted / weight_sum[:, :, None]).reshape(row_count, local_cols).astype(jnp.bfloat16)
    )
    att_terms = jnp.dot(context, w_out, preferred_element_type=jnp.float32)
    att_summed = lax.psum_scatter(
        att_terms.astype(jnp.bfloat16), "mp", scatter_dimension=1, tiled=True
    ).astype(jnp.float32)
    middle = (tokens.astype(jnp.float32) + att_summed).astype(jnp.bfloat16)
    whole_mid = lax.all_gather(middle, "mp", axis=1, tiled=True)
    normed_conv = layer_norm(whole_mid.astype(jnp.float32), ln_conv_gain).astype(jnp.bfloat16)
    both_halves = jnp.dot(
        normed_conv, w_glu.reshape(full_width, -1), preferred_element_type=jnp.float32
    )
    gated = (both_halves[:, :local_cols] * jax.nn.sigmoid(both_halves[:, local_cols:])).astype(
        jnp.bfloat16
    )
    half_width = (w_depth.shape[0] - 1) // 2
    extended = with_halo(gated, (("tm", 0),), half_width).astype(jnp.float32)
    padded_segs = jnp.pad(all_segs, (half_width, half_width), constant_values=-1)
    window_segs = lax.dynamic_slice_in_dim(padded_segs, anchor, row_count + 2 * half_width, 0)
    depth = jnp.zeros((row_count, local_cols), jnp.float32)
    for tap_index in range(w_depth.shape[0]):
        same_seg = (window_segs[tap_index : tap_index + row_count] == segment_ids)[:, None]
        shifted = jnp.where(same_seg, extended[tap_index : tap_index + row_count], 0.0)
        depth = depth + shifted * w_depth[tap_index].astype(jnp.float32)
    normalized = depth * bn_scale + bn_shift
    swished = (normalized * jax.nn.sigmoid(normalized)).astype(jnp.bfloat16)
    conv_terms = jnp.dot(swished, w_proj, preferred_element_type=jnp.float32)
    conv_summed = lax.psum_scatter(
        conv_terms.astype(jnp.bfloat16), "mp", scatter_dimension=1, tiled=True
    ).astype(jnp.float32)
    return (middle.astype(jnp.float32) + conv_summed).astype(jnp.bfloat16)


NEG = -1e30
HALO = 16
LANES = 128
PIECES = ((0, 128), (128, 128), (256, 128))
RS = 128
CHUNKS = ((320, 64), (192, 128), (0, 128), (128, 64))
REGIONS = (((208, 160),), ((16, 96),), ((0, 16), (368, 16)), ((112, 96),))
MESH = pl.DeviceIdType.MESH
F32 = jnp.float32
BF16 = jnp.bfloat16


def block_kernel(
    T, taps,
    tokens_h, seg_h, g_att_h, wq_h, wkv_h, wo_h, g_conv_h, wg_h, wdep_h, bn_s_h, bn_b_h, wp_h,
    out, seg, g_att, g_conv, wdep, bn_s, bn_b, small, segcol, gains, bns, bnb,
    tok, seg_all, seg_ext, rawq, raw, wide32, sc, pw, wq, wkv, wo, wg, wp, nrm, qp, kp, vp, mst, lst, acc,
    ctx, swi, keep, keep2, mid, ext, wdf, sa, ra, sx, rx, sa2, ra2, sx2, rx2, sb2, rb2,
    wsem, tok_recv, z_send, x_send, m_send, r_send, seg_send, seg_recv, hs_send, hs_recv,
    hg_send, hg_recv, ar_send, ar_recv, mid_send, mid_recv, rs_send, rs_recv,
):
    R, C = tokens_h.shape
    M = 4
    D = M * C
    heads = C // HEAD_DIM
    HP = heads * LANES
    tiles = C // LANES
    t = lax.axis_index("tm")
    m = lax.axis_index("mp")
    mate = m + 1 - 2 * (m % 2)
    cross = (m + 2) % 4
    diag = (mate + 2) % 4

    def rcopy(src, dst, ssem, rsem, **dev):
        return pltpu.make_async_remote_copy(
            src_ref=src, dst_ref=dst, send_sem=ssem, recv_sem=rsem,
            device_id=dev, device_id_type=MESH,
        )

    firsts = [
        pltpu.make_async_copy(src, dst, small.at[i])
        for i, (src, dst) in enumerate([
            (tokens_h, tok.at[t, m]), (seg_h, seg), (g_att_h, g_att), (g_conv_h, g_conv),
            (wdep_h, wdep), (bn_s_h, bn_s), (bn_b_h, bn_b)])
    ]
    loads, at = {}, 0

    def load(name, src, dst):
        nonlocal at
        loads[name] = pltpu.make_async_copy(src, dst, wsem.at[at])
        at += 1

    for k in range(tiles):
        load(("kv", k), wkv_h.at[:, :, pl.ds(k * LANES, LANES)], raw.at[0, k])
    load("q", wq_h, rawq)
    for k in range(tiles):
        load(("g", k), wg_h.at[:, :, pl.ds(k * LANES, LANES)], raw.at[1, k])
    for b in range(M):
        cols = pl.ds(b * C, C)
        for h in range(heads):
            load(("o", b, h), wo_h.at[pl.ds(h * HEAD_DIM, HEAD_DIM), cols],
                 wo.at[b, pl.ds(h * LANES, HEAD_DIM)])
    for b in range(M):
        load(("p", b), wp_h.at[:, pl.ds(b * C, C)], wp.at[b])
    for c in firsts:
        c.start()

    barrier = pltpu.get_barrier_semaphore()
    for peer in (mate, cross):
        pl.semaphore_signal(barrier, inc=1, device_id={"mp": peer}, device_id_type=MESH)
    for d in range(1, T):
        pl.semaphore_signal(
            barrier, inc=1, device_id={"tm": (t + d) % T}, device_id_type=MESH
        )
    for c in loads.values():
        c.start()
    for c in firsts[:2]:
        c.wait()
    ids = seg[...].reshape(1, R)
    seg_all[t] = jnp.broadcast_to(ids, (8, R))
    pl.semaphore_wait(barrier, 1 + T)

    def z_right(s, p):
        piece = tok.at[s, m, pl.ds(*PIECES[p])]
        return rcopy(piece, piece, z_send.at[0, s, p], tok_recv.at[s, m, p], tm=(t + 1) % T)

    def z_left(s, p):
        piece = tok.at[s, m, pl.ds(*PIECES[p])]
        return rcopy(piece, piece, z_send.at[1, s, p], tok_recv.at[s, m, p], tm=(t + T - 1) % T)

    def over_x(s, col, p):
        piece = tok.at[s, col, pl.ds(*PIECES[p])]
        return rcopy(piece, piece, x_send.at[s, p], tok_recv.at[s, col, p], mp=cross)

    def to_mate(s, col, k, p):
        piece = tok.at[s, col, pl.ds(*PIECES[p])]
        return rcopy(piece, piece, m_send.at[s, k, p], tok_recv.at[s, col, p], mp=mate)

    def launch(s, p):
        @pl.when(jnp.logical_and(s <= t, t < T - 1))
        def _():
            z_right(s, p).start()

        @pl.when(jnp.logical_and(s >= t, t > 0))
        def _():
            z_left(s, p).start()

    def straight(s, p):
        inner = jnp.logical_and(s > 0, s < T - 1)
        return jnp.logical_or(p < 2, jnp.logical_or(s == t, inner))

    def round_right(s):
        piece = tok.at[s, cross, pl.ds(*PIECES[2])]
        return rcopy(piece, piece, r_send.at[0], tok_recv.at[s, cross, 2], tm=(t + 1) % T)

    def round_left(s):
        piece = tok.at[s, cross, pl.ds(*PIECES[2])]
        return rcopy(piece, piece, r_send.at[1], tok_recv.at[s, cross, 2], tm=(t + T - 1) % T)

    def send_round(s):
        @pl.when(jnp.logical_and(s == 0, t < T - 1))
        def _():
            round_right(s).start()

        @pl.when(jnp.logical_and(s == T - 1, t > 0))
        def _():
            round_left(s).start()

    for p in range(3):
        over_x(t, m, p).start()
        launch(t, p)
        to_mate(t, m, 0, p).start()

    def seg_copy(d):
        return rcopy(seg_all.at[t], seg_all.at[t], seg_send.at[d], seg_recv.at[t],
                     tm=(t + d) % T)

    for d in range(1, T):
        seg_copy(d).start()

    def halo_right(ref, ssem, rsem):
        return rcopy(ref.at[:, pl.ds(R, HALO)], ref.at[:, pl.ds(0, HALO)], ssem.at[0],
                     rsem.at[0], tm=(t + 1) % T)

    def halo_left(ref, ssem, rsem):
        return rcopy(ref.at[:, pl.ds(HALO, HALO)], ref.at[:, pl.ds(R + HALO, HALO)],
                     ssem.at[1], rsem.at[1], tm=(t + T - 1) % T)

    has_right = t < T - 1
    has_left = t > 0
    edge = jnp.logical_or(t == 0, t == T - 1)

    segcol[...] = jnp.transpose(jnp.broadcast_to(ids, (LANES, R)))
    seg_ext[0, pl.ds(HALO, R), :] = segcol[...]

    @pl.when(has_right)
    def _():
        halo_right(seg_ext, hs_send, hs_recv).start()

    @pl.when(has_left)
    def _():
        halo_left(seg_ext, hs_send, hs_recv).start()

    @pl.when(jnp.logical_not(has_left))
    def _():
        seg_ext[0, pl.ds(0, HALO), :] = jnp.full((HALO, LANES), -1, jnp.int32)
        ext[:, pl.ds(0, HALO), :] = jnp.zeros((tiles, HALO, LANES), F32)

    @pl.when(jnp.logical_not(has_right))
    def _():
        seg_ext[0, pl.ds(R + HALO, HALO), :] = jnp.full((HALO, LANES), -1, jnp.int32)
        ext[:, pl.ds(R + HALO, HALO), :] = jnp.zeros((tiles, HALO, LANES), F32)

    for c in firsts[2:]:
        c.wait()
    gains[0] = g_att[...].reshape(1, D)
    gains[1] = g_conv[...].reshape(1, D)
    bns[...] = bn_s[...].reshape(1, C)
    bnb[...] = bn_b[...].reshape(1, C)

    def by_head(x):
        gap = jnp.zeros((x.shape[0], LANES - HEAD_DIM), F32)
        cols = []
        for h in range(heads):
            cols += [x[:, h * HEAD_DIM:(h + 1) * HEAD_DIM], gap]
        return jnp.concatenate(cols, axis=1).astype(BF16)

    for k in range(tiles):
        loads["kv", k].wait()

    def widen(b, i, n):
        for k in range(tiles):
            wide32[k, pl.ds(0, 2 * n), :] = raw.at[b, k].reshape(2 * D, LANES)[
                pl.ds(pl.multiple_of(i * 2 * n, 2 * n), 2 * n), :].astype(F32)

    @pl.loop(0, D // 256)
    def _(i):
        rows = pl.ds(pl.multiple_of(i * 256, 256), 256)
        widen(0, i, 256)
        for j in range(2):
            x = jnp.concatenate([wide32[k, pl.ds(j, 256, 2), :] for k in range(tiles)], axis=1)
            wkv[rows, pl.ds(j * HP, HP)] = by_head(x)

    loads["q"].wait()

    @pl.loop(0, D // 256)
    def _(i):
        rows = pl.ds(pl.multiple_of(i * 256, 256), 256)
        wq[rows, :] = by_head(rawq[rows, :].astype(F32))

    def split_gates():
        for k in range(tiles):
            loads["g", k].wait()

        @pl.loop(0, D // 128)
        def _(i):
            rows = pl.ds(pl.multiple_of(i * 128, 128), 128)
            widen(1, i, 128)
            for j in range(2):
                for k in range(tiles):
                    wg[rows, pl.ds(j * C + k * LANES, LANES)] = (
                        wide32[k, pl.ds(j, 128, 2), :].astype(BF16))

    wdf[pl.ds(0, taps), :] = wdep[...].astype(F32)
    mst[...] = jnp.full(mst.shape, NEG, F32)
    lst[...] = jnp.zeros(lst.shape, F32)
    acc[...] = jnp.zeros(acc.shape, F32)
    for b in range(M):
        for h in range(heads):
            wo[b, pl.ds(h * LANES + HEAD_DIM, LANES - HEAD_DIM), :] = jnp.zeros(
                (LANES - HEAD_DIM, C), BF16)

    def norm_rows(load_part, gain, r0, n):
        parts = [load_part(b, r0, n).astype(F32) for b in range(M)]
        total = parts[0] + parts[1] + parts[2] + parts[3]
        mean = jnp.sum(total, axis=1, keepdims=True) * (1.0 / D)
        parts = [p - mean for p in parts]
        sq = parts[0] * parts[0]
        for p in parts[1:]:
            sq = sq + p * p
        inv = lax.rsqrt(jnp.sum(sq, axis=1, keepdims=True) * (1.0 / D) + 1e-05)
        for b in range(M):
            nrm[pl.ds(r0, n), pl.ds(b * C, C)] = (
                parts[b] * inv * gains[gain, :, pl.ds(b * C, C)]
            ).astype(BF16)

    coef = float(HEAD_DIM ** (-0.5) * 1.4426950408889634)

    hs = range(heads)

    def lanes(h):
        return pl.ds(h * LANES, LANES)

    def weigh(key_ids, r0, n, score, keep_weights):
        rows, nk = pl.ds(r0, n), key_ids.shape[1]

        def fold(x):
            return sum(x[:, k * LANES:(k + 1) * LANES] for k in range(1, nk // LANES)) + x[:, :LANES]

        def wide(col):
            return jnp.concatenate([col] * (nk // LANES), axis=1)

        bias = jnp.where(wide(segcol[rows, :]) == key_ids, 0.0, NEG)
        xs = [score(h) + bias for h in hs]
        olds = [mst[h, rows, :] for h in hs]
        sums = [lst[h, rows, :] for h in hs]
        accs = [acc[rows, lanes(h)] for h in hs]
        news = [jnp.maximum(o, jnp.max(x, axis=1, keepdims=True)) for o, x in zip(olds, xs)]
        fs = [jnp.exp2((o - v) * coef) for o, v in zip(olds, news)]
        ps = [jnp.exp2((x - wide(v)) * coef) for x, v in zip(xs, news)]
        sums = [v * f + fold(w) for v, f, w in zip(sums, fs, ps)]
        for h in hs:
            mst[h, rows, :] = news[h]
            lst[h, rows, :] = sums[h]
        keep_weights([w.astype(BF16) for w in ps], [a * f for a, f in zip(accs, fs)])

    def score_block(r0, n, c0, nk, h):
        return lax.dot_general(
            qp[pl.ds(r0, n), lanes(h)], kp[pl.ds(c0, nk), lanes(h)], (((1,), (1,)), ((), ())),
            preferred_element_type=F32)

    def ids_of(s):
        return seg_all[s, pl.ds(0, 1), :]

    def attend(s):
        for h in hs:
            sc[h] = score_block(0, R, 0, R, h)

        @pl.loop(0, R // RS)
        def _(rt):
            r0 = pl.multiple_of(rt * RS, RS)
            rows = pl.ds(r0, RS)

            def kept(ws, scaled):
                for h in hs:
                    pw[h, rows, :] = ws[h]
                    acc[rows, lanes(h)] = scaled[h]

            weigh(ids_of(s), r0, RS, lambda h: sc[h, rows, :], kept)

        for h in hs:
            acc[:, lanes(h)] += jnp.dot(
                pw[h], vp[pl.ds(0, R), lanes(h)], preferred_element_type=F32)

    def attend_last(r0, n):
        rows = pl.ds(r0, n)

        def kept(ws, scaled):
            for h in hs:
                total = scaled[h] + jnp.dot(
                    ws[h], vp[:, lanes(h)], preferred_element_type=F32)
                den = jnp.sum(lst[h, rows, :], axis=1, keepdims=True)
                ctx[rows, lanes(h)] = (total / den).astype(BF16)

        key_ids = jnp.concatenate([ids_of(late), ids_of(final)], axis=1)
        weigh(key_ids, r0, n, lambda h: score_block(r0, n, 0, 2 * R, h), kept)

    def project(s, r0, n, base, with_queries, midway):
        rows, spot = pl.ds(r0, n), pl.ds(base + r0, n)

        @pl.loop(0, n // 128)
        def _(rt):
            norm_rows(lambda b, at, k: tok[s, b, pl.ds(at, k), :], 0,
                      pl.multiple_of(r0 + rt * 128, 128), 128)

        if with_queries is not None:
            @pl.when(with_queries)
            def _():
                qp[rows, :] = jnp.dot(
                    nrm[rows, :], wq[...], preferred_element_type=F32).astype(BF16)

        kp[spot, :] = jnp.dot(
            nrm[rows, :], wkv[:, pl.ds(0, HP)], preferred_element_type=F32).astype(BF16)
        midway()
        vp[spot, :] = jnp.dot(
            nrm[rows, :], wkv[:, pl.ds(HP, HP)], preferred_element_type=F32).astype(BF16)

    def digit(code, i):
        return (code // (T ** i)) % T

    order = 228 - 3 * ((t + 3) // 4) - 195 * ((t + 2) // 4) - 3 * ((t + 1) // 4)

    def take(s, p):
        over_x(s, cross, p).wait_recv()
        to_mate(s, cross, 1, p).start()

    def arrive(s, p):
        to_mate(s, mate, 0, p).wait_recv()
        to_mate(s, diag, 1, p).wait_recv()

    def ids_arrive(s):
        rcopy(seg_all.at[s], seg_all.at[s], seg_send.at[0], seg_recv.at[s],
              tm=(t + 1) % T).wait_recv()

    def block_step(i, carry):
        code, before = carry
        s, nxt, after = digit(code, 0), digit(code, 1), digit(code, 2)

        def relay(ps):
            for p in ps:
                @pl.when(jnp.logical_or(i == 0, edge))
                def _():
                    z_right(nxt, p).wait_recv()
                    launch(nxt, p)

                @pl.when(straight(nxt, p))
                def _():
                    over_x(nxt, m, p).start()

                to_mate(nxt, m, 0, p).start()

                @pl.when(jnp.logical_and(jnp.logical_not(edge), i < 2))
                def _():
                    z_right(after, p).wait_recv()
                    launch(after, p)

            for p in ps:
                take(s, p)
                if p == 2:
                    send_round(s)

        @pl.when(jnp.logical_and(jnp.logical_not(edge), i == T - 2))
        def _():
            take(nxt, 2)
            send_round(nxt)

        relay((0, 1))

        @pl.when(i > 0)
        def _():
            attend(before)
            ids_arrive(s)

        def early():
            @pl.when(i == T - 2)
            def _():
                take(nxt, 0)

            @pl.when(jnp.logical_and(edge, i == T - 2))
            def _():
                take(nxt, 2)

        arrive(s, 0)
        arrive(s, 1)
        project(s, 0, 256, 0, i == 0, lambda: relay((2,)))
        arrive(s, 2)
        project(s, 256, 128, 0, i == 0, early)
        return code // T, s

    late, final = digit(order, T - 2), digit(order, T - 1)
    lax.fori_loop(0, T - 1, block_step, (order, t))
    ids_arrive(final)
    arrive(final, 2)
    project(final, 256, 128, R, None, lambda: take(final, 1))
    arrive(final, 0)
    project(final, 0, 128, R, None, lambda: None)
    arrive(final, 1)
    project(final, 128, 128, R, None, lambda: None)

    def ar_mate(i):
        rows = pl.ds(*CHUNKS[i])
        return rcopy(sa.at[:, rows], ra.at[:, rows], ar_send.at[i, 0], ar_recv.at[i, 0], mp=mate)

    def ar_x(i):
        rows = pl.ds(*CHUNKS[i])
        return rcopy(sx.at[:, rows], rx.at[:, rows], ar_send.at[i, 1], ar_recv.at[i, 1], mp=cross)

    def mid_copy(i, j, col):
        piece = mid.at[col, pl.ds(*CHUNKS[i])]
        return rcopy(piece, piece, mid_send.at[i, j], mid_recv.at[i, j], mp=mate)

    def rounded(a, w):
        return jnp.dot(a, w, preferred_element_type=F32).astype(BF16)

    def project_out(i):
        rows = pl.ds(*CHUNKS[i])
        a = ctx[rows, :]
        sa[0, rows, :] = rounded(a, wo[mate])
        sa[1, rows, :] = rounded(a, wo[diag])
        ar_mate(i).start()
        keep[0, rows, :] = rounded(a, wo[m]).astype(F32)
        keep[1, rows, :] = rounded(a, wo[cross]).astype(F32)

    def chip_sum(i):
        rows = pl.ds(*CHUNKS[i])
        ar_mate(i).wait_recv()
        for j in range(2):
            both = keep[j, rows, :] + ra[j, rows, :].astype(F32)
            keep[j, rows, :] = both
            sx[1 - j, rows, :] = both.astype(BF16)
        ar_x(i).start()

    def middle(i):
        rows = pl.ds(*CHUNKS[i])
        ar_x(i).wait_recv()
        for j, col in enumerate((m, cross)):
            mid[col, rows, :] = (
                tok[t, col, rows, :].astype(F32) + (keep[j, rows, :] + rx[j, rows, :].astype(F32))
            ).astype(BF16)
            mid_copy(i, j, col).start()

    def gate(i):
        r0, n = CHUNKS[i]
        rows = pl.ds(r0, n)
        for j, col in enumerate((mate, diag)):
            mid_copy(i, j, col).wait_recv()

        @pl.loop(0, n // 64)
        def _(rt):
            norm_rows(lambda b, at, k: mid[b, pl.ds(at, k), :], 1,
                      pl.multiple_of(r0 + rt * 64, 64), 64)

        both = jnp.dot(nrm[rows, :], wg[...], preferred_element_type=F32)
        gated = (both[:, :C] * jax.nn.sigmoid(both[:, C:])).astype(BF16).astype(F32)
        for k in range(tiles):
            ext[k, pl.ds(HALO + r0, n), :] = gated[:, k * LANES:(k + 1) * LANES]

    half = (taps - 1) // 2
    RT = 64
    places, place = [], 0
    for region in REGIONS:
        first = place
        spots = []
        for r0, n in region:
            spots.append((r0, n, place))
            place += n
        places.append((first, place - first, spots))

    def rs_a(i):
        rows = pl.ds(*places[i][:2])
        return rcopy(sa2.at[rows], ra2.at[rows], rs_send.at[i, 0], rs_recv.at[i, 0], mp=mate)

    def rs_x(i):
        rows = pl.ds(*places[i][:2])
        return rcopy(sx2.at[rows], rx2.at[rows], rs_send.at[i, 1], rs_recv.at[i, 1], mp=cross)

    def rs_b(i):
        rows = pl.ds(*places[i][:2])
        return rcopy(sb2.at[rows], rb2.at[rows], rs_send.at[i, 2], rs_recv.at[i, 2], mp=mate)

    def convolve_rows(r0, n, to):
        here = segcol[pl.ds(r0, n), :]
        groups = [pl.ds(k * LANES, LANES) for k in range(tiles)]
        depth = [jnp.zeros((n, LANES), F32) for _ in groups]
        for j in range(taps):
            at = pl.ds(r0 + (j + HALO - half), n)
            same = seg_ext[0, at, :] == here
            for k, g in enumerate(groups):
                depth[k] += jnp.where(same, ext[k, at, :], 0.0) * wdf[pl.ds(j, 1), g]
        for k, g in enumerate(groups):
            z = depth[k] * bns[:, g] + bnb[:, g]
            swi[pl.ds(to, n), g] = (z * jax.nn.sigmoid(z)).astype(BF16)

    def convolve(i):
        for r0, n, to in places[i][2]:
            if n >= RT:
                @pl.loop(0, n // RT)
                def _(rt):
                    convolve_rows(pl.multiple_of(r0 + rt * RT, 16), RT,
                                  pl.multiple_of(to + rt * RT, 16))
            if n % RT:
                done = n - n % RT
                convolve_rows(r0 + done, n % RT, to + done)

        rows = pl.ds(*places[i][:2])
        a = swi[rows, :]
        sa2[rows, :] = rounded(a, wp[diag])
        rs_a(i).start()
        keep2[rows, :] = jnp.dot(a, wp[cross], preferred_element_type=F32)
        sb2[rows, :] = rounded(a, wp[mate])
        rs_b(i).start()

    def pass_on(i):
        rows = pl.ds(*places[i][:2])
        rs_a(i).wait_recv()
        sx2[rows, :] = (keep2[rows, :] + ra2[rows, :].astype(F32)).astype(BF16)
        rs_x(i).start()
        keep2[rows, :] = rounded(swi[rows, :], wp[m]).astype(F32)

    for b in range(M):
        for h in range(heads):
            loads["o", b, h].wait()
    attend_last(*CHUNKS[0])
    project_out(0)
    attend_last(*CHUNKS[1])
    chip_sum(0)
    project_out(1)
    attend_last(*CHUNKS[2])
    chip_sum(1)
    project_out(2)
    attend_last(*CHUNKS[3])
    chip_sum(2)
    project_out(3)
    split_gates()
    chip_sum(3)
    for b in range(M):
        loads["p", b].wait()
    middle(0)
    gate(0)

    @pl.when(has_right)
    def _():
        halo_right(ext, hg_send, hg_recv).start()

    middle(1)
    gate(1)
    convolve(0)
    middle(2)
    pass_on(0)
    gate(2)

    @pl.when(has_left)
    def _():
        halo_left(ext, hg_send, hg_recv).start()

    middle(3)
    convolve(1)
    gate(3)
    pass_on(1)
    convolve(3)

    @pl.when(has_left)
    def _():
        halo_right(seg_ext, hs_send, hs_recv).wait_recv()
        halo_right(ext, hg_send, hg_recv).wait_recv()

    @pl.when(has_right)
    def _():
        halo_left(seg_ext, hs_send, hs_recv).wait_recv()
        halo_left(ext, hg_send, hg_recv).wait_recv()

    convolve(2)
    pass_on(3)
    pass_on(2)
    for i in (0, 1, 3, 2):
        rs_b(i).wait_recv()
        rs_x(i).wait_recv()
        for r0, n, to in places[i][2]:
            rows, spot = pl.ds(r0, n), pl.ds(to, n)
            summed = (keep2[spot, :] + rb2[spot, :].astype(F32)) + rx2[spot, :].astype(F32)
            out[rows, :] = (mid[m, rows, :].astype(F32) + summed).astype(BF16)

    @pl.when(has_right)
    def _():
        round_right(0).wait_send()

    @pl.when(has_left)
    def _():
        round_left(T - 1).wait_send()

    for p in range(3):
        for s in range(T):
            @pl.when(jnp.logical_and(s <= t, t < T - 1))
            def _():
                z_right(s, p).wait_send()

            @pl.when(jnp.logical_and(s >= t, t > 0))
            def _():
                z_left(s, p).wait_send()

            @pl.when(straight(s, p))
            def _():
                over_x(s, m, p).wait_send()

            to_mate(s, m, 0, p).wait_send()
            to_mate(s, cross, 1, p).wait_send()
    for d in range(1, T):
        seg_copy(d).wait_send()

    @pl.when(has_right)
    def _():
        halo_right(seg_ext, hs_send, hs_recv).wait_send()
        halo_right(ext, hg_send, hg_recv).wait_send()

    @pl.when(has_left)
    def _():
        halo_left(seg_ext, hs_send, hs_recv).wait_send()
        halo_left(ext, hg_send, hg_recv).wait_send()

    for i in range(len(CHUNKS)):
        ar_mate(i).wait_send()
        ar_x(i).wait_send()
        mid_copy(i, 0, m).wait_send()
        mid_copy(i, 1, cross).wait_send()
    for i in range(len(REGIONS)):
        rs_a(i).wait_send()
        rs_x(i).wait_send()
        rs_b(i).wait_send()


def fused_device(
    tokens, segment_ids, ln_att_gain, w_query, w_keyval, w_out, ln_conv_gain, w_glu,
    w_depth, bn_scale, bn_shift, w_proj,
):
    R, C = tokens.shape
    D = ln_att_gain.shape[0]
    T = lax.axis_size("tm")
    M = D // C
    heads = C // HEAD_DIM
    HP = heads * LANES
    tiles = C // LANES
    taps = w_depth.shape[0]
    vmem = pl.BlockSpec(memory_space=pltpu.VMEM)
    hbm = pl.BlockSpec(memory_space=pltpu.HBM)
    dma = pltpu.SemaphoreType.DMA
    NC, NR = len(CHUNKS), len(REGIONS)
    part, pair = pltpu.VMEM((R, C), BF16), pltpu.VMEM((2, R, C), BF16)
    return pl.pallas_call(
        functools.partial(block_kernel, T, taps),
        out_shape=jax.ShapeDtypeStruct((R, C), BF16),
        in_specs=[hbm] * 12,
        out_specs=vmem,
        scratch_shapes=[
            pltpu.VMEM((R,), jnp.int32), pltpu.VMEM((D,), F32), pltpu.VMEM((D,), F32),
            pltpu.VMEM((taps, C), BF16), pltpu.VMEM((C,), F32), pltpu.VMEM((C,), F32), dma((7,)),
            pltpu.VMEM((R, LANES), jnp.int32),
            pltpu.VMEM((2, 1, D), F32),
            pltpu.VMEM((1, C), F32),
            pltpu.VMEM((1, C), F32),
            pltpu.VMEM((T, M, R, C), BF16),
            pltpu.VMEM((T, 8, R), jnp.int32),
            pltpu.VMEM((1, R + 2 * HALO, LANES), jnp.int32),
            pltpu.VMEM((D, C), BF16),
            pltpu.VMEM((2, tiles, D, 2, LANES), BF16),
            pltpu.VMEM((tiles, 512, LANES), F32),
            pltpu.VMEM((heads, R, R), F32),
            pltpu.VMEM((heads, R, R), BF16),
            pltpu.VMEM((D, HP), BF16),
            pltpu.VMEM((D, 2 * HP), BF16),
            pltpu.VMEM((M, HP, C), BF16),
            pltpu.VMEM((D, 2 * C), BF16),
            pltpu.VMEM((M, C, C), BF16),
            pltpu.VMEM((R, D), BF16),
            pltpu.VMEM((R, HP), BF16),
            pltpu.VMEM((2 * R, HP), BF16),
            pltpu.VMEM((2 * R, HP), BF16),
            pltpu.VMEM((heads, R, LANES), F32),
            pltpu.VMEM((heads, R, LANES), F32),
            pltpu.VMEM((R, HP), F32),
            pltpu.VMEM((R, HP), BF16),
            part,
            pltpu.VMEM((2, R, C), F32),
            pltpu.VMEM((R, C), F32),
            pltpu.VMEM((M, R, C), BF16),
            pltpu.VMEM((tiles, R + 2 * HALO, LANES), F32),
            pltpu.VMEM((32, C), F32),
            pair, pair, pair, pair, part, part, part, part, part, part,
            dma((2 * tiles + 1 + M * heads + M,)),
            dma((T, M, 3)), dma((2, T, 3)), dma((T, 3)), dma((T, 2, 3)), dma((2,)),
            dma((T,)), dma((T,)), dma((2,)), dma((2,)), dma((2,)), dma((2,)),
            dma((NC, 2)), dma((NC, 2)), dma((NC, 2)), dma((NC, 2)), dma((NR, 3)), dma((NR, 3)),
        ],
        compiler_params=pltpu.CompilerParams(
            collective_id=0, has_side_effects=True, vmem_limit_bytes=52 * 2**20
        ),
    )(*[
        pltpu.with_memory_space_constraint(x, pltpu.HBM)
        for x in (tokens, segment_ids, ln_att_gain, w_query, w_keyval, w_out, ln_conv_gain,
                  w_glu, w_depth, bn_scale, bn_shift, w_proj)
    ])


def solution(mesh):
    placed = (
        P(("group", "tm"), "mp"),
        P(("group", "tm")),
        P(),
        P(None, "mp"),
        P(None, None, "mp"),
        P("mp", None),
        P(),
        P(None, None, "mp"),
        P(None, "mp"),
        P("mp"),
        P("mp"),
        P("mp", None),
    )
    fused = mesh.shape["tm"] == 4 and mesh.shape["mp"] == 4
    return jax.shard_map(
        fused_device if fused else per_device, mesh=mesh, in_specs=placed, out_specs=P(("group", "tm"), "mp"), check_vma=False
    )
```

```python
import functools

import jax
import jax.numpy as jnp
from jax import lax
from jax.experimental import pallas as pl
from jax.experimental.pallas import tpu as pltpu
from jax.sharding import PartitionSpec as P

HEAD_DIM = 96


def with_halo(value, sides, width):
    for axis, dim in sides:
        count, length = (lax.axis_size(axis), value.shape[dim])
        up = [(i, (i + 1) % count) for i in range(count - 1)]
        down = [(j, i) for i, j in up]
        last = lax.slice_in_dim(value, length - width, length, axis=dim)
        initial = lax.slice_in_dim(value, 0, width, axis=dim)
        before = lax.ppermute(last, axis, up)
        after = lax.ppermute(initial, axis, down)
        value = jnp.concatenate([before, value, after], axis=dim)
    return value


def layer_norm(values_in, gain_vec):
    row_mean = jnp.mean(values_in, axis=-1, keepdims=True)
    centered = values_in - row_mean
    spread = jnp.mean(centered * centered, axis=-1, keepdims=True)
    return centered * lax.rsqrt(spread + 1e-05) * gain_vec


def fold_keys(carry_state, query_heads, query_segs, keyval, key_segs, local_cols, score_scale):
    row_max, weight_sum, weighted = carry_state
    key_rows = keyval.shape[0]
    heads_here = query_heads.shape[1]
    key_part = keyval[:, :local_cols].reshape(key_rows, heads_here, -1)
    value_part = keyval[:, local_cols:].reshape(key_rows, heads_here, -1)
    scores = (
        jnp.einsum("qhd,khd->qhk", query_heads, key_part, preferred_element_type=jnp.float32)
        * score_scale
    )
    same_seg = (query_segs[:, None] == key_segs[None, :])[:, None, :]
    scores = jnp.where(same_seg, scores, -jnp.inf)
    new_max = jnp.maximum(row_max, jnp.max(scores, axis=2))
    safe_max = jnp.where(new_max == -jnp.inf, 0.0, new_max)
    weights = jnp.exp(scores - safe_max[:, :, None])
    factor = jnp.exp(row_max - safe_max)
    weight_sum = weight_sum * factor + jnp.sum(weights, axis=2)
    weighted = weighted * factor[:, :, None] + jnp.einsum(
        "qhk,khd->qhd", weights.astype(jnp.bfloat16), value_part, preferred_element_type=jnp.float32
    )
    return (new_max, weight_sum, weighted)


def maybe_fold(carry_state, query_heads, query_segs, keyval, key_segs, local_cols, score_scale):
    return fold_keys(
        carry_state, query_heads, query_segs, keyval, key_segs, local_cols, score_scale
    )


def per_device(
    tokens,
    segment_ids,
    ln_att_gain,
    w_query,
    w_keyval,
    w_out,
    ln_conv_gain,
    w_glu,
    w_depth,
    bn_scale,
    bn_shift,
    w_proj,
):
    row_count = tokens.shape[0]
    full_width = ln_att_gain.shape[0]
    local_cols = w_query.shape[1]
    heads_here = local_cols // HEAD_DIM
    score_scale = HEAD_DIM ** (-0.5)
    all_segs = lax.all_gather(segment_ids, "tm", axis=0, tiled=True)
    anchor = lax.axis_index("tm") * row_count
    whole_rows = lax.all_gather(tokens, "mp", axis=1, tiled=True)
    normed = layer_norm(whole_rows.astype(jnp.float32), ln_att_gain).astype(jnp.bfloat16)
    queries = jnp.dot(normed, w_query, preferred_element_type=jnp.float32).astype(jnp.bfloat16)
    keyval = jnp.dot(
        normed, w_keyval.reshape(full_width, -1), preferred_element_type=jnp.float32
    ).astype(jnp.bfloat16)
    query_heads = queries.reshape(row_count, heads_here, HEAD_DIM)
    initial = (
        jnp.full((row_count, heads_here), -jnp.inf, jnp.float32),
        jnp.zeros((row_count, heads_here), jnp.float32),
        jnp.zeros((row_count, heads_here, HEAD_DIM), jnp.float32),
    )
    segment = lax.all_gather(keyval, "tm", axis=0, tiled=True)
    piece_rows = segment.shape[0]
    block_count = piece_rows // row_count

    def inner_step(state_in, element):
        return (
            maybe_fold(
                state_in, query_heads, segment_ids, element[0], element[1], local_cols, score_scale
            ),
            None,
        )

    stacked = (
        segment.reshape(block_count, row_count, -1),
        all_segs.reshape(block_count, row_count),
    )
    result, unused = lax.scan(inner_step, initial, stacked)
    row_max, weight_sum, weighted = result
    context = (
        (weighted / weight_sum[:, :, None]).reshape(row_count, local_cols).astype(jnp.bfloat16)
    )
    att_terms = jnp.dot(context, w_out, preferred_element_type=jnp.float32)
    att_summed = lax.psum_scatter(
        att_terms.astype(jnp.bfloat16), "mp", scatter_dimension=1, tiled=True
    ).astype(jnp.float32)
    middle = (tokens.astype(jnp.float32) + att_summed).astype(jnp.bfloat16)
    whole_mid = lax.all_gather(middle, "mp", axis=1, tiled=True)
    normed_conv = layer_norm(whole_mid.astype(jnp.float32), ln_conv_gain).astype(jnp.bfloat16)
    both_halves = jnp.dot(
        normed_conv, w_glu.reshape(full_width, -1), preferred_element_type=jnp.float32
    )
    gated = (both_halves[:, :local_cols] * jax.nn.sigmoid(both_halves[:, local_cols:])).astype(
        jnp.bfloat16
    )
    half_width = (w_depth.shape[0] - 1) // 2
    extended = with_halo(gated, (("tm", 0),), half_width).astype(jnp.float32)
    padded_segs = jnp.pad(all_segs, (half_width, half_width), constant_values=-1)
    window_segs = lax.dynamic_slice_in_dim(padded_segs, anchor, row_count + 2 * half_width, 0)
    depth = jnp.zeros((row_count, local_cols), jnp.float32)
    for tap_index in range(w_depth.shape[0]):
        same_seg = (window_segs[tap_index : tap_index + row_count] == segment_ids)[:, None]
        shifted = jnp.where(same_seg, extended[tap_index : tap_index + row_count], 0.0)
        depth = depth + shifted * w_depth[tap_index].astype(jnp.float32)
    normalized = depth * bn_scale + bn_shift
    swished = (normalized * jax.nn.sigmoid(normalized)).astype(jnp.bfloat16)
    conv_terms = jnp.dot(swished, w_proj, preferred_element_type=jnp.float32)
    conv_summed = lax.psum_scatter(
        conv_terms.astype(jnp.bfloat16), "mp", scatter_dimension=1, tiled=True
    ).astype(jnp.float32)
    return (middle.astype(jnp.float32) + conv_summed).astype(jnp.bfloat16)


NEG = -1e30
HALO = 16
LANES = 128
PIECES = ((0, 128), (128, 128), (256, 128))
RS = 128
CHUNKS = ((320, 64), (192, 128), (0, 128), (128, 64))
REGIONS = (((208, 160),), ((16, 96),), ((0, 16), (368, 16)), ((112, 96),))
MESH = pl.DeviceIdType.MESH
F32 = jnp.float32
BF16 = jnp.bfloat16


def block_kernel(
    T, taps,
    tokens_h, seg_h, g_att_h, wq_h, wkv_h, wo_h, g_conv_h, wg_h, wdep_h, bn_s_h, bn_b_h, wp_h,
    out, seg, g_att, g_conv, wdep, bn_s, bn_b, small, segcol, gains, bns, bnb,
    tok, seg_all, seg_ext, rawq, raw, wide32, sc, pw, wq, wkv, wo, wg, wp, nrm, qp, kp, vp, mst, lst, acc,
    ctx, swi, keep, keep2, mid, ext, wdf, sa, ra, sx, rx, sa2, ra2, sx2, rx2, sb2, rb2,
    wsem, tok_recv, z_send, x_send, m_send, r_send, seg_send, seg_recv, hs_send, hs_recv,
    hg_send, hg_recv, ar_send, ar_recv, mid_send, mid_recv, rs_send, rs_recv,
):
    R, C = tokens_h.shape
    M = 4
    D = M * C
    heads = C // HEAD_DIM
    HP = heads * LANES
    tiles = C // LANES
    t = lax.axis_index("tm")
    m = lax.axis_index("mp")
    mate = m + 1 - 2 * (m % 2)
    cross = (m + 2) % 4
    diag = (mate + 2) % 4

    def rcopy(src, dst, ssem, rsem, **dev):
        return pltpu.make_async_remote_copy(
            src_ref=src, dst_ref=dst, send_sem=ssem, recv_sem=rsem,
            device_id=dev, device_id_type=MESH,
        )

    firsts = [
        pltpu.make_async_copy(src, dst, small.at[i])
        for i, (src, dst) in enumerate([
            (tokens_h, tok.at[t, m]), (seg_h, seg), (g_att_h, g_att), (g_conv_h, g_conv),
            (wdep_h, wdep), (bn_s_h, bn_s), (bn_b_h, bn_b)])
    ]
    loads, at = {}, 0

    def load(name, src, dst):
        nonlocal at
        loads[name] = pltpu.make_async_copy(src, dst, wsem.at[at])
        at += 1

    for k in range(tiles):
        load(("kv", k), wkv_h.at[:, :, pl.ds(k * LANES, LANES)], raw.at[0, k])
    load("q", wq_h, rawq)
    for k in range(tiles):
        load(("g", k), wg_h.at[:, :, pl.ds(k * LANES, LANES)], raw.at[1, k])
    for b in range(M):
        cols = pl.ds(b * C, C)
        for h in range(heads):
            load(("o", b, h), wo_h.at[pl.ds(h * HEAD_DIM, HEAD_DIM), cols],
                 wo.at[b, pl.ds(h * LANES, HEAD_DIM)])
    for b in range(M):
        load(("p", b), wp_h.at[:, pl.ds(b * C, C)], wp.at[b])
    for c in firsts:
        c.start()

    barrier = pltpu.get_barrier_semaphore()
    for peer in (mate, cross):
        pl.semaphore_signal(barrier, inc=1, device_id={"mp": peer}, device_id_type=MESH)
    for d in range(1, T):
        pl.semaphore_signal(
            barrier, inc=1, device_id={"tm": (t + d) % T}, device_id_type=MESH
        )
    for c in loads.values():
        c.start()
    for c in firsts[:2]:
        c.wait()
    ids = seg[...].reshape(1, R)
    seg_all[t] = jnp.broadcast_to(ids, (8, R))
    pl.semaphore_wait(barrier, 1 + T)

    def z_right(s, p):
        piece = tok.at[s, m, pl.ds(*PIECES[p])]
        return rcopy(piece, piece, z_send.at[0, s, p], tok_recv.at[s, m, p], tm=(t + 1) % T)

    def z_left(s, p):
        piece = tok.at[s, m, pl.ds(*PIECES[p])]
        return rcopy(piece, piece, z_send.at[1, s, p], tok_recv.at[s, m, p], tm=(t + T - 1) % T)

    def over_x(s, col, p):
        piece = tok.at[s, col, pl.ds(*PIECES[p])]
        return rcopy(piece, piece, x_send.at[s, p], tok_recv.at[s, col, p], mp=cross)

    def to_mate(s, col, k, p):
        piece = tok.at[s, col, pl.ds(*PIECES[p])]
        return rcopy(piece, piece, m_send.at[s, k, p], tok_recv.at[s, col, p], mp=mate)

    def launch(s, p):
        @pl.when(jnp.logical_and(s <= t, t < T - 1))
        def _():
            z_right(s, p).start()

        @pl.when(jnp.logical_and(s >= t, t > 0))
        def _():
            z_left(s, p).start()

    def straight(s, p):
        inner = jnp.logical_and(s > 0, s < T - 1)
        return jnp.logical_or(p < 2, jnp.logical_or(s == t, inner))

    def round_right(s):
        piece = tok.at[s, cross, pl.ds(*PIECES[2])]
        return rcopy(piece, piece, r_send.at[0], tok_recv.at[s, cross, 2], tm=(t + 1) % T)

    def round_left(s):
        piece = tok.at[s, cross, pl.ds(*PIECES[2])]
        return rcopy(piece, piece, r_send.at[1], tok_recv.at[s, cross, 2], tm=(t + T - 1) % T)

    def send_round(s):
        @pl.when(jnp.logical_and(s == 0, t < T - 1))
        def _():
            round_right(s).start()

        @pl.when(jnp.logical_and(s == T - 1, t > 0))
        def _():
            round_left(s).start()

    for p in range(3):
        over_x(t, m, p).start()
        launch(t, p)
        to_mate(t, m, 0, p).start()

    def seg_copy(d):
        return rcopy(seg_all.at[t], seg_all.at[t], seg_send.at[d], seg_recv.at[t],
                     tm=(t + d) % T)

    for d in range(1, T):
        seg_copy(d).start()

    def halo_right(ref, ssem, rsem):
        return rcopy(ref.at[:, pl.ds(R, HALO)], ref.at[:, pl.ds(0, HALO)], ssem.at[0],
                     rsem.at[0], tm=(t + 1) % T)

    def halo_left(ref, ssem, rsem):
        return rcopy(ref.at[:, pl.ds(HALO, HALO)], ref.at[:, pl.ds(R + HALO, HALO)],
                     ssem.at[1], rsem.at[1], tm=(t + T - 1) % T)

    has_right = t < T - 1
    has_left = t > 0
    edge = jnp.logical_or(t == 0, t == T - 1)

    segcol[...] = jnp.transpose(jnp.broadcast_to(ids, (LANES, R)))
    seg_ext[0, pl.ds(HALO, R), :] = segcol[...]

    @pl.when(has_right)
    def _():
        halo_right(seg_ext, hs_send, hs_recv).start()

    @pl.when(has_left)
    def _():
        halo_left(seg_ext, hs_send, hs_recv).start()

    @pl.when(jnp.logical_not(has_left))
    def _():
        seg_ext[0, pl.ds(0, HALO), :] = jnp.full((HALO, LANES), -1, jnp.int32)
        ext[:, pl.ds(0, HALO), :] = jnp.zeros((tiles, HALO, LANES), F32)

    @pl.when(jnp.logical_not(has_right))
    def _():
        seg_ext[0, pl.ds(R + HALO, HALO), :] = jnp.full((HALO, LANES), -1, jnp.int32)
        ext[:, pl.ds(R + HALO, HALO), :] = jnp.zeros((tiles, HALO, LANES), F32)

    for c in firsts[2:]:
        c.wait()
    gains[0] = g_att[...].reshape(1, D)
    gains[1] = g_conv[...].reshape(1, D)
    bns[...] = bn_s[...].reshape(1, C)
    bnb[...] = bn_b[...].reshape(1, C)

    def by_head(x):
        gap = jnp.zeros((x.shape[0], LANES - HEAD_DIM), F32)
        cols = []
        for h in range(heads):
            cols += [x[:, h * HEAD_DIM:(h + 1) * HEAD_DIM], gap]
        return jnp.concatenate(cols, axis=1).astype(BF16)

    for k in range(tiles):
        loads["kv", k].wait()

    def widen(b, i, n):
        for k in range(tiles):
            wide32[k, pl.ds(0, 2 * n), :] = raw.at[b, k].reshape(2 * D, LANES)[
                pl.ds(pl.multiple_of(i * 2 * n, 2 * n), 2 * n), :].astype(F32)

    @pl.loop(0, D // 256)
    def _(i):
        rows = pl.ds(pl.multiple_of(i * 256, 256), 256)
        widen(0, i, 256)
        for j in range(2):
            x = jnp.concatenate([wide32[k, pl.ds(j, 256, 2), :] for k in range(tiles)], axis=1)
            wkv[rows, pl.ds(j * HP, HP)] = by_head(x)

    loads["q"].wait()

    @pl.loop(0, D // 256)
    def _(i):
        rows = pl.ds(pl.multiple_of(i * 256, 256), 256)
        wq[rows, :] = by_head(rawq[rows, :].astype(F32))

    def split_gates():
        for k in range(tiles):
            loads["g", k].wait()

        @pl.loop(0, D // 128)
        def _(i):
            rows = pl.ds(pl.multiple_of(i * 128, 128), 128)
            widen(1, i, 128)
            for j in range(2):
                for k in range(tiles):
                    wg[rows, pl.ds(j * C + k * LANES, LANES)] = (
                        wide32[k, pl.ds(j, 128, 2), :].astype(BF16))

    wdf[pl.ds(0, taps), :] = wdep[...].astype(F32)
    mst[...] = jnp.full(mst.shape, NEG, F32)
    lst[...] = jnp.zeros(lst.shape, F32)
    acc[...] = jnp.zeros(acc.shape, F32)
    for b in range(M):
        for h in range(heads):
            wo[b, pl.ds(h * LANES + HEAD_DIM, LANES - HEAD_DIM), :] = jnp.zeros(
                (LANES - HEAD_DIM, C), BF16)

    def norm_rows(load_part, gain, r0, n):
        parts = [load_part(b, r0, n).astype(F32) for b in range(M)]
        total = parts[0] + parts[1] + parts[2] + parts[3]
        mean = jnp.sum(total, axis=1, keepdims=True) * (1.0 / D)
        parts = [p - mean for p in parts]
        sq = parts[0] * parts[0]
        for p in parts[1:]:
            sq = sq + p * p
        inv = lax.rsqrt(jnp.sum(sq, axis=1, keepdims=True) * (1.0 / D) + 1e-05)
        for b in range(M):
            nrm[pl.ds(r0, n), pl.ds(b * C, C)] = (
                parts[b] * inv * gains[gain, :, pl.ds(b * C, C)]
            ).astype(BF16)

    coef = float(HEAD_DIM ** (-0.5) * 1.4426950408889634)

    hs = range(heads)

    def lanes(h):
        return pl.ds(h * LANES, LANES)

    def weigh(key_ids, r0, n, score, keep_weights):
        rows, nk = pl.ds(r0, n), key_ids.shape[1]

        def fold(x):
            return sum(x[:, k * LANES:(k + 1) * LANES] for k in range(1, nk // LANES)) + x[:, :LANES]

        def wide(col):
            return jnp.concatenate([col] * (nk // LANES), axis=1)

        bias = jnp.where(wide(segcol[rows, :]) == key_ids, 0.0, NEG)
        xs = [score(h) + bias for h in hs]
        olds = [mst[h, rows, :] for h in hs]
        sums = [lst[h, rows, :] for h in hs]
        accs = [acc[rows, lanes(h)] for h in hs]
        news = [jnp.maximum(o, jnp.max(x, axis=1, keepdims=True)) for o, x in zip(olds, xs)]
        fs = [jnp.exp2((o - v) * coef) for o, v in zip(olds, news)]
        ps = [jnp.exp2((x - wide(v)) * coef) for x, v in zip(xs, news)]
        sums = [v * f + fold(w) for v, f, w in zip(sums, fs, ps)]
        for h in hs:
            mst[h, rows, :] = news[h]
            lst[h, rows, :] = sums[h]
        keep_weights([w.astype(BF16) for w in ps], [a * f for a, f in zip(accs, fs)])

    def score_block(r0, n, c0, nk, h):
        return lax.dot_general(
            qp[pl.ds(r0, n), lanes(h)], kp[pl.ds(c0, nk), lanes(h)], (((1,), (1,)), ((), ())),
            preferred_element_type=F32)

    def ids_of(s):
        return seg_all[s, pl.ds(0, 1), :]

    def attend(s):
        for h in hs:
            sc[h] = score_block(0, R, 0, R, h)

        @pl.loop(0, R // RS)
        def _(rt):
            r0 = pl.multiple_of(rt * RS, RS)
            rows = pl.ds(r0, RS)

            def kept(ws, scaled):
                for h in hs:
                    pw[h, rows, :] = ws[h]
                    acc[rows, lanes(h)] = scaled[h]

            weigh(ids_of(s), r0, RS, lambda h: sc[h, rows, :], kept)

        for h in hs:
            acc[:, lanes(h)] += jnp.dot(
                pw[h], vp[pl.ds(0, R), lanes(h)], preferred_element_type=F32)

    def attend_last(r0, n):
        rows = pl.ds(r0, n)

        def kept(ws, scaled):
            for h in hs:
                total = scaled[h] + jnp.dot(
                    ws[h], vp[:, lanes(h)], preferred_element_type=F32)
                den = jnp.sum(lst[h, rows, :], axis=1, keepdims=True)
                ctx[rows, lanes(h)] = (total / den).astype(BF16)

        key_ids = jnp.concatenate([ids_of(late), ids_of(final)], axis=1)
        weigh(key_ids, r0, n, lambda h: score_block(r0, n, 0, 2 * R, h), kept)

    def project(s, r0, n, base, with_queries, midway):
        rows, spot = pl.ds(r0, n), pl.ds(base + r0, n)

        @pl.loop(0, n // 128)
        def _(rt):
            norm_rows(lambda b, at, k: tok[s, b, pl.ds(at, k), :], 0,
                      pl.multiple_of(r0 + rt * 128, 128), 128)

        if with_queries is not None:
            @pl.when(with_queries)
            def _():
                qp[rows, :] = jnp.dot(
                    nrm[rows, :], wq[...], preferred_element_type=F32).astype(BF16)

        kp[spot, :] = jnp.dot(
            nrm[rows, :], wkv[:, pl.ds(0, HP)], preferred_element_type=F32).astype(BF16)
        midway()
        vp[spot, :] = jnp.dot(
            nrm[rows, :], wkv[:, pl.ds(HP, HP)], preferred_element_type=F32).astype(BF16)

    def digit(code, i):
        return (code // (T ** i)) % T

    order = 228 - 3 * ((t + 3) // 4) - 195 * ((t + 2) // 4) - 3 * ((t + 1) // 4)

    def take(s, p):
        over_x(s, cross, p).wait_recv()
        to_mate(s, cross, 1, p).start()

    def arrive(s, p):
        to_mate(s, mate, 0, p).wait_recv()
        to_mate(s, diag, 1, p).wait_recv()

    def ids_arrive(s):
        rcopy(seg_all.at[s], seg_all.at[s], seg_send.at[0], seg_recv.at[s],
              tm=(t + 1) % T).wait_recv()

    def block_step(i, carry):
        code, before = carry
        s, nxt, after = digit(code, 0), digit(code, 1), digit(code, 2)

        def relay(ps):
            for p in ps:
                @pl.when(jnp.logical_or(i == 0, edge))
                def _():
                    z_right(nxt, p).wait_recv()
                    launch(nxt, p)

                @pl.when(straight(nxt, p))
                def _():
                    over_x(nxt, m, p).start()

                to_mate(nxt, m, 0, p).start()

                @pl.when(jnp.logical_and(jnp.logical_not(edge), i < 2))
                def _():
                    z_right(after, p).wait_recv()
                    launch(after, p)

            for p in ps:
                take(s, p)
                if p == 2:
                    send_round(s)

        @pl.when(jnp.logical_and(jnp.logical_not(edge), i == T - 2))
        def _():
            take(nxt, 2)
            send_round(nxt)

        relay((0, 1))

        @pl.when(i > 0)
        def _():
            attend(before)
            ids_arrive(s)

        def early():
            @pl.when(i == T - 2)
            def _():
                take(nxt, 0)

            @pl.when(jnp.logical_and(edge, i == T - 2))
            def _():
                take(nxt, 2)

        arrive(s, 0)
        arrive(s, 1)
        project(s, 0, 256, 0, i == 0, lambda: relay((2,)))
        arrive(s, 2)
        project(s, 256, 128, 0, i == 0, early)
        return code // T, s

    late, final = digit(order, T - 2), digit(order, T - 1)
    lax.fori_loop(0, T - 1, block_step, (order, t))
    ids_arrive(final)
    arrive(final, 2)
    project(final, 256, 128, R, None, lambda: take(final, 1))
    arrive(final, 0)
    project(final, 0, 128, R, None, lambda: None)
    arrive(final, 1)
    project(final, 128, 128, R, None, lambda: None)

    def ar_mate(i):
        rows = pl.ds(*CHUNKS[i])
        return rcopy(sa.at[:, rows], ra.at[:, rows], ar_send.at[i, 0], ar_recv.at[i, 0], mp=mate)

    def ar_x(i):
        rows = pl.ds(*CHUNKS[i])
        return rcopy(sx.at[:, rows], rx.at[:, rows], ar_send.at[i, 1], ar_recv.at[i, 1], mp=cross)

    def mid_copy(i, j, col):
        piece = mid.at[col, pl.ds(*CHUNKS[i])]
        return rcopy(piece, piece, mid_send.at[i, j], mid_recv.at[i, j], mp=mate)

    def rounded(a, w):
        return jnp.dot(a, w, preferred_element_type=F32).astype(BF16)

    def project_out(i):
        rows = pl.ds(*CHUNKS[i])
        a = ctx[rows, :]
        sa[0, rows, :] = rounded(a, wo[mate])
        sa[1, rows, :] = rounded(a, wo[diag])
        ar_mate(i).start()
        keep[0, rows, :] = rounded(a, wo[m]).astype(F32)
        keep[1, rows, :] = rounded(a, wo[cross]).astype(F32)

    def chip_sum(i):
        rows = pl.ds(*CHUNKS[i])
        ar_mate(i).wait_recv()
        for j in range(2):
            both = keep[j, rows, :] + ra[j, rows, :].astype(F32)
            keep[j, rows, :] = both
            sx[1 - j, rows, :] = both.astype(BF16)
        ar_x(i).start()

    def middle(i):
        rows = pl.ds(*CHUNKS[i])
        ar_x(i).wait_recv()
        for j, col in enumerate((m, cross)):
            mid[col, rows, :] = (
                tok[t, col, rows, :].astype(F32) + (keep[j, rows, :] + rx[j, rows, :].astype(F32))
            ).astype(BF16)
            mid_copy(i, j, col).start()

    def gate(i):
        r0, n = CHUNKS[i]
        rows = pl.ds(r0, n)
        for j, col in enumerate((mate, diag)):
            mid_copy(i, j, col).wait_recv()

        norm_rows(lambda b, at, k: mid[b, pl.ds(at, k), :], 1, r0, n)

        both = jnp.dot(nrm[rows, :], wg[...], preferred_element_type=F32)
        gated = (both[:, :C] * jax.nn.sigmoid(both[:, C:])).astype(BF16).astype(F32)
        for k in range(tiles):
            ext[k, pl.ds(HALO + r0, n), :] = gated[:, k * LANES:(k + 1) * LANES]

    half = (taps - 1) // 2
    RT = 64
    places, place = [], 0
    for region in REGIONS:
        first = place
        spots = []
        for r0, n in region:
            spots.append((r0, n, place))
            place += n
        places.append((first, place - first, spots))

    def rs_a(i):
        rows = pl.ds(*places[i][:2])
        return rcopy(sa2.at[rows], ra2.at[rows], rs_send.at[i, 0], rs_recv.at[i, 0], mp=mate)

    def rs_x(i):
        rows = pl.ds(*places[i][:2])
        return rcopy(sx2.at[rows], rx2.at[rows], rs_send.at[i, 1], rs_recv.at[i, 1], mp=cross)

    def rs_b(i):
        rows = pl.ds(*places[i][:2])
        return rcopy(sb2.at[rows], rb2.at[rows], rs_send.at[i, 2], rs_recv.at[i, 2], mp=mate)

    def convolve_rows(r0, n, to):
        here = segcol[pl.ds(r0, n), :]
        groups = [pl.ds(k * LANES, LANES) for k in range(tiles)]
        depth = [jnp.zeros((n, LANES), F32) for _ in groups]
        for j in range(taps):
            at = pl.ds(r0 + (j + HALO - half), n)
            same = seg_ext[0, at, :] == here
            for k, g in enumerate(groups):
                depth[k] += jnp.where(same, ext[k, at, :], 0.0) * wdf[pl.ds(j, 1), g]
        for k, g in enumerate(groups):
            z = depth[k] * bns[:, g] + bnb[:, g]
            swi[pl.ds(to, n), g] = (z * jax.nn.sigmoid(z)).astype(BF16)

    def convolve(i):
        for r0, n, to in places[i][2]:
            if n >= RT:
                @pl.loop(0, n // RT)
                def _(rt):
                    convolve_rows(pl.multiple_of(r0 + rt * RT, 16), RT,
                                  pl.multiple_of(to + rt * RT, 16))
            if n % RT:
                done = n - n % RT
                convolve_rows(r0 + done, n % RT, to + done)

        rows = pl.ds(*places[i][:2])
        a = swi[rows, :]
        sa2[rows, :] = rounded(a, wp[diag])
        rs_a(i).start()
        keep2[rows, :] = jnp.dot(a, wp[cross], preferred_element_type=F32)
        sb2[rows, :] = rounded(a, wp[mate])
        rs_b(i).start()

    def pass_on(i):
        rows = pl.ds(*places[i][:2])
        rs_a(i).wait_recv()
        sx2[rows, :] = (keep2[rows, :] + ra2[rows, :].astype(F32)).astype(BF16)
        rs_x(i).start()
        keep2[rows, :] = rounded(swi[rows, :], wp[m]).astype(F32)

    for b in range(M):
        for h in range(heads):
            loads["o", b, h].wait()
    attend_last(*CHUNKS[0])
    project_out(0)
    attend_last(*CHUNKS[1])
    chip_sum(0)
    project_out(1)
    attend_last(*CHUNKS[2])
    chip_sum(1)
    project_out(2)
    attend_last(*CHUNKS[3])
    chip_sum(2)
    project_out(3)
    split_gates()
    chip_sum(3)
    for b in range(M):
        loads["p", b].wait()
    middle(0)
    gate(0)

    @pl.when(has_right)
    def _():
        halo_right(ext, hg_send, hg_recv).start()

    middle(1)
    gate(1)
    convolve(0)
    middle(2)
    pass_on(0)
    gate(2)

    @pl.when(has_left)
    def _():
        halo_left(ext, hg_send, hg_recv).start()

    middle(3)
    convolve(1)
    gate(3)
    pass_on(1)
    convolve(3)

    @pl.when(has_left)
    def _():
        halo_right(seg_ext, hs_send, hs_recv).wait_recv()
        halo_right(ext, hg_send, hg_recv).wait_recv()

    @pl.when(has_right)
    def _():
        halo_left(seg_ext, hs_send, hs_recv).wait_recv()
        halo_left(ext, hg_send, hg_recv).wait_recv()

    convolve(2)
    pass_on(3)
    pass_on(2)
    for i in (0, 1, 3, 2):
        rs_b(i).wait_recv()
        rs_x(i).wait_recv()
        for r0, n, to in places[i][2]:
            rows, spot = pl.ds(r0, n), pl.ds(to, n)
            summed = (keep2[spot, :] + rb2[spot, :].astype(F32)) + rx2[spot, :].astype(F32)
            out[rows, :] = (mid[m, rows, :].astype(F32) + summed).astype(BF16)

    @pl.when(has_right)
    def _():
        round_right(0).wait_send()

    @pl.when(has_left)
    def _():
        round_left(T - 1).wait_send()

    for p in range(3):
        for s in range(T):
            @pl.when(jnp.logical_and(s <= t, t < T - 1))
            def _():
                z_right(s, p).wait_send()

            @pl.when(jnp.logical_and(s >= t, t > 0))
            def _():
                z_left(s, p).wait_send()

            @pl.when(straight(s, p))
            def _():
                over_x(s, m, p).wait_send()

            to_mate(s, m, 0, p).wait_send()
            to_mate(s, cross, 1, p).wait_send()
    for d in range(1, T):
        seg_copy(d).wait_send()

    @pl.when(has_right)
    def _():
        halo_right(seg_ext, hs_send, hs_recv).wait_send()
        halo_right(ext, hg_send, hg_recv).wait_send()

    @pl.when(has_left)
    def _():
        halo_left(seg_ext, hs_send, hs_recv).wait_send()
        halo_left(ext, hg_send, hg_recv).wait_send()

    for i in range(len(CHUNKS)):
        ar_mate(i).wait_send()
        ar_x(i).wait_send()
        mid_copy(i, 0, m).wait_send()
        mid_copy(i, 1, cross).wait_send()
    for i in range(len(REGIONS)):
        rs_a(i).wait_send()
        rs_x(i).wait_send()
        rs_b(i).wait_send()


def fused_device(
    tokens, segment_ids, ln_att_gain, w_query, w_keyval, w_out, ln_conv_gain, w_glu,
    w_depth, bn_scale, bn_shift, w_proj,
):
    R, C = tokens.shape
    D = ln_att_gain.shape[0]
    T = lax.axis_size("tm")
    M = D // C
    heads = C // HEAD_DIM
    HP = heads * LANES
    tiles = C // LANES
    taps = w_depth.shape[0]
    vmem = pl.BlockSpec(memory_space=pltpu.VMEM)
    hbm = pl.BlockSpec(memory_space=pltpu.HBM)
    dma = pltpu.SemaphoreType.DMA
    NC, NR = len(CHUNKS), len(REGIONS)
    part, pair = pltpu.VMEM((R, C), BF16), pltpu.VMEM((2, R, C), BF16)
    return pl.pallas_call(
        functools.partial(block_kernel, T, taps),
        out_shape=jax.ShapeDtypeStruct((R, C), BF16),
        in_specs=[hbm] * 12,
        out_specs=vmem,
        scratch_shapes=[
            pltpu.VMEM((R,), jnp.int32), pltpu.VMEM((D,), F32), pltpu.VMEM((D,), F32),
            pltpu.VMEM((taps, C), BF16), pltpu.VMEM((C,), F32), pltpu.VMEM((C,), F32), dma((7,)),
            pltpu.VMEM((R, LANES), jnp.int32),
            pltpu.VMEM((2, 1, D), F32),
            pltpu.VMEM((1, C), F32),
            pltpu.VMEM((1, C), F32),
            pltpu.VMEM((T, M, R, C), BF16),
            pltpu.VMEM((T, 8, R), jnp.int32),
            pltpu.VMEM((1, R + 2 * HALO, LANES), jnp.int32),
            pltpu.VMEM((D, C), BF16),
            pltpu.VMEM((2, tiles, D, 2, LANES), BF16),
            pltpu.VMEM((tiles, 512, LANES), F32),
            pltpu.VMEM((heads, R, R), F32),
            pltpu.VMEM((heads, R, R), BF16),
            pltpu.VMEM((D, HP), BF16),
            pltpu.VMEM((D, 2 * HP), BF16),
            pltpu.VMEM((M, HP, C), BF16),
            pltpu.VMEM((D, 2 * C), BF16),
            pltpu.VMEM((M, C, C), BF16),
            pltpu.VMEM((R, D), BF16),
            pltpu.VMEM((R, HP), BF16),
            pltpu.VMEM((2 * R, HP), BF16),
            pltpu.VMEM((2 * R, HP), BF16),
            pltpu.VMEM((heads, R, LANES), F32),
            pltpu.VMEM((heads, R, LANES), F32),
            pltpu.VMEM((R, HP), F32),
            pltpu.VMEM((R, HP), BF16),
            part,
            pltpu.VMEM((2, R, C), F32),
            pltpu.VMEM((R, C), F32),
            pltpu.VMEM((M, R, C), BF16),
            pltpu.VMEM((tiles, R + 2 * HALO, LANES), F32),
            pltpu.VMEM((32, C), F32),
            pair, pair, pair, pair, part, part, part, part, part, part,
            dma((2 * tiles + 1 + M * heads + M,)),
            dma((T, M, 3)), dma((2, T, 3)), dma((T, 3)), dma((T, 2, 3)), dma((2,)),
            dma((T,)), dma((T,)), dma((2,)), dma((2,)), dma((2,)), dma((2,)),
            dma((NC, 2)), dma((NC, 2)), dma((NC, 2)), dma((NC, 2)), dma((NR, 3)), dma((NR, 3)),
        ],
        compiler_params=pltpu.CompilerParams(
            collective_id=0, has_side_effects=True, vmem_limit_bytes=52 * 2**20
        ),
    )(*[
        pltpu.with_memory_space_constraint(x, pltpu.HBM)
        for x in (tokens, segment_ids, ln_att_gain, w_query, w_keyval, w_out, ln_conv_gain,
                  w_glu, w_depth, bn_scale, bn_shift, w_proj)
    ])


def solution(mesh):
    placed = (
        P(("group", "tm"), "mp"),
        P(("group", "tm")),
        P(),
        P(None, "mp"),
        P(None, None, "mp"),
        P("mp", None),
        P(),
        P(None, None, "mp"),
        P(None, "mp"),
        P("mp"),
        P("mp"),
        P("mp", None),
    )
    fused = mesh.shape["tm"] == 4 and mesh.shape["mp"] == 4
    return jax.shard_map(
        fused_device if fused else per_device, mesh=mesh, in_specs=placed, out_specs=P(("group", "tm"), "mp"), check_vma=False
    )
```
